32 devices in a mesh: seq: 16 (over z, y, x), wa: 2 (over core).
Axes of the slice: x: 2, y: 2, z: 4, core: 2. Of those that a mesh axis runs over, the one named last changes fastest.
Arguments:
- tokens: bfloat16 [2, 5120, 768], P('wa', 'seq'), may hold values from -6 to 6
- cotangent: bfloat16 [2, 5120, 768], P('wa', 'seq'), may hold values from -6 to 6
- w_qkv: bfloat16 [3, 768, 768], P(None, None, 'wa'), may hold values from -0.21875 to 0.21875
- w_out: bfloat16 [768, 768], P('wa'), may hold values from -0.875 to 0.875
- w_up: bfloat16 [768, 3072], P(None, 'wa'), may hold values from -0.21875 to 0.21875
- w_down: bfloat16 [3072, 768], P('wa'), may hold values from -0.109375 to 0.109375
- gain_attn: bfloat16 [768], P('wa'), may hold values from 0.25 to 1.75
- gain_mlp: bfloat16 [768], P('wa'), may hold values from 0.25 to 1.75
- router: bfloat16 [768], P('wa'), may hold values from -0.21875 to 0.21875
- picked: int32 [2, 1280], replicated, may hold values from 0 to 319, as said below
- counts: int32 [2, 16], replicated, may hold values from 1 to 80, as said below
Outputs:
- mixed: bfloat16 [2, 5120, 768], P('wa', 'seq')
- grad_tokens: bfloat16 [2, 5120, 768], P('wa', 'seq')
- grad_qkv: float32 [3, 768, 768], P(None, None, 'wa')
- grad_out: float32 [768, 768], P('wa')
- grad_up: float32 [768, 3072], P(None, 'wa')
- grad_down: float32 [3072, 768], P('wa')
- grad_gain_attn: float32 [768], P('wa')
- grad_gain_mlp: float32 [768], P('wa')
- grad_router: float32 [768], P('wa')
The draws below stay inside these ranges and needn't reach their ends.
Inputs may be any that keep to these rules, and one draw needn't show every extreme that they name: For stream s and device d, entries d * 80 to d * 80 + counts[s, d] - 1 of picked[s] are the indices of that device's selected tokens within its block; the 80 entries of one device are distinct. `counts`: selected tokens of stream s on device d; in each stream some device has exactly 80.
All inputs are finite; a program needn't handle non-finite values.
Results may differ from the reference program's by a relative error of at most 0.014.
The reference program's roundings to bfloat16 on the way count: a program that leaves them out, or rounds other values in their place, can miss the bound.
Values may be sent and summed in bfloat16 or wider, within the bound.
A program may use at most 320 MiB of HBM per device.

```python
import jax
import jax.numpy as jnp
from jax import lax

D = 768
HEADS = 12
FF = 3072
TOK_DEV = 320
HD = 64
CAP = 80
STREAMS = 2
STREAM_LEN = 5120
N_SEQ = 16


def draw_picked(key, part):
    keys = jax.random.split(jax.random.fold_in(key, 11), STREAMS * N_SEQ)
    rows = jax.vmap(lambda single: jax.random.permutation(single, TOK_DEV)[:CAP])(keys)
    return rows.reshape(STREAMS, N_SEQ * CAP).astype(jnp.int32)


def draw_counts(key, part):
    first, second = jax.random.split(jax.random.fold_in(key, 23))
    drawn = jax.random.randint(first, (STREAMS, N_SEQ), 1, CAP + 1)
    full_at = jax.random.randint(second, (STREAMS, 1), 0, N_SEQ)
    return jnp.where(jnp.arange(N_SEQ)[None, :] == full_at, CAP, drawn).astype(jnp.int32)


def level_of(key, extent, cuts, low, largest):
    level = 1.0
    for dim, shards_of in cuts:
        draws = jax.random.uniform(jax.random.fold_in(jax.random.fold_in(key, 6), dim), (shards_of,), jnp.float32, low / len(cuts), largest / len(cuts))
        level = level * jnp.repeat(jnp.exp(draws), extent[dim] // shards_of).reshape((-1,) + (1,) * (len(extent) - 1 - dim))
    return level


def gaussian(stream_key, dims, scale, most, shards=(), kind=jnp.bfloat16):
    entries = jax.random.normal(stream_key, dims, jnp.float32) * scale
    if len(shards) > 0:
        entries = level_of(stream_key, dims, shards, -0.22, 0.18) * entries
    return jnp.clip(entries, min=-most, max=most).astype(kind)


def setup_inputs(seed: int = 0) -> dict:
    key_of = jax.random.split(jax.random.key(seed), 12)
    return {
        "tokens": gaussian(key_of[0], (STREAMS, STREAM_LEN, D), 1.0, 6.0, ((0, 2), (1, 16))),
        "cotangent": gaussian(key_of[1], (STREAMS, STREAM_LEN, D), 1.0, 6.0, ((0, 2), (1, 16))),
        "w_qkv": gaussian(key_of[2], (3, D, D), D ** -0.5, 0.21875, ((2, 2),)),
        "w_out": gaussian(key_of[3], (D, D), (D // 16) ** -0.5, 0.875, ((0, 2),)),
        "w_up": gaussian(key_of[4], (D, FF), D ** -0.5, 0.21875, ((1, 2),)),
        "w_down": gaussian(key_of[5], (FF, D), FF ** -0.5, 0.109375, ((0, 2),)),
        "gain_attn": jnp.clip(1.0 + 0.15 * jax.random.normal(key_of[6], (D,), jnp.float32), 0.25, 1.75).astype(jnp.bfloat16),
        "gain_mlp": jnp.clip(1.0 + 0.15 * jax.random.normal(key_of[7], (D,), jnp.float32), 0.25, 1.75).astype(jnp.bfloat16),
        "router": gaussian(key_of[8], (D,), D ** -0.5, 0.21875, ((0, 2),)),
        "picked": draw_picked(jax.random.fold_in(key_of[11], 71), 0),
        "counts": draw_counts(jax.random.fold_in(key_of[11], 71), 0),
    }


@jax.custom_vjp
def low(v):
    return lax.optimization_barrier(v.astype(jnp.bfloat16)).astype(jnp.float32)

@jax.custom_vjp
def low_back(v):
    return v

def low_keep(v):
    return (low(v), None)

def low_pass(kept, grad):
    return (grad,)

def back_keep(v):
    return (v, None)

def back_low(kept, grad):
    return (low(grad),)
low.defvjp(low_keep, low_pass)
low_back.defvjp(back_keep, back_low)
EPS = 1e-05
NEG = -1e+30
HIGH = lax.Precision.HIGHEST

def norm_rows(value, gain):
    return value * lax.rsqrt(lax.optimization_barrier(jnp.mean(value * value, axis=-1, keepdims=True)) + EPS) * gain

def reference(tokens, cotangent, w_qkv, w_out, w_up, w_down, gain_attn, gain_mlp, router, picked, counts):
    f32 = jnp.float32
    slot_total = N_SEQ * CAP
    index = jnp.arange(slot_total, dtype=jnp.int32)
    device = index // CAP
    slot = index % CAP
    row = (device[None, :] * TOK_DEV + picked).astype(jnp.int32)
    flat = (jnp.arange(STREAMS, dtype=jnp.int32)[:, None] * STREAM_LEN + row).reshape(-1)
    live = slot[None, :] < counts[:, device]
    live_f = live.astype(f32)
    position = (picked * N_SEQ + device[None, :]).astype(jnp.int32)
    rows_q = 4 * CAP
    blocks = slot_total // rows_q

    def stream_attention(query, keys, values, k_pos, k_live):

        def one_block(args):
            q_block, q_pos, q_index = args
            raw = low_back(jnp.einsum('qhd,khd->hqk', q_block, keys, precision=HIGH) * HD ** (-0.5))
            allowed = (k_pos[None, :] <= q_pos[:, None]) & (k_live[None, :] | (index[None, :] == q_index[:, None]))
            raw = jnp.where(allowed[None], raw, NEG)
            top = lax.optimization_barrier(jnp.max(raw, axis=-1, keepdims=True))
            expd = jnp.exp(raw - top)
            probs = expd / lax.optimization_barrier(jnp.sum(expd, axis=-1, keepdims=True))
            return jnp.einsum('hqk,khd->qhd', low(probs), values, precision=HIGH)
        out = lax.map(jax.checkpoint(one_block), (query.reshape(blocks, rows_q, HEADS, HD), k_pos.reshape(blocks, rows_q), index.reshape(blocks, rows_q)))
        return out.reshape(slot_total, HEADS * HD)

    def forward(xf, wq, wo, wu, wd, ga, gm, wr):
        xs = xf.reshape(-1, D)[flat].reshape(STREAMS, slot_total, D)
        weight = jax.nn.sigmoid(jnp.einsum('srd,d->sr', xs, wr, precision=HIGH))
        u = low(norm_rows(xs, ga))
        qkv = low_back(low(jnp.einsum('srd,cde->csre', u, wq, precision=HIGH)))
        qkv = qkv.reshape(3, STREAMS, slot_total, HEADS, HD)
        mixed = jnp.stack([stream_attention(qkv[0, s], qkv[1, s], qkv[2, s], position[s], live[s]) for s in range(STREAMS)])
        mixed = low_back(low(mixed))
        attn = low_back(jnp.einsum('sre,ed->srd', mixed, wo, precision=HIGH))
        resid = xs + attn
        normed = low(norm_rows(resid, gm))
        pre = low_back(jnp.einsum('srd,df->srf', normed, wu, precision=HIGH))
        act = low(jax.nn.gelu(pre, approximate=True))
        mlp = low_back(jnp.einsum('srf,fd->srd', act, wd, precision=HIGH))
        lift = (weight * live_f)[..., None] * (attn + mlp)
        return xf.reshape(-1, D).at[flat].add(lift.reshape(-1, D)).reshape(xf.shape)
    inputs = (tokens.astype(f32), w_qkv.astype(f32), w_out.astype(f32), w_up.astype(f32), w_down.astype(f32), gain_attn.astype(f32), gain_mlp.astype(f32), router.astype(f32))
    result, pull = jax.vjp(forward, *inputs)
    grads = pull(cotangent.astype(f32))
    return (result.astype(jnp.bfloat16), grads[0].astype(jnp.bfloat16), grads[1], grads[2], grads[3], grads[4], grads[5], grads[6], grads[7])
```

```python
import jax
import jax.numpy as jnp
from jax import lax
from jax.sharding import PartitionSpec as P

HD = 64
CAP = 80


EPS = 1e-05
NEG = -1e30


def norm_rows(value, gain):
    scale = lax.rsqrt(jnp.mean(value * value, axis=-1, keepdims=True) + EPS)
    return (value * scale * gain, scale)


def norm_back(value, scale, gain, grad_out):
    normed = value * scale
    weighted = grad_out * gain
    grad_value = scale * (weighted - normed * jnp.mean(weighted * normed, axis=-1, keepdims=True))
    return (grad_value, normed)


def gelu_back(pre, grad):
    unused, pull = jax.vjp(lambda value: jax.nn.gelu(value, approximate=True), pre)
    return pull(grad)[0]


def body(
    tokens, cotangent, w_qkv, w_out, w_up, w_down, gain_attn, gain_mlp, router, picked, counts
):
    f32 = jnp.float32
    bf16 = jnp.bfloat16
    nseq = lax.axis_size("seq")
    me = lax.axis_index("seq")
    side = lax.axis_index("wa")
    slots = jnp.arange(CAP, dtype=jnp.int32)
    own_rows = lax.dynamic_slice(picked, (side, me * CAP), (1, CAP))[0]
    x_own = jnp.take(tokens[0], own_rows, axis=0)
    dy_own = jnp.take(cotangent[0], own_rows, axis=0).astype(f32)
    x_rows, g_attn, g_mlp, w_router = (
        lax.all_gather(x_own[None], "wa", axis=0, tiled=True),
        lax.all_gather(gain_attn, "wa", axis=0, tiled=True),
        lax.all_gather(gain_mlp, "wa", axis=0, tiled=True),
        lax.all_gather(router, "wa", axis=0, tiled=True),
    )
    qkv_w, out_w, up_w, down_w = (w_qkv, w_out, w_up, w_down)
    streams = jnp.arange(lax.axis_size("wa"))
    stream_picked = jnp.take(picked, streams, axis=0)
    stream_counts = jnp.take(counts, streams, axis=0)
    key_index = jnp.arange(nseq * CAP, dtype=jnp.int32)
    key_device = key_index // CAP
    key_pos = stream_picked * nseq + key_device[None, :]
    key_live = (key_index % CAP)[None, :] < jnp.take(stream_counts, key_device, axis=1)
    query_index = me * CAP + slots
    query_pos = lax.dynamic_slice_in_dim(key_pos, me * CAP, CAP, 1)
    own_live = (slots < counts[side, me]).astype(f32)
    gains_a = g_attn.astype(f32)
    gains_m = g_mlp.astype(f32)
    x_keep = x_own.astype(f32)
    weight = jax.nn.sigmoid(jnp.dot(x_own, w_router, preferred_element_type=f32))
    x_wide = x_rows.astype(f32)
    normed_a, scale_a = norm_rows(x_wide, gains_a)
    u_rows = normed_a.astype(bf16)
    qkv = jnp.einsum("srd,cde->csre", u_rows, qkv_w, preferred_element_type=f32).astype(bf16)
    query = qkv[0]
    local_kv = qkv[1:]
    batch = query.shape[0]
    heads = query.shape[-1] // HD
    factor = HD ** (-0.5)
    split_q = query.reshape(batch, CAP, heads, HD)
    kv_all = lax.all_gather(local_kv, "seq", axis=2, tiled=True)
    block = 8 * CAP
    nblock = kv_all.shape[2] // block

    def block_of(start):
        keys_b = lax.dynamic_slice_in_dim(kv_all[0], start, block, 1).reshape(
            batch, block, heads, HD
        )
        vals_b = lax.dynamic_slice_in_dim(kv_all[1], start, block, 1).reshape(
            batch, block, heads, HD
        )
        k_pos = lax.dynamic_slice_in_dim(key_pos, start, block, 1)
        k_live = lax.dynamic_slice_in_dim(key_live, start, block, 1)
        k_index = start + jnp.arange(block, dtype=jnp.int32)
        allowed = (k_pos[:, None, :] <= query_pos[:, :, None]) & (
            k_live[:, None, :] | (k_index[None, None, :] == query_index[None, :, None])
        )
        raw = jnp.einsum("sqhd,skhd->shqk", split_q, keys_b, preferred_element_type=f32) * factor
        return (keys_b, vals_b, allowed, jnp.where(allowed[:, None], raw, NEG))

    def max_sum(number, carry):
        top, total = carry
        unused_k, unused_v, allowed, scores = block_of(number * block)
        new_top = jnp.maximum(top, jnp.max(scores, axis=-1, keepdims=True))
        expd = jnp.where(allowed[:, None], jnp.exp(scores - new_top), 0.0)
        return (new_top, total * jnp.exp(top - new_top) + jnp.sum(expd, axis=-1, keepdims=True))

    top_start = jnp.full((batch, heads, CAP, 1), NEG, f32)
    top, total = lax.fori_loop(
        0, nblock, max_sum, (top_start, jnp.zeros((batch, heads, CAP, 1), f32))
    )
    lse = top + jnp.log(total)

    def weigh(number, acc):
        unused_k, vals_b, allowed, scores = block_of(number * block)
        probs_low = jnp.exp(scores - lse).astype(bf16)
        return acc + jnp.einsum("shqk,skhd->sqhd", probs_low, vals_b, preferred_element_type=f32)

    acc = lax.fori_loop(0, nblock, weigh, jnp.zeros((batch, CAP, heads, HD), f32))
    attended = acc.reshape(query.shape).astype(bf16)
    attn_part = jnp.einsum("sqe,ed->sqd", attended, out_w, preferred_element_type=f32)
    attn_own = lax.psum_scatter(attn_part, "wa", scatter_dimension=0, tiled=True)[0]
    resid = x_keep + attn_own
    normed_m, scale_m = norm_rows(resid, gains_m)
    w_own = normed_m.astype(bf16)
    w_rows = lax.all_gather(w_own[None], "wa", axis=0, tiled=True)
    pre = jnp.einsum("srd,df->srf", w_rows, up_w, preferred_element_type=f32)
    act = jax.nn.gelu(pre, approximate=True).astype(bf16)
    mlp_part = jnp.einsum("srf,fd->srd", act, down_w, preferred_element_type=f32)
    mlp_own = lax.psum_scatter(
        mlp_part.astype(jnp.bfloat16), "wa", scatter_dimension=0, tiled=True
    ).astype(jnp.float32)[0]
    branch = attn_own + mlp_own
    lift = (weight * own_live)[:, None]
    out_rows = (x_keep + lift * branch).astype(bf16)
    mixed_out = tokens.at[0, own_rows].set(out_rows)
    grad_branch = dy_own * lift
    grad_logit = jnp.sum(dy_own * branch, axis=-1) * own_live * weight * (1.0 - weight)
    grad_router = jnp.dot(grad_logit, x_keep, precision=lax.Precision.HIGHEST)
    grad_m = grad_branch.astype(bf16)
    grad_m_rows = lax.all_gather(grad_m[None], "wa", axis=0, tiled=True)
    grad_down = jnp.einsum("srf,srd->fd", act, grad_m_rows, preferred_element_type=f32)
    grad_act = jnp.einsum("srd,fd->srf", grad_m_rows, down_w, preferred_element_type=f32)
    grad_pre = gelu_back(pre, grad_act).astype(bf16)
    grad_up = jnp.einsum("srd,srf->df", w_rows, grad_pre, preferred_element_type=f32)
    grad_w_part = jnp.einsum("srf,df->srd", grad_pre, up_w, preferred_element_type=f32)
    grad_w_own = lax.psum_scatter(grad_w_part, "wa", scatter_dimension=0, tiled=True)[0]
    grad_resid, hat_m = norm_back(resid, scale_m, gains_m, grad_w_own)
    grad_gain_m = jnp.sum(grad_w_own * hat_m, axis=0)
    grad_a = (grad_branch + grad_resid).astype(bf16)
    grad_a_rows = lax.all_gather(grad_a[None], "wa", axis=0, tiled=True)
    grad_out = jnp.einsum("sqe,sqd->ed", attended, grad_a_rows, preferred_element_type=f32)
    grad_attended = jnp.einsum(
        "sqd,ed->sqe", grad_a_rows, out_w, preferred_element_type=f32
    ).astype(bf16)
    split_do = grad_attended.reshape(batch, CAP, heads, HD)

    def delta_step(number, delta):
        unused_k, vals_b, allowed, scores = block_of(number * block)
        probs = jnp.exp(scores - lse)
        grad_probs = jnp.einsum("sqhd,skhd->shqk", split_do, vals_b, preferred_element_type=f32)
        return delta + jnp.sum(grad_probs * probs, axis=-1, keepdims=True)

    delta = lax.fori_loop(0, nblock, delta_step, jnp.zeros((batch, heads, CAP, 1), f32))

    def grad_step(number, carry):
        grad_query, holder = carry
        start = number * block
        keys_b, vals_b, allowed, scores = block_of(start)
        probs = jnp.exp(scores - lse)
        grad_probs = jnp.einsum("sqhd,skhd->shqk", split_do, vals_b, preferred_element_type=f32)
        grad_scores = (probs * (grad_probs - delta)).astype(bf16)
        grad_query = (
            grad_query
            + jnp.einsum("shqk,skhd->sqhd", grad_scores, keys_b, preferred_element_type=f32)
            * factor
        )
        grad_keys = (
            jnp.einsum("shqk,sqhd->skhd", grad_scores, split_q, preferred_element_type=f32) * factor
        )
        grad_values = jnp.einsum(
            "shqk,sqhd->skhd", probs.astype(bf16), split_do, preferred_element_type=f32
        )
        paired = jnp.stack([grad_keys, grad_values]).reshape(2, batch, block, heads * HD)
        holder = lax.dynamic_update_slice_in_dim(holder, paired, start, 2)
        return (grad_query, holder)

    grad_query, holder = lax.fori_loop(
        0,
        nblock,
        grad_step,
        (jnp.zeros((batch, CAP, heads, HD), f32), jnp.zeros(kv_all.shape, f32)),
    )
    kv_total = lax.psum_scatter(holder.astype(bf16), "seq", scatter_dimension=2, tiled=True)
    grad_qkv_rows = jnp.concatenate(
        [grad_query.reshape(query.shape)[None].astype(bf16), kv_total.astype(bf16)], axis=0
    )
    grad_qkv = jnp.einsum("srd,csre->cde", u_rows, grad_qkv_rows, preferred_element_type=f32)
    grad_u_part = jnp.einsum("csre,cde->srd", grad_qkv_rows, qkv_w, preferred_element_type=f32)
    part_gain_a = jnp.sum(grad_u_part * (x_wide * scale_a), axis=(0, 1))
    grad_u_all, grad_gain_a, grad_gain_m, grad_router = (
        lax.psum_scatter(
            grad_u_part.astype(jnp.bfloat16), "wa", scatter_dimension=0, tiled=True
        ).astype(jnp.float32),
        lax.psum_scatter(
            part_gain_a.astype(jnp.bfloat16), "wa", scatter_dimension=0, tiled=True
        ).astype(jnp.float32),
        lax.psum_scatter(
            grad_gain_m.astype(jnp.bfloat16), "wa", scatter_dimension=0, tiled=True
        ).astype(jnp.float32),
        lax.psum_scatter(
            grad_router.astype(jnp.bfloat16), "wa", scatter_dimension=0, tiled=True
        ).astype(jnp.float32),
    )
    grad_u_own = grad_u_all[0]
    grad_x_norm, unused = norm_back(x_keep, scale_a[side], gains_a, grad_u_own)
    grad_rows = grad_x_norm + grad_resid + grad_logit[:, None] * w_router.astype(f32)[None, :]
    grad_tokens = cotangent.astype(f32).at[0, own_rows].add(grad_rows).astype(bf16)
    shares = (grad_qkv, grad_out, grad_up, grad_down, grad_gain_a, grad_gain_m, grad_router)
    large = lax.psum(tuple(share.astype(bf16) for share in shares[:4]), "seq")
    small = lax.psum(shares[4:], "seq")
    summed = tuple(part.astype(f32) for part in large) + small
    return (
        mixed_out,
        grad_tokens,
        summed[0],
        summed[1],
        summed[2],
        summed[3],
        summed[4],
        summed[5],
        summed[6],
    )


def solution(mesh):
    return jax.shard_map(
        body,
        mesh=mesh,
        in_specs=(
            P("wa", "seq", None),
            P("wa", "seq", None),
            P(None, None, "wa"),
            P("wa", None),
            P(None, "wa"),
            P("wa", None),
            P("wa"),
            P("wa"),
            P("wa"),
            P(),
            P(),
        ),
        out_specs=(
            P("wa", "seq", None),
            P("wa", "seq", None),
            P(None, None, "wa"),
            P("wa", None),
            P(None, "wa"),
            P("wa", None),
            P("wa"),
            P("wa"),
            P("wa"),
        ),
        check_vma=False,
    )
```

```python
import functools

import jax
import jax.numpy as jnp
from jax import lax
from jax.experimental import pallas as pl
from jax.experimental.pallas import tpu as pltpu
from jax.sharding import PartitionSpec as P

HD = 64
EPS = 1e-05
NEG = -1e30
FAR = 1 << 30
MESSAGES = 160
VMEM_BYTES = 64 << 20
LINES = 4
MESH = pl.DeviceIdType.MESH
F32 = jnp.float32
BF16 = jnp.bfloat16
NN = (((1,), (0,)), ((), ()))
NT = (((1,), (1,)), ((), ()))
TN = (((0,), (0,)), ((), ()))
GELU_A = 0.7978845608028654
GELU_B = 0.044715


def mm(a, b, dims=NN):
    return lax.dot_general(a, b, dims, preferred_element_type=F32)


def gelu_parts(pre):
    square = pre * pre
    t = jnp.tanh(GELU_A * pre * (1.0 + GELU_B * square))
    half = 0.5 * (1.0 + t)
    slope = half + 0.5 * pre * (1.0 - t * t) * (GELU_A * (1.0 + 3.0 * GELU_B * square))
    return pre * half, slope


class Links:
    def __init__(self, send, recv):
        self.send, self.recv, self.used, self.pending = send, recv, 0, []

    def copy(self, src, dst, device):
        i = self.used
        self.used += 1
        made = pltpu.make_async_remote_copy(
            src_ref=src,
            dst_ref=dst,
            send_sem=self.send.at[i],
            recv_sem=self.recv.at[i],
            device_id=device,
            device_id_type=MESH,
        )
        made.start()
        self.pending.append(made)
        return made

    def finish(self, made):
        made.wait()
        self.pending = [other for other in self.pending if other is not made]

    def drain(self):
        for made in self.pending:
            made.wait_send()
        self.pending = []


class Place:
    def __init__(self, nz):
        me, self.c = lax.axis_index("seq"), lax.axis_index("wa")
        self.nz = nz
        self.me = me
        self.z, self.l = lax.div(me, LINES), lax.rem(me, LINES)
        y, x = lax.div(self.l, 2), lax.rem(self.l, 2)
        over_y, over_x = self.l + 2 - 4 * y, self.l + 1 - 2 * x
        self.l2 = over_y * (1 - self.c) + over_x * self.c
        self.l3 = over_x * (1 - self.c) + over_y * self.c
        self.l23 = 3 - self.l
        self.sibling = (me, 1 - self.c)

    def around(self, k):
        return lax.rem(self.z + k, self.nz)

    def at(self, z, line):
        return (z * LINES + line, self.c)


class Gather:
    def __init__(self, place, links, buf, share):
        self.p, self.links, self.buf, self.share = place, links, buf, share
        self.lent = {}

    def start(self):
        p, own = self.p, self.buf.at[self.p.l, self.p.z]
        if self.share is not None:
            self.lent[0, 0] = self.links.copy(own, own, p.sibling)
        self.first, self.second, self.third = {}, {}, {}
        for k in (2, 1, 3)[: p.nz - 1] if p.nz == 4 else range(1, p.nz):
            self.first[k] = self.links.copy(own, own, p.at(p.around(k), p.l))
        self.second[0] = self.links.copy(own, own, p.at(p.z, p.l2))
        self.third[0, 0] = self.links.copy(own, own, p.at(p.z, p.l3))

    def order(self):
        return (1, 3, 2) if self.p.nz == 4 else tuple(range(1, self.p.nz))

    def lend(self, key, ref):
        if self.share is not None:
            self.lent[key] = self.links.copy(ref, ref, self.p.sibling)

    def from_z(self, k):
        p = self.p
        self.first[k].wait_recv()
        ref = self.buf.at[p.l, p.around(p.nz - k)]
        self.second[k] = self.links.copy(ref, ref, p.at(p.z, p.l2))
        self.third[0, k] = self.links.copy(ref, ref, p.at(p.z, p.l3))
        self.lend((0, k), ref)

    def from_second(self, k):
        p = self.p
        self.second[k].wait_recv()
        ref = self.buf.at[p.l2, p.around(p.nz - k)]
        self.third[1, k] = self.links.copy(ref, ref, p.at(p.z, p.l3))
        self.lend((1, k), ref)

    def from_third(self, j, k):
        p = self.p
        self.third[j, k].wait_recv()
        line = p.l3 if j == 0 else p.l23
        self.lend((2 + j, k), self.buf.at[line, p.around(p.nz - k)])

    def lent_line(self, j):
        for k in range(self.p.nz):
            if (j, k) in self.lent:
                self.lent.pop((j, k)).wait_recv()

    def steps(self):
        ks = self.order()
        out = [functools.partial(self.from_z, k) for k in ks]
        out += [functools.partial(self.from_second, k) for k in (0, *ks)]
        out += [functools.partial(self.from_third, j, k) for j in range(2) for k in (0, *ks)]
        return out


class Scatter:
    def __init__(self, place, links, acc, got1, got2, got3):
        self.p, self.links = place, links
        self.acc, self.got1, self.got2, self.got3 = acc, got1, got2, got3
        self.m1, self.m2, self.m3 = {}, {}, {}

    def order(self):
        return (2, 1, 3, 0) if self.p.nz == 4 else (*range(1, self.p.nz), 0)

    def add(self, line, z, got):
        acc = self.acc
        total = acc[line, z].astype(F32) + got.astype(F32)
        acc[line, z] = total.astype(BF16)

    def start(self):
        p = self.p
        for o in self.order():
            zz = p.around(o)
            for j, line in ((0, p.l23), (1, p.l3)):
                self.m1[j, o] = self.links.copy(self.acc.at[line, zz], self.got1.at[j, zz], p.at(p.z, p.l3))

    def stage2(self, o):
        p = self.p
        zz = p.around(o)
        self.m1[0, o].wait_recv()
        self.add(p.l2, zz, self.got1[0, zz])
        self.m2[o] = self.links.copy(self.acc.at[p.l2, zz], self.got2.at[zz], p.at(p.z, p.l2))
        self.m1[1, o].wait_recv()
        self.add(p.l, zz, self.got1[1, zz])

    def stage3(self, o):
        p = self.p
        zz = p.around(o)
        self.m2[o].wait_recv()
        if o:
            self.add(p.l, zz, self.got2[zz])
            self.m3[o] = self.links.copy(self.acc.at[p.l, zz], self.got3.at[o - 1], p.at(zz, p.l))

    def total(self):
        p = self.p
        total = self.acc[p.l, p.z].astype(F32) + self.got2[p.z].astype(F32)
        for o in range(1, p.nz):
            self.m3[o].wait_recv()
            total = total + self.got3[o - 1].astype(F32)
        return total

    def steps(self):
        seq = self.order()
        out = [functools.partial(self.stage2, seq[0])]
        for i in range(1, len(seq)):
            out += [functools.partial(self.stage2, seq[i]), functools.partial(self.stage3, seq[i - 1])]
        out += [functools.partial(self.stage3, seq[-1])]
        return out


def layer_kernel(
    nz,
    tokens, cot, cols, kpos, vec, wqkv_h, wout_h, wup_h, wdown_h,
    mixed_o, gtok_o, res_o, gup_o, gdown_o, small_o,
    wqkv, wout, wup, wdown, wsem,
    gvec, xall, uall, kall, vall, qst, bias, probs, att, rall,
    xo, dy, attn_s, resid_s, col_s, part, got_a, got_m, got_w,
    wall, gall, pre_s, act_s, gpre_s, gattn, dost, gq, gkv,
    gsib, gu1, gu2, gu3, share, sh1, sh2, sh3, res,
    sm, smz, smy, smx, smw, actb, gpreb, stage_u, stage_d, osem,
    send, recv,
):
    place = Place(nz)
    links = Links(send, recv)
    c, l, z = place.c, place.l, place.z
    rows, width = xo.shape
    block = tokens.shape[0]
    half = wout.shape[0]
    pairs = half // 128
    line_rows = nz * rows
    total_rows = LINES * line_rows
    ff = wup.shape[1]

    barrier = pltpu.get_barrier_semaphore()
    peers = [place.at(place.around(k), l) for k in range(1, nz)]
    peers += [place.at(z, place.l2), place.at(z, place.l3), place.sibling]
    for peer in peers:
        pl.semaphore_signal(barrier, inc=1, device_id=peer, device_id_type=MESH)
    loads = [
        pltpu.make_async_copy(h, v, wsem.at[i])
        for i, (h, v) in enumerate(((wqkv_h, wqkv), (wout_h, wout), (wup_h, wup), (wdown_h, wdown)))
    ]
    for load in loads:
        load.start()

    pick = jnp.where(
        lax.broadcasted_iota(jnp.int32, (rows, block), 1) == cols[:, 0:1], 1.0, 0.0
    ).astype(BF16)
    own_x = mm(pick, tokens[...])
    xo[...] = own_x
    xall[c, l, z] = own_x.astype(BF16)
    gvec[c] = vec[...]
    pl.semaphore_wait(barrier, len(peers))

    gx = Gather(place, links, xall.at[c], True)
    gx.start()
    vec_copy = links.copy(gvec.at[c], gvec.at[c], place.sibling)
    dy[...] = mm(pick, cot[...])
    own_live = cols[:, 1:2].astype(F32)
    slot = (l * nz + z) * rows
    for s in range(2):
        near = kpos[s : s + 1, :] <= cols[:, 2 + s : 3 + s]
        itself = lax.broadcasted_iota(jnp.int32, (rows, total_rows), 1) == (
            lax.broadcasted_iota(jnp.int32, (rows, total_rows), 0) + slot
        )
        bias[s] = jnp.where(near | itself, 0.0, NEG)
    vec_copy.wait_recv()

    vectors = jnp.concatenate([gvec[0].astype(F32), gvec[1].astype(F32)], axis=1)
    gain_a, gain_m, router = vectors[0:1], vectors[1:2], vectors[2:3]
    loads[0].wait()

    def project(s, line):
        def norm(zz, carry):
            value = xall[s, line, zz].astype(F32)
            scale = lax.rsqrt(jnp.mean(value * value, axis=-1, keepdims=True) + EPS)
            uall[s, line, zz] = (value * scale * gain_a).astype(BF16)
            rall[s, line, zz] = scale
            return carry

        lax.fori_loop(0, nz, norm, 0)
        u = uall[s, line].reshape(line_rows, width)
        for j, out in ((1, kall), (2, vall)):
            value = mm(u, wqkv[j]).astype(BF16)
            for p in range(pairs):
                out[s * pairs + p, line] = value[:, p * 128 : (p + 1) * 128]

    other = 1 - c
    ks = gx.order()
    for k in ks:
        gx.from_z(k)
    project(c, l)
    for k in (0, *ks):
        gx.from_second(k)
    gx.lent_line(0)
    project(other, l)
    low = lax.broadcasted_iota(jnp.int32, (rows, 128), 1) < HD
    own_u = uall[:, l, z].reshape(2 * rows, width)
    query = mm(own_u, wqkv[0]).astype(BF16) * HD ** (-0.5)

    def stacked(value, s, p):
        piece = value[s * rows : (s + 1) * rows, p * 128 : (p + 1) * 128]
        zero = jnp.zeros_like(piece)
        return jnp.concatenate([jnp.where(low, piece, zero), jnp.where(low, zero, piece)], axis=0)

    query = query.astype(BF16)
    for s in range(2):
        for p in range(pairs):
            qst[s * pairs + p] = stacked(query, s, p)
    project(c, place.l2)
    for k in (0, *ks):
        gx.from_third(0, k)
    gx.lent_line(1)
    project(other, place.l3)
    project(c, place.l3)
    for k in (0, *ks):
        gx.from_third(1, k)
    gx.lent_line(2)
    project(other, place.l2)
    project(c, place.l23)
    gx.lent_line(3)
    project(other, place.l23)

    def attend(i, carry):
        s, p = lax.div(i, pairs), lax.rem(i, pairs)
        keys = kall[i].reshape(total_rows, 128)
        vals = vall[i].reshape(total_rows, 128)
        hide = bias[s]
        raw = mm(qst[i], keys, NT) + jnp.concatenate([hide, hide], axis=0)
        expd = jnp.exp(raw - jnp.max(raw, axis=-1, keepdims=True))
        prob = expd * (1.0 / jnp.sum(expd, axis=-1, keepdims=True))
        probs[i] = prob
        out = mm(prob.astype(BF16), vals)
        at = pl.multiple_of(p * 128, 128)
        att[s, :, pl.ds(at, 128)] = jnp.where(low, out[:rows], out[rows:]).astype(BF16)
        return carry

    lax.fori_loop(0, 2 * pairs, attend, 0)
    loads[1].wait()
    part[...] = mm(att[...].reshape(2 * rows, half), wout[...]).reshape(2, rows, width)
    swap = links.copy(part.at[other], got_a, place.sibling)
    x_keep = xo[...]
    weight = jax.nn.sigmoid(jnp.sum(x_keep * router, axis=-1, keepdims=True))
    links.finish(swap)
    attn = part[c] + got_a[...]
    attn_s[...] = attn
    resid = x_keep + attn
    scale_m = lax.rsqrt(jnp.mean(resid * resid, axis=-1, keepdims=True) + EPS)
    resid_s[...] = resid
    wall[c, l, z] = (resid * scale_m * gain_m).astype(BF16)
    gw = Gather(place, links, wall.at[c], True)
    gw.start()
    todo = gw.steps()

    def pump(n):
        for _ in range(min(n, len(todo))):
            todo.pop(0)()

    for load in loads[2:]:
        load.wait()
    gw.lent.pop((0, 0)).wait_recv()

    fb = 384
    own_w = wall[:, l, z].reshape(2 * rows, width)
    for b in range(ff // fb):
        cut = slice(b * fb, (b + 1) * fb)
        pre = mm(own_w, wup[:, cut])
        pre_s[:, cut] = pre
        act_s[:, cut] = gelu_parts(pre)[0].astype(BF16)
    pump(3)
    part[...] = mm(act_s[...], wdown[...]).reshape(2, rows, width)
    swap = links.copy(part.at[other], got_m, place.sibling)
    pump(2)
    lift = weight * own_live
    links.finish(swap)
    branch = attn_s[...] + (part[c] + got_m[...])
    dy_own = dy[...]
    grad_branch = dy_own * lift
    gall[c, l, z] = grad_branch.astype(BF16)
    gg = Gather(place, links, gall.at[c], True)
    gg.start()
    todo += gg.steps()
    out_rows = (x_keep + lift * branch).astype(BF16)
    grad_logit = (
        jnp.sum(dy_own * branch, axis=-1, keepdims=True) * own_live * weight * (1.0 - weight)
    )
    sm[...] = jnp.zeros_like(sm)
    sm[2:3, :] = jnp.sum(grad_logit * x_keep, axis=0, keepdims=True)
    chosen = mm(pick, jnp.ones((rows, width), BF16), TN) > 0.5
    mixed_o[...] = jnp.where(chosen, mm(pick, out_rows, TN), tokens[...].astype(F32)).astype(BF16)
    gg.lent.pop((0, 0)).wait_recv()

    own_g = gall[:, l, z].reshape(2 * rows, width)
    for b in range(ff // fb):
        cut = slice(b * fb, (b + 1) * fb)
        grad_act = mm(own_g, wdown[cut, :], NT)
        gpre_s[:, cut] = (gelu_parts(pre_s[:, cut])[1] * grad_act).astype(BF16)
    pump(2)
    part[...] = mm(gpre_s[...], wup[...], NT).reshape(2, rows, width)
    swap = links.copy(part.at[other], got_w, place.sibling)
    pump(2)
    links.finish(swap)
    grad_w = part[c] + got_w[...]
    resid = resid_s[...]
    scale_m = lax.rsqrt(jnp.mean(resid * resid, axis=-1, keepdims=True) + EPS)
    hat = resid * scale_m
    sm[1:2, :] = jnp.sum(grad_w * hat, axis=0, keepdims=True)
    lifted = grad_w * gain_m
    grad_resid = scale_m * (lifted - hat * jnp.mean(lifted * hat, axis=-1, keepdims=True))
    resid_s[...] = grad_resid
    gattn[c] = (dy[...] * lift + grad_resid).astype(BF16)
    swap = links.copy(gattn.at[c], gattn.at[c], place.sibling)
    pump(2)
    swap.wait_recv()
    both = gattn[...].reshape(2 * rows, width)
    attended = att[...].reshape(2 * rows, half)
    grad_o = mm(attended, both, TN).astype(BF16)
    chunk = width // nz
    share[3] = jnp.concatenate([grad_o[:, :half], grad_o[:, half:]], axis=0).reshape(nz, chunk, half)
    grad_att = mm(both, wout[...], NT).astype(BF16)
    for s in range(2):
        for p in range(pairs):
            dost[s * pairs + p] = stacked(grad_att, s, p)

    def attend_back(i, carry):
        s, p = lax.div(i, pairs), lax.rem(i, pairs)
        keys = kall[i].reshape(total_rows, 128)
        vals = vall[i].reshape(total_rows, 128)
        prob = probs[i]
        grad_p = mm(dost[i], vals, NT)
        delta = jnp.sum(grad_p * prob, axis=-1, keepdims=True)
        grad_s = (prob * (grad_p - delta)).astype(BF16)
        out = mm(grad_s, keys) * HD ** (-0.5)
        at = pl.multiple_of(p * 128, 128)
        gq[s, :, pl.ds(at, 128)] = jnp.where(low, out[:rows], out[rows:]).astype(BF16)
        gkv[s, :, pl.ds(at, 128)] = mm(grad_s, qst[i], TN).astype(BF16)
        gkv[s, :, pl.ds(pl.multiple_of(half + p * 128, 128), 128)] = mm(
            prob.astype(BF16), dost[i], TN
        ).astype(BF16)
        return carry

    for i in range(pairs):
        lax.fori_loop(2 * i, 2 * i + 2, attend_back, 0)
        pump(4)

    both_q = gq[...].reshape(2 * rows, half)
    own_u = uall[:, l, z].reshape(2 * rows, width)
    share[0] = mm(own_u, both_q, TN).astype(BF16).reshape(nz, chunk, half)
    pump(2)
    for t in range(3):
        cut = slice(t * (width // 3), (t + 1) * (width // 3))
        lhs = uall[:, :, :, :, cut].reshape(2 * total_rows, width // 3)
        value = mm(lhs, gkv[...].reshape(2 * total_rows, 2 * half), TN).astype(BF16)
        piece = width // 3
        for j in range(2):
            for r in range(piece // (chunk // 3)):
                row = t * piece + r * (chunk // 3)
                share[1 + j, row // chunk, row % chunk : row % chunk + chunk // 3] = value[
                    r * (chunk // 3) : (r + 1) * (chunk // 3), j * half : (j + 1) * half
                ]
        pump(3)
    pump(len(todo))
    for j in range(LINES):
        gw.lent_line(j)
        gg.lent_line(j)
    reduce_w = Scatter(place, links, share, sh1, sh2, sh3)
    reduce_w.start()

    def grad_u(s, line):
        got = gkv[s, pl.ds(pl.multiple_of(line * line_rows, line_rows), line_rows), :]
        return mm(got[:, :half], wqkv[1], NT) + mm(got[:, half:], wqkv[2], NT)

    own_gu = mm(both_q, wqkv[0], NT).reshape(2, rows, width)
    part[...] = own_gu
    lines = (place.l23, place.l3, place.l2, l)
    theirs = (place.l23, place.l2, place.l3, l)
    lent = []
    for j, line in enumerate(theirs):
        uall[other, line] = grad_u(other, line).astype(BF16).reshape(nz, rows, width)
        if j == 3:
            uall[other, l, z] = (uall[other, l, z].astype(F32) + part[other]).astype(BF16)
        lent.append(links.copy(uall.at[other, line], gsib.at[line], place.sibling))
    gain_total = jnp.zeros((1, width), F32)
    for j, line in enumerate(lines):
        part_u = grad_u(c, line).reshape(nz, rows, width)
        lent[j].wait_recv()
        part_u = part_u + gsib[line].astype(F32)
        uall[c, line] = part_u.astype(BF16)
        if j == 3:
            uall[c, l, z] = (uall[c, l, z].astype(F32) + part[c]).astype(BF16)
            gain_total = gain_total + jnp.sum(part[c] * (x_keep * rall[c, l, z]), axis=0, keepdims=True)
        for zz in range(nz):
            hat = xall[c, line, zz].astype(F32) * rall[c, line, zz]
            gain_total = gain_total + jnp.sum(part_u[zz] * hat, axis=0, keepdims=True)
    sm[0:1, :] = gain_total
    reduce_u = Scatter(place, links, uall.at[c], gu1, gu2, gu3)
    reduce_u.start()

    small_first = [
        links.copy(sm, smz.at[k - 1], place.at(place.around(k), l)) for k in range(1, nz)
    ]

    def small_z():
        total = jnp.zeros(sm.shape, F32)
        for made in small_first:
            links.finish(made)
        for source in range(nz):
            for k in range(nz):
                piece = sm[...] if k == 0 else smz[k - 1]
                here = place.around(nz - k) == source
                total = total + jnp.where(here, piece, 0.0)
        smy[0] = total
        place.small = links.copy(smy.at[0], smy.at[1], place.at(z, place.l2))

    def small_2():
        place.small.wait_recv()
        smx[0] = smy[0] + smy[1]
        place.small = links.copy(smx.at[0], smx.at[1], place.at(z, place.l3))

    def small_3():
        place.small.wait_recv()
        smw[0] = smx[0] + smx[1]
        place.small = links.copy(smw.at[0], smw.at[1], place.sibling)

    def small_4():
        place.small.wait_recv()
        total = smw[0] + smw[1]
        small_o[...] = jnp.where(c == 0, total[:, :half], total[:, half:])

    def weights_out():
        res[l, z] = reduce_w.total().astype(BF16)
        place.gather = Gather(place, links, res, None)
        place.gather.start()
        todo.extend(place.gather.steps())

    def tokens_out():
        grad = reduce_u.total()
        x_own = xo[...]
        scale = lax.rsqrt(jnp.mean(x_own * x_own, axis=-1, keepdims=True) + EPS)
        hat = x_own * scale
        lifted = grad * gain_a
        grad_x = scale * (lifted - hat * jnp.mean(lifted * hat, axis=-1, keepdims=True))
        grad_rows = grad_x + resid_s[...] + grad_logit * router
        hi = grad_rows.astype(BF16)
        rest = grad_rows - hi.astype(F32)
        mid = rest.astype(BF16)
        lo = (rest - mid.astype(F32)).astype(BF16)
        spread = mm(pick, hi, TN) + (mm(pick, mid, TN) + mm(pick, lo, TN))
        gtok_o[...] = (cot[...].astype(F32) + spread).astype(BF16)

    todo += reduce_w.steps()
    todo += [small_z, weights_out]
    later = reduce_u.steps()
    later += [small_2, small_3, small_4, tokens_out]

    hb = actb.shape[1]
    tile = line_rows
    outs = []
    for b in range(ff // hb):
        cut = slice(b * hb, (b + 1) * hb)

        def tile_step(t, carry):
            s, line = lax.div(t, LINES), lax.rem(t, LINES)
            w_rows = wall[s, line].reshape(tile, width)
            g_rows = gall[s, line].reshape(tile, width)
            act, slope = gelu_parts(mm(w_rows, wup[:, cut]))
            at = pl.ds(pl.multiple_of(t * tile, tile), tile)
            actb[at, :] = act.astype(BF16)
            gpreb[at, :] = (slope * mm(g_rows, wdown[cut, :], NT)).astype(BF16)
            return carry

        lax.fori_loop(0, 2 * LINES, tile_step, 0)
        pump(2)
        if not todo:
            todo += later
            later = []
        slot = b % 2
        if b >= 2:
            outs[2 * (b - 2)].wait()
            outs[2 * (b - 2) + 1].wait()
        stage_d[slot] = mm(actb[...], gall[...].reshape(2 * total_rows, width), TN)
        outs.append(pltpu.make_async_copy(stage_d.at[slot], gdown_o.at[cut, :], osem.at[0, slot]))
        outs[-1].start()
        pump(3)
        if not todo:
            todo += later
            later = []
        stage_u[slot] = mm(wall[...].reshape(2 * total_rows, width), gpreb[...], TN)
        outs.append(pltpu.make_async_copy(stage_u.at[slot], gup_o.at[:, cut], osem.at[1, slot]))
        outs[-1].start()
        pump(2)
        if not todo:
            todo += later
            later = []
    pump(len(todo))
    todo += later
    pump(len(todo))
    pump(len(todo))
    out_copy = pltpu.make_async_copy(res, res_o, osem.at[0, 2])
    out_copy.start()
    for made in outs[-4:]:
        made.wait()
    links.drain()
    out_copy.wait()


def fused_body(
    tokens, cotangent, w_qkv, w_out, w_up, w_down, gain_attn, gain_mlp, router, picked, counts
):
    nseq = lax.axis_size("seq")
    nz = nseq // LINES
    me, side = lax.axis_index("seq"), lax.axis_index("wa")
    rows = picked.shape[1] // nseq
    block, width = tokens.shape[1:]
    half, ff = w_out.shape[0], w_up.shape[1]
    pairs = half // 128
    line_rows = nz * rows
    total_rows = LINES * line_rows
    slots = jnp.arange(rows, dtype=jnp.int32)
    grid = picked.reshape(2, nz, LINES, rows)
    chips = jnp.arange(nseq, dtype=jnp.int32).reshape(1, nz, LINES, 1)
    live = slots < counts.reshape(2, nz, LINES, 1)
    kpos = jnp.where(live, grid * nseq + chips, FAR).transpose(0, 2, 1, 3).reshape(2, total_rows)
    mine = lax.dynamic_slice(picked, (0, me * rows), (2, rows))
    own = lax.dynamic_index_in_dim(mine, side, 0, keepdims=False)
    own_live = (slots < counts[side, me]).astype(jnp.int32)
    cols = jnp.stack([own, own_live, mine[0] * nseq + me, mine[1] * nseq + me], axis=1)
    vec = jnp.pad(jnp.stack([gain_attn, gain_mlp, router]), ((0, 13), (0, 0)))

    hb = 256
    vm = pltpu.VMEM
    dma = pltpu.SemaphoreType.DMA
    wide = (2, LINES, nz, rows, width)
    heads = (2 * pairs, LINES, line_rows, 128)
    chunk = width // nz
    scratch = [
        vm((3, width, half), BF16), vm((half, width), BF16), vm((width, ff), BF16), vm((ff, width), BF16), dma((4,)),
        vm((2, 16, half), BF16), vm(wide, BF16), vm(wide, BF16), vm(heads, BF16), vm(heads, BF16),
        vm((2 * pairs, 2 * rows, 128), BF16), vm((2, rows, total_rows), F32),
        vm((2 * pairs, 2 * rows, total_rows), F32), vm((2, rows, half), BF16), vm((2, LINES, nz, rows, 1), F32),
        vm((rows, width), F32), vm((rows, width), F32), vm((rows, width), F32), vm((rows, width), F32),
        vm((rows, 128), F32), vm((2, rows, width), F32),
        vm((rows, width), F32), vm((rows, width), F32), vm((rows, width), F32),
        vm(wide, BF16), vm(wide, BF16), vm((2 * rows, ff), F32), vm((2 * rows, ff), BF16), vm((2 * rows, ff), BF16),
        vm((2, rows, width), BF16), vm((2 * pairs, 2 * rows, 128), BF16), vm((2, rows, half), BF16),
        vm((2, total_rows, 2 * half), BF16),
        vm((LINES, nz, rows, width), BF16), vm((2, nz, rows, width), BF16), vm((nz, rows, width), BF16),
        vm((nz - 1, rows, width), BF16),
        vm((LINES, nz, chunk, half), BF16), vm((2, nz, chunk, half), BF16), vm((nz, chunk, half), BF16),
        vm((nz - 1, chunk, half), BF16), vm((LINES, nz, chunk, half), BF16),
        vm((8, width), F32), vm((nz - 1, 8, width), F32), vm((2, 8, width), F32), vm((2, 8, width), F32),
        vm((2, 8, width), F32),
        vm((2 * total_rows, hb), BF16), vm((2 * total_rows, hb), BF16),
        vm((2, width, hb), F32), vm((2, hb, width), F32), dma((2, 3)),
        dma((MESSAGES,)), dma((MESSAGES,)),
    ]
    in_vmem = pl.BlockSpec(memory_space=pltpu.VMEM)
    in_hbm = pl.BlockSpec(memory_space=pl.ANY)
    mixed, grad_tokens, res, grad_up, grad_down, small = pl.pallas_call(
        functools.partial(layer_kernel, nz),
        out_shape=(
            jax.ShapeDtypeStruct((block, width), BF16),
            jax.ShapeDtypeStruct((block, width), BF16),
            jax.ShapeDtypeStruct((LINES, nz, chunk, half), BF16),
            jax.ShapeDtypeStruct((width, ff), F32),
            jax.ShapeDtypeStruct((ff, width), F32),
            jax.ShapeDtypeStruct((8, half), F32),
        ),
        in_specs=[in_vmem] * 5 + [in_hbm] * 4,
        out_specs=(in_vmem, in_vmem, in_hbm, in_hbm, in_hbm, in_vmem),
        scratch_shapes=scratch,
        compiler_params=pltpu.CompilerParams(
            collective_id=0, has_side_effects=True, vmem_limit_bytes=VMEM_BYTES
        ),
        name="layer",
    )(tokens[0], cotangent[0], cols, kpos, vec, w_qkv, w_out, w_up, w_down)
    parts = res.reshape(LINES, width, half).astype(F32)
    grad_out = jnp.concatenate([parts[3, :half], parts[3, half:]], axis=1)
    return (
        mixed[None], grad_tokens[None], parts[:3], grad_out, grad_up, grad_down, small[0], small[1], small[2],
    )


def body(tokens, *rest):
    nseq, cores = lax.axis_size("seq"), lax.axis_size("wa")
    fits = nseq == 4 * LINES and cores == 2 and rest[-2].shape[1] == nseq * CAP
    return (fused_body if fits else spread_body)(tokens, *rest)


CAP = 80


def norm_rows(value, gain):
    scale = lax.rsqrt(jnp.mean(value * value, axis=-1, keepdims=True) + EPS)
    return (value * scale * gain, scale)


def norm_back(value, scale, gain, grad_out):
    normed = value * scale
    weighted = grad_out * gain
    grad_value = scale * (weighted - normed * jnp.mean(weighted * normed, axis=-1, keepdims=True))
    return (grad_value, normed)


def gelu_back(pre, grad):
    unused, pull = jax.vjp(lambda value: jax.nn.gelu(value, approximate=True), pre)
    return pull(grad)[0]


def spread_body(
    tokens, cotangent, w_qkv, w_out, w_up, w_down, gain_attn, gain_mlp, router, picked, counts
):
    f32 = jnp.float32
    bf16 = jnp.bfloat16
    nseq = lax.axis_size("seq")
    me = lax.axis_index("seq")
    side = lax.axis_index("wa")
    slots = jnp.arange(CAP, dtype=jnp.int32)
    own_rows = lax.dynamic_slice(picked, (side, me * CAP), (1, CAP))[0]
    x_own = jnp.take(tokens[0], own_rows, axis=0)
    dy_own = jnp.take(cotangent[0], own_rows, axis=0).astype(f32)
    x_rows, g_attn, g_mlp, w_router = (
        lax.all_gather(x_own[None], "wa", axis=0, tiled=True),
        lax.all_gather(gain_attn, "wa", axis=0, tiled=True),
        lax.all_gather(gain_mlp, "wa", axis=0, tiled=True),
        lax.all_gather(router, "wa", axis=0, tiled=True),
    )
    qkv_w, out_w, up_w, down_w = (w_qkv, w_out, w_up, w_down)
    streams = jnp.arange(lax.axis_size("wa"))
    stream_picked = jnp.take(picked, streams, axis=0)
    stream_counts = jnp.take(counts, streams, axis=0)
    key_index = jnp.arange(nseq * CAP, dtype=jnp.int32)
    key_device = key_index // CAP
    key_pos = stream_picked * nseq + key_device[None, :]
    key_live = (key_index % CAP)[None, :] < jnp.take(stream_counts, key_device, axis=1)
    query_index = me * CAP + slots
    query_pos = lax.dynamic_slice_in_dim(key_pos, me * CAP, CAP, 1)
    own_live = (slots < counts[side, me]).astype(f32)
    gains_a = g_attn.astype(f32)
    gains_m = g_mlp.astype(f32)
    x_keep = x_own.astype(f32)
    weight = jax.nn.sigmoid(jnp.dot(x_own, w_router, preferred_element_type=f32))
    x_wide = x_rows.astype(f32)
    normed_a, scale_a = norm_rows(x_wide, gains_a)
    u_rows = normed_a.astype(bf16)
    qkv = jnp.einsum("srd,cde->csre", u_rows, qkv_w, preferred_element_type=f32).astype(bf16)
    query = qkv[0]
    local_kv = qkv[1:]
    batch = query.shape[0]
    heads = query.shape[-1] // HD
    factor = HD ** (-0.5)
    split_q = query.reshape(batch, CAP, heads, HD)
    kv_all = lax.all_gather(local_kv, "seq", axis=2, tiled=True)
    block = 8 * CAP
    nblock = kv_all.shape[2] // block

    def block_of(start):
        keys_b = lax.dynamic_slice_in_dim(kv_all[0], start, block, 1).reshape(
            batch, block, heads, HD
        )
        vals_b = lax.dynamic_slice_in_dim(kv_all[1], start, block, 1).reshape(
            batch, block, heads, HD
        )
        k_pos = lax.dynamic_slice_in_dim(key_pos, start, block, 1)
        k_live = lax.dynamic_slice_in_dim(key_live, start, block, 1)
        k_index = start + jnp.arange(block, dtype=jnp.int32)
        allowed = (k_pos[:, None, :] <= query_pos[:, :, None]) & (
            k_live[:, None, :] | (k_index[None, None, :] == query_index[None, :, None])
        )
        raw = jnp.einsum("sqhd,skhd->shqk", split_q, keys_b, preferred_element_type=f32) * factor
        return (keys_b, vals_b, allowed, jnp.where(allowed[:, None], raw, NEG))

    def max_sum(number, carry):
        top, total = carry
        unused_k, unused_v, allowed, scores = block_of(number * block)
        new_top = jnp.maximum(top, jnp.max(scores, axis=-1, keepdims=True))
        expd = jnp.where(allowed[:, None], jnp.exp(scores - new_top), 0.0)
        return (new_top, total * jnp.exp(top - new_top) + jnp.sum(expd, axis=-1, keepdims=True))

    top_start = jnp.full((batch, heads, CAP, 1), NEG, f32)
    top, total = lax.fori_loop(
        0, nblock, max_sum, (top_start, jnp.zeros((batch, heads, CAP, 1), f32))
    )
    lse = top + jnp.log(total)

    def weigh(number, acc):
        unused_k, vals_b, allowed, scores = block_of(number * block)
        probs_low = jnp.exp(scores - lse).astype(bf16)
        return acc + jnp.einsum("shqk,skhd->sqhd", probs_low, vals_b, preferred_element_type=f32)

    acc = lax.fori_loop(0, nblock, weigh, jnp.zeros((batch, CAP, heads, HD), f32))
    attended = acc.reshape(query.shape).astype(bf16)
    attn_part = jnp.einsum("sqe,ed->sqd", attended, out_w, preferred_element_type=f32)
    attn_own = lax.psum_scatter(attn_part, "wa", scatter_dimension=0, tiled=True)[0]
    resid = x_keep + attn_own
    normed_m, scale_m = norm_rows(resid, gains_m)
    w_own = normed_m.astype(bf16)
    w_rows = lax.all_gather(w_own[None], "wa", axis=0, tiled=True)
    pre = jnp.einsum("srd,df->srf", w_rows, up_w, preferred_element_type=f32)
    act = jax.nn.gelu(pre, approximate=True).astype(bf16)
    mlp_part = jnp.einsum("srf,fd->srd", act, down_w, preferred_element_type=f32)
    mlp_own = lax.psum_scatter(
        mlp_part.astype(jnp.bfloat16), "wa", scatter_dimension=0, tiled=True
    ).astype(jnp.float32)[0]
    branch = attn_own + mlp_own
    lift = (weight * own_live)[:, None]
    out_rows = (x_keep + lift * branch).astype(bf16)
    mixed_out = tokens.at[0, own_rows].set(out_rows)
    grad_branch = dy_own * lift
    grad_logit = jnp.sum(dy_own * branch, axis=-1) * own_live * weight * (1.0 - weight)
    grad_router = jnp.dot(grad_logit, x_keep, precision=lax.Precision.HIGHEST)
    grad_m = grad_branch.astype(bf16)
    grad_m_rows = lax.all_gather(grad_m[None], "wa", axis=0, tiled=True)
    grad_down = jnp.einsum("srf,srd->fd", act, grad_m_rows, preferred_element_type=f32)
    grad_act = jnp.einsum("srd,fd->srf", grad_m_rows, down_w, preferred_element_type=f32)
    grad_pre = gelu_back(pre, grad_act).astype(bf16)
    grad_up = jnp.einsum("srd,srf->df", w_rows, grad_pre, preferred_element_type=f32)
    grad_w_part = jnp.einsum("srf,df->srd", grad_pre, up_w, preferred_element_type=f32)
    grad_w_own = lax.psum_scatter(grad_w_part, "wa", scatter_dimension=0, tiled=True)[0]
    grad_resid, hat_m = norm_back(resid, scale_m, gains_m, grad_w_own)
    grad_gain_m = jnp.sum(grad_w_own * hat_m, axis=0)
    grad_a = (grad_branch + grad_resid).astype(bf16)
    grad_a_rows = lax.all_gather(grad_a[None], "wa", axis=0, tiled=True)
    grad_out = jnp.einsum("sqe,sqd->ed", attended, grad_a_rows, preferred_element_type=f32)
    grad_attended = jnp.einsum(
        "sqd,ed->sqe", grad_a_rows, out_w, preferred_element_type=f32
    ).astype(bf16)
    split_do = grad_attended.reshape(batch, CAP, heads, HD)

    def delta_step(number, delta):
        unused_k, vals_b, allowed, scores = block_of(number * block)
        probs = jnp.exp(scores - lse)
        grad_probs = jnp.einsum("sqhd,skhd->shqk", split_do, vals_b, preferred_element_type=f32)
        return delta + jnp.sum(grad_probs * probs, axis=-1, keepdims=True)

    delta = lax.fori_loop(0, nblock, delta_step, jnp.zeros((batch, heads, CAP, 1), f32))

    def grad_step(number, carry):
        grad_query, holder = carry
        start = number * block
        keys_b, vals_b, allowed, scores = block_of(start)
        probs = jnp.exp(scores - lse)
        grad_probs = jnp.einsum("sqhd,skhd->shqk", split_do, vals_b, preferred_element_type=f32)
        grad_scores = (probs * (grad_probs - delta)).astype(bf16)
        grad_query = (
            grad_query
            + jnp.einsum("shqk,skhd->sqhd", grad_scores, keys_b, preferred_element_type=f32)
            * factor
        )
        grad_keys = (
            jnp.einsum("shqk,sqhd->skhd", grad_scores, split_q, preferred_element_type=f32) * factor
        )
        grad_values = jnp.einsum(
            "shqk,sqhd->skhd", probs.astype(bf16), split_do, preferred_element_type=f32
        )
        paired = jnp.stack([grad_keys, grad_values]).reshape(2, batch, block, heads * HD)
        holder = lax.dynamic_update_slice_in_dim(holder, paired, start, 2)
        return (grad_query, holder)

    grad_query, holder = lax.fori_loop(
        0,
        nblock,
        grad_step,
        (jnp.zeros((batch, CAP, heads, HD), f32), jnp.zeros(kv_all.shape, f32)),
    )
    kv_total = lax.psum_scatter(holder.astype(bf16), "seq", scatter_dimension=2, tiled=True)
    grad_qkv_rows = jnp.concatenate(
        [grad_query.reshape(query.shape)[None].astype(bf16), kv_total.astype(bf16)], axis=0
    )
    grad_qkv = jnp.einsum("srd,csre->cde", u_rows, grad_qkv_rows, preferred_element_type=f32)
    grad_u_part = jnp.einsum("csre,cde->srd", grad_qkv_rows, qkv_w, preferred_element_type=f32)
    part_gain_a = jnp.sum(grad_u_part * (x_wide * scale_a), axis=(0, 1))
    grad_u_all, grad_gain_a, grad_gain_m, grad_router = (
        lax.psum_scatter(
            grad_u_part.astype(jnp.bfloat16), "wa", scatter_dimension=0, tiled=True
        ).astype(jnp.float32),
        lax.psum_scatter(
            part_gain_a.astype(jnp.bfloat16), "wa", scatter_dimension=0, tiled=True
        ).astype(jnp.float32),
        lax.psum_scatter(
            grad_gain_m.astype(jnp.bfloat16), "wa", scatter_dimension=0, tiled=True
        ).astype(jnp.float32),
        lax.psum_scatter(
            grad_router.astype(jnp.bfloat16), "wa", scatter_dimension=0, tiled=True
        ).astype(jnp.float32),
    )
    grad_u_own = grad_u_all[0]
    grad_x_norm, unused = norm_back(x_keep, scale_a[side], gains_a, grad_u_own)
    grad_rows = grad_x_norm + grad_resid + grad_logit[:, None] * w_router.astype(f32)[None, :]
    grad_tokens = cotangent.astype(f32).at[0, own_rows].add(grad_rows).astype(bf16)
    shares = (grad_qkv, grad_out, grad_up, grad_down, grad_gain_a, grad_gain_m, grad_router)
    large = lax.psum(tuple(share.astype(bf16) for share in shares[:4]), "seq")
    small = lax.psum(shares[4:], "seq")
    summed = tuple(part.astype(f32) for part in large) + small
    return (
        mixed_out,
        grad_tokens,
        summed[0],
        summed[1],
        summed[2],
        summed[3],
        summed[4],
        summed[5],
        summed[6],
    )


def solution(mesh):
    return jax.shard_map(
        body,
        mesh=mesh,
        in_specs=(
            P("wa", "seq", None),
            P("wa", "seq", None),
            P(None, None, "wa"),
            P("wa", None),
            P(None, "wa"),
            P("wa", None),
            P("wa"),
            P("wa"),
            P("wa"),
            P(),
            P(),
        ),
        out_specs=(
            P("wa", "seq", None),
            P("wa", "seq", None),
            P(None, None, "wa"),
            P("wa", None),
            P(None, "wa"),
            P("wa", None),
            P("wa"),
            P("wa"),
            P("wa"),
        ),
        check_vma=False,
    )
```

```python
import functools

import jax
import jax.numpy as jnp
from jax import lax
from jax.experimental import pallas as pl
from jax.experimental.pallas import tpu as pltpu
from jax.sharding import PartitionSpec as P

HD = 64
EPS = 1e-05
NEG = -1e30
FAR = 1e9
LINES = 4
MESSAGES = 200
VMEM_BYTES = 64 << 20
MESH = pl.DeviceIdType.MESH
F32 = jnp.float32
BF16 = jnp.bfloat16
NN = (((1,), (0,)), ((), ()))
NT = (((1,), (1,)), ((), ()))
TN = (((0,), (0,)), ((), ()))
GELU_A = 0.7978845608028654
GELU_B = 0.044715


def mm(a, b, dims=NN):
    return lax.dot_general(a, b, dims, preferred_element_type=F32)


def gelu_parts(pre):
    square = pre * pre
    t = jnp.tanh(GELU_A * pre * (1.0 + GELU_B * square))
    half = 0.5 * (1.0 + t)
    slope = half + 0.5 * pre * (1.0 - t * t) * (GELU_A * (1.0 + 3.0 * GELU_B * square))
    return pre * half, slope


def row_scale(value):
    return lax.rsqrt(jnp.mean(value * value, axis=-1, keepdims=True) + EPS)


class Message:
    def __init__(self, links, i, ends):
        self.links, self.i, self.ends = links, i, ends

    def make(self):
        src, dst, device = self.ends()
        return pltpu.make_async_remote_copy(
            src_ref=src,
            dst_ref=dst,
            send_sem=self.links.send.at[self.i],
            recv_sem=self.links.recv.at[self.i],
            device_id=device,
            device_id_type=MESH,
        )

    def start(self):
        self.make().start()
        self.links.pending.append(self)
        return self

    def wait_recv(self):
        self.make().wait_recv()

    def wait_send(self):
        self.links.pending = [m for m in self.links.pending if m is not self]
        self.make().wait_send()

    def wait(self):
        self.wait_send()
        self.wait_recv()


class Links:
    def __init__(self, send, recv):
        self.send, self.recv, self.used, self.pending = send, recv, 0, []

    def message(self, ends):
        self.used += 1
        return Message(self, self.used - 1, ends)

    def copy(self, ends):
        return self.message(ends).start()

    def drain(self):
        for message in list(self.pending):
            message.wait_send()


class Place:
    def __init__(self, nz):
        self.me, self.c = lax.axis_index("seq"), lax.axis_index("wa")
        self.nz = nz
        self.z, self.l = lax.div(self.me, LINES), lax.rem(self.me, LINES)
        y, x = lax.div(self.l, 2), lax.rem(self.l, 2)
        over_y, over_x = self.l + 2 - 4 * y, self.l + 1 - 2 * x
        self.l2 = over_y * (1 - self.c) + over_x * self.c
        self.l3 = over_x * (1 - self.c) + over_y * self.c
        self.l23 = 3 - self.l
        self.sibling = (self.me, 1 - self.c)
        self.ks = (1, 3, 2) if nz == 4 else tuple(range(1, nz))

    def around(self, k):
        return lax.rem(self.z + k, self.nz)

    def at(self, z, line):
        return (z * LINES + line, self.c)


class Gather:
    def __init__(self, place, links, buf, lend, own=False):
        self.p, self.buf, self.lend, self.own = place, buf, lend, own
        p, ks = place, (0, *place.ks)

        def message(line, k, device):
            def ends():
                shard = buf().at[p.around(p.nz - k), line]
                return shard, shard, device()

            return links.message(ends)

        lines = (p.l, p.l2, p.l3, p.l23)
        self.first = {k: message(p.l, 0, lambda k=k: p.at(p.around(k), p.l)) for k in p.ks}
        self.second = {k: message(p.l, k, lambda: p.at(p.z, p.l2)) for k in ks}
        self.third = {(j, k): message(lines[j], k, lambda: p.at(p.z, p.l3)) for j in range(2) for k in ks}
        self.lent = {}
        if lend:
            keys = [(j, k) for j in range(4) for k in ks if j or k or own]
            self.lent = {key: message(lines[key[0]], key[1], lambda: p.sibling) for key in keys}
        self.waited = set()

    def hand_over(self, *key):
        if key in self.lent:
            self.lent[key].start()

    def start(self):
        self.hand_over(0, 0)
        self.second[0].start()
        self.third[0, 0].start()
        for k in self.p.ks:
            self.first[k].start()

    def from_z(self, k):
        self.first[k].wait_recv()
        self.third[0, k].start()
        self.second[k].start()
        self.hand_over(0, k)

    def from_second(self, k):
        self.second[k].wait_recv()
        self.third[1, k].start()
        self.hand_over(1, k)

    def from_third(self, j, k):
        self.third[j, k].wait_recv()
        self.hand_over(2 + j, k)

    def lent_line(self, j):
        for k in range(self.p.nz):
            if (j, k) in self.lent and (j, k) not in self.waited:
                self.waited.add((j, k))
                self.lent[j, k].wait_recv()

    def steps(self):
        ks = self.p.ks
        out = [functools.partial(self.from_z, k) for k in ks]
        out += [functools.partial(self.from_second, k) for k in (0, *ks)]
        out += [functools.partial(self.from_third, j, k) for j in range(2) for k in (0, *ks)]
        return out


class Scatter:
    def __init__(self, place, links, acc, got1, got2, got3):
        self.p = p = place
        self.acc, self.got1, self.got2, self.got3 = acc, got1, got2, got3
        self.order = (2, 1, 3, 0) if p.nz == 4 else (*range(1, p.nz), 0)

        def one(o, j, line):
            return lambda: (acc().at[p.around(o), line], got1().at[p.around(o), j], p.at(p.z, p.l3))

        def two(o):
            return lambda: (acc().at[p.around(o), p.l2], got2().at[p.around(o)], p.at(p.z, p.l2))

        def three(o):
            return lambda: (acc().at[p.around(o), p.l], got3().at[o - 1], p.at(p.around(o), p.l))

        self.m1 = {
            (j, o): links.message(one(o, j, line)) for o in self.order for j, line in ((0, p.l23), (1, p.l3))
        }
        self.m2 = {o: links.message(two(o)) for o in self.order}
        self.m3 = {o: links.message(three(o)) for o in range(1, p.nz)}

    def add(self, z, line, got):
        acc = self.acc()
        acc[z, line] = (acc[z, line].astype(F32) + got.astype(F32)).astype(BF16)

    def start(self):
        for message in self.m1.values():
            message.start()

    def stage2(self, o):
        p, zz = self.p, self.p.around(o)
        self.m1[0, o].wait_recv()
        self.add(zz, p.l2, self.got1()[zz, 0])
        self.m2[o].start()
        self.m1[1, o].wait_recv()
        self.add(zz, p.l, self.got1()[zz, 1])

    def stage3(self, o):
        p, zz = self.p, self.p.around(o)
        self.m2[o].wait_recv()
        if o:
            self.add(zz, p.l, self.got2()[zz])
            self.m3[o].start()

    def total(self):
        p = self.p
        total = self.acc()[p.z, p.l].astype(F32) + self.got2()[p.z].astype(F32)
        for o in range(1, p.nz):
            self.m3[o].wait_recv()
            total = total + self.got3()[o - 1].astype(F32)
        return total

    def steps(self):
        out = [functools.partial(self.stage2, self.order[0])]
        for now, before in zip(self.order[1:], self.order):
            out += [functools.partial(self.stage2, now), functools.partial(self.stage3, before)]
        return out + [functools.partial(self.stage3, self.order[-1])]


def layer_kernel(
    nz,
    tokens, cot, picked, counts, gain_a_r, gain_m_r, router_r, wqkv_h, wout_h, wup_h, wdown_h,
    pick_o, rows_o, grow_o, res_o, gup_o, gdown_o, small_o,
    wqkv, wout, wup, wdown, wsem,
    gvec, xall, uall, kall, vall, qst, bias, probs, att,
    dyb, attn_s, resid_s, logit_s, part, got_a, got_m,
    wall, gall, pre_s, act_s, gpre_s, dost, gq, gkv,
    gsib, gu1, gu2, gu3, share, sh1, sh2, sh3, res,
    sm, smz, smy, smx, smw, stage_u, stage_d, osem,
    send, recv,
):
    place = Place(nz)
    links = Links(send, recv)
    c, l, z = place.c, place.l, place.z
    other = 1 - c
    rows, width = grow_o.shape
    both = 2 * rows
    block = tokens.shape[0]
    half = wout.shape[0]
    pairs = half // 128
    nseq = nz * LINES
    total_rows = nseq * rows
    ff = wup.shape[1]
    ks = place.ks

    barrier = pltpu.get_barrier_semaphore()
    peers = [place.at(place.around(k), l) for k in range(1, nz)]
    peers += [place.at(z, place.l2), place.at(z, place.l3), place.sibling]
    for peer in peers:
        pl.semaphore_signal(barrier, inc=1, device_id=peer, device_id_type=MESH)
    loads = [
        pltpu.make_async_copy(h, v, wsem.at[i])
        for i, (h, v) in enumerate(((wqkv_h, wqkv), (wout_h, wout), (wup_h, wup), (wdown_h, wdown)))
    ]
    for load in loads:
        load.start()

    itself = lax.broadcasted_iota(jnp.int32, (rows, total_rows), 1) == (
        lax.broadcasted_iota(jnp.int32, (rows, total_rows), 0) + place.me * rows
    )
    picked_f = picked[...].astype(F32)
    own_index = [
        jnp.sum(jnp.where(itself, picked_f[s : s + 1], 0.0), axis=-1, keepdims=True) for s in range(2)
    ]
    own_row = jnp.where(c == 0, own_index[0], own_index[1])
    pick = jnp.where(
        lax.broadcasted_iota(jnp.int32, (rows, block), 1).astype(F32) == own_row, 1.0, 0.0
    ).astype(BF16)
    pick_o[...] = pick
    xall[c, z, l] = mm(pick, tokens[...]).astype(BF16)
    gvec[c] = jnp.zeros(gvec.shape[1:], F32)
    for i, ref in enumerate((gain_a_r, gain_m_r, router_r)):
        gvec[c, i : i + 1] = ref[...].astype(F32).reshape(1, half)
    pl.semaphore_wait(barrier, len(peers))

    gx = Gather(place, links, lambda: xall.at[c], True, own=True)
    gx.start()
    vec_copy = links.copy(lambda: (gvec.at[c], gvec.at[c], place.sibling))
    dyb[c] = mm(pick, cot[...]).astype(BF16)
    dy_copy = links.copy(lambda: (dyb.at[c], dyb.at[c], place.sibling))

    lane = lax.broadcasted_iota(jnp.int32, (2, total_rows), 1)
    stream = lax.broadcasted_iota(jnp.int32, (2, total_rows), 0)

    def place_keys(d, carry):
        until = d * rows + jnp.where(stream == 0, counts[0, d], counts[1, d])
        mine = (lane >= d * rows) & (lane < until)
        return jnp.where(mine, picked_f * nseq + d.astype(F32), carry)

    kpos = lax.fori_loop(0, nseq, place_keys, jnp.full((2, total_rows), FAR, F32))
    for s in range(2):
        near = kpos[s : s + 1] <= own_index[s] * nseq + place.me.astype(F32)
        bias[s] = jnp.where(near | itself, 0.0, NEG)
    slot = lax.broadcasted_iota(jnp.int32, (both, 1), 0)
    first = slot < rows
    own_live = jnp.where(
        slot - jnp.where(first, 0, rows) < jnp.where(first, counts[0, place.me], counts[1, place.me]), 1.0, 0.0
    )
    on_core = jnp.where(first, (1 - c).astype(F32), c.astype(F32))
    vec_copy.wait_recv()
    vectors = jnp.concatenate([gvec[0], gvec[1]], axis=1)
    gain_a, gain_m, router = vectors[0:1], vectors[1:2], vectors[2:3]
    loads[0].wait()

    def project(s, line):
        def norm(zz, carry):
            value = xall[s, zz, line].astype(F32)
            uall[s, zz, line] = (value * row_scale(value) * gain_a).astype(BF16)
            return carry

        lax.fori_loop(0, nz, norm, 0)
        u = jnp.concatenate([uall[s, zz, line] for zz in range(nz)], axis=0)
        for j, out in ((1, kall), (2, vall)):
            value = mm(u, wqkv[j]).astype(BF16)
            for p in range(pairs):
                for zz in range(nz):
                    out[s * pairs + p, zz, line] = value[
                        zz * rows : (zz + 1) * rows, p * 128 : (p + 1) * 128
                    ]

    def arrive(j):
        if j == 0:
            for k in ks:
                gx.from_z(k)
        if j == 1:
            for k in (0, *ks):
                gx.from_second(k)
            gx.lent_line(0)
        if j == 3:
            gx.lent_line(1)
        if j == 4:
            for k in (0, *ks):
                gx.from_third(0, k)
        if j == 5:
            gx.lent_line(2)
        if j == 6:
            for k in (0, *ks):
                gx.from_third(1, k)
        if j == 7:
            gx.lent_line(3)

    def take_line(j, carry):
        for i in (0, 1, 3, 4, 5, 6, 7):
            pl.when(j == i)(functools.partial(arrive, i))
        mine = lax.rem(j, 2) == 0
        step = lax.div(j, 2)
        one, two = jnp.where(mine, place.l2, place.l3), jnp.where(mine, place.l3, place.l2)
        line = jnp.where(
            step == 0, l, jnp.where(step == 1, one, jnp.where(step == 2, two, place.l23))
        )
        project(jnp.where(mine, c, other), line)
        return carry

    lax.fori_loop(0, 8, take_line, 0)
    early = links.used
    low = lax.broadcasted_iota(jnp.int32, (rows, 128), 1) < HD

    def stacked(value, s, p):
        piece = value[s * rows : (s + 1) * rows, p * 128 : (p + 1) * 128]
        zero = jnp.zeros_like(piece)
        return jnp.concatenate([jnp.where(low, piece, zero), jnp.where(low, zero, piece)], axis=0)

    own_u = uall[:, z, l].reshape(both, width)
    query = mm(own_u, wqkv[0]).astype(BF16) * jnp.asarray(HD ** (-0.5), BF16)
    for s in range(2):
        for p in range(pairs):
            qst[s * pairs + p] = stacked(query, s, p)

    def attend(i, carry):
        s, p = lax.div(i, pairs), lax.rem(i, pairs)
        keys = kall[i].reshape(total_rows, 128)
        vals = vall[i].reshape(total_rows, 128)
        hide = bias[s]
        raw = mm(qst[i], keys, NT) + jnp.concatenate([hide, hide], axis=0)
        expd = jnp.exp(raw - jnp.max(raw, axis=-1, keepdims=True))
        prob = expd * (1.0 / jnp.sum(expd, axis=-1, keepdims=True))
        probs[i] = prob
        out = mm(prob.astype(BF16), vals)
        at = pl.multiple_of(p * 128, 128)
        att[s, :, pl.ds(at, 128)] = jnp.where(low, out[:rows], out[rows:]).astype(BF16)
        return carry

    lax.fori_loop(0, 2 * pairs, attend, 0)
    loads[1].wait()
    part[...] = mm(att[...].reshape(both, half), wout[...])
    swap = links.copy(lambda: (part, got_a, place.sibling))
    x_both = xall[:, z, l].reshape(both, width).astype(F32)
    weight = jax.nn.sigmoid(jnp.sum(x_both * router, axis=-1, keepdims=True))
    lift = weight * own_live
    dy_copy.wait_recv()
    swap.wait()
    attn = part[...] + got_a[...]
    attn_s[...] = attn
    resid = x_both + attn
    resid_s[...] = resid
    w_both = (resid * row_scale(resid) * gain_m).astype(BF16)
    wall[:, z, l] = w_both.reshape(2, rows, width)
    gw = Gather(place, links, lambda: wall.at[c], True)
    gw.start()
    todo = gw.steps()

    def pump(n):
        for _ in range(min(n, len(todo))):
            todo.pop(0)()

    for load in loads[2:]:
        load.wait()

    fb = 384
    for b in range(ff // fb):
        cut = slice(b * fb, (b + 1) * fb)
        pre = mm(w_both, wup[:, cut])
        pre_s[:, cut] = pre
        act_s[:, cut] = gelu_parts(pre)[0].astype(BF16)
    pump(3)
    part[...] = mm(act_s[...], wdown[...])
    swap = links.copy(lambda: (part, got_m, place.sibling))
    pump(2)
    swap.wait()
    branch = attn_s[...] + (part[...] + got_m[...])
    x_both = xall[:, z, l].reshape(both, width).astype(F32)
    dy_both = dyb[...].reshape(both, width).astype(F32)
    grad_branch = dy_both * lift
    g_both = grad_branch.astype(BF16)
    gall[:, z, l] = g_both.reshape(2, rows, width)
    gg = Gather(place, links, lambda: gall.at[c], True)
    gg.start()
    todo += gg.steps()
    attn_s[...] = x_both + lift * branch
    rows_o[...] = attn_s[pl.ds(pl.multiple_of(c * rows, rows), rows), :].astype(BF16)
    grad_logit = (
        jnp.sum(dy_both * branch, axis=-1, keepdims=True) * own_live * weight * (1.0 - weight)
    )
    logit_s[...] = grad_logit
    sm[...] = jnp.zeros_like(sm)
    sm[2:3] = jnp.sum(grad_logit * on_core * x_both, axis=0, keepdims=True)
    pump(2)
    for b in range(ff // fb):
        cut = slice(b * fb, (b + 1) * fb)
        grad_act = mm(g_both, wdown[cut, :], NT)
        gpre_s[:, cut] = (gelu_parts(pre_s[:, cut])[1] * grad_act).astype(BF16)
    pump(2)
    part[...] = mm(gpre_s[...], wup[...], NT)
    swap = links.copy(lambda: (part, got_a, place.sibling))
    pump(2)
    swap.wait()
    grad_w = part[...] + got_a[...]
    resid = resid_s[...]
    scale_m = row_scale(resid)
    hat = resid * scale_m
    sm[1:2] = jnp.sum(grad_w * on_core * hat, axis=0, keepdims=True)
    lifted = grad_w * gain_m
    grad_resid = scale_m * (lifted - hat * jnp.mean(lifted * hat, axis=-1, keepdims=True))
    resid_s[...] = grad_resid
    ga_both = (dyb[...].reshape(both, width).astype(F32) * lift + grad_resid).astype(BF16)
    attended = att[...].reshape(both, half)
    piece = width // nseq
    grad_o = mm(attended, ga_both, TN).astype(BF16)
    for i in range(3):
        value = jnp.concatenate(
            [grad_o[:, 256 * i : 256 * i + 128], grad_o[:, 256 * i + 128 : 256 * i + 256]], axis=0
        )
        share[0, :, :, 0, i] = value.reshape(nz, LINES, piece, 128)
    grad_att = mm(ga_both, wout[...], NT).astype(BF16)
    for s in range(2):
        for p in range(pairs):
            dost[s * pairs + p] = stacked(grad_att, s, p)

    scatters = [
        Scatter(
            place, links, lambda g=g: share.at[g], lambda g=g: sh1.at[g], lambda g=g: sh2.at[g], lambda g=g: sh3.at[g]
        )
        for g in range(2)
    ]

    def attend_back(s, p):
        i = s * pairs + p
        keys = kall[i].reshape(total_rows, 128)
        vals = vall[i].reshape(total_rows, 128)
        prob = probs[i]
        grad_p = mm(dost[i], vals, NT)
        delta = jnp.sum(grad_p * prob, axis=-1, keepdims=True)
        grad_s = (prob * (grad_p - delta)).astype(BF16)
        out = mm(grad_s, keys) * HD ** (-0.5)
        gq[p, s] = jnp.where(low, out[:rows], out[rows:]).astype(BF16)
        gkv[p, s, :, :128] = mm(grad_s, qst[i], TN).astype(BF16)
        gkv[p, s, :, 128:] = mm(prob.astype(BF16), dost[i], TN).astype(BF16)

    def share_pair(p):
        group, unit = lax.div(p + 1, 2), lax.rem(p + 1, 2)
        grad_q = mm(uall[:, z, l].reshape(both, width), gq[p].reshape(both, 128), TN)
        share[group, :, :, unit, 0] = grad_q.astype(BF16).reshape(nz, LINES, piece, 128)
        span = width // 2

        def half_of(h, carry):
            at = pl.ds(pl.multiple_of(h * span, span), span)
            value = mm(uall[0, :, :, :, at].reshape(total_rows, span), gkv[p, 0], TN)
            value = value + mm(uall[1, :, :, :, at].reshape(total_rows, span), gkv[p, 1], TN)
            value = value.astype(BF16)
            zs = pl.ds(h * (nz // 2), nz // 2)
            for j in range(2):
                share[group, zs, :, unit, 1 + j] = value[:, 128 * j : 128 * (j + 1)].reshape(
                    nz // 2, LINES, piece, 128
                )
            return carry

        lax.fori_loop(0, 2, half_of, 0)

    counts_at = [3, 3, 3, 3, 3, 3]
    queue = [[todo.pop(0) for _ in range(min(n, len(todo)))] for n in counts_at]
    queue[-1] += todo
    del todo[:]

    def back(i, carry):
        p, s = lax.div(i, 2), lax.rem(i, 2)
        attend_back(s, p)
        pl.when(s == 1)(lambda: share_pair(p))
        for j, steps in enumerate(queue):

            def go(steps=steps, j=j):
                for step in steps:
                    step()
                if j == 1:
                    scatters[0].start()
                if j == 5:
                    scatters[1].start()

            pl.when(i == j)(go)
        return carry

    lax.fori_loop(0, 2 * pairs, back, 0)
    for message in list(links.pending):
        if message.i < early:
            message.wait_send()

    own_gq = jnp.concatenate([gq[p].reshape(both, 128) for p in range(pairs)], axis=1)
    part[...] = mm(own_gq, wqkv[0], NT)

    def grad_u(s, zz):
        at = pl.ds(pl.multiple_of(zz * (LINES * rows), LINES * rows), LINES * rows)
        gk = jnp.concatenate([gkv[p, s, at, :128] for p in range(pairs)], axis=1)
        gv = jnp.concatenate([gkv[p, s, at, 128:] for p in range(pairs)], axis=1)
        return mm(gk, wqkv[1], NT) + mm(gv, wqkv[2], NT)

    def part_of(s):
        return part[pl.ds(pl.multiple_of(s * rows, rows), rows), :]

    def theirs(j, carry):
        zz = place.around(j + 1)
        xall[other, zz] = grad_u(other, zz).astype(BF16).reshape(LINES, rows, width)
        return carry

    lax.fori_loop(0, nz, theirs, 0)
    xall[other, z, l] = (xall[other, z, l].astype(F32) + part_of(other)).astype(BF16)
    lent = [
        links.copy(
            lambda j=j: (xall.at[other, place.around(j + 1)], gsib.at[place.around(j + 1)], place.sibling)
        )
        for j in range(nz)
    ]

    def ours(j, gain_total):
        zz = place.around(j + 1)
        value = grad_u(c, zz).reshape(LINES, rows, width)
        for i in range(nz):
            pl.when(j == i)(lent[i].wait_recv)
        value = value + gsib[zz].astype(F32)
        rows_x = xall[c, zz].astype(F32)
        hat = rows_x * row_scale(rows_x)
        xall[c, zz] = value.astype(BF16)
        return gain_total + jnp.sum(value * hat, axis=(0, 1)).reshape(1, width)

    x_own = xall[c, z, l].astype(F32)
    gain_total = jnp.sum(part_of(c) * (x_own * row_scale(x_own)), axis=0, keepdims=True)
    attn_s[pl.ds(0, rows), :] = x_own
    gain_total = lax.fori_loop(0, nz, ours, gain_total)
    xall[c, z, l] = (xall[c, z, l].astype(F32) + part_of(c)).astype(BF16)
    sm[0:1] = gain_total
    reduce_u = Scatter(place, links, lambda: xall.at[c], lambda: gu1, lambda: gu2, lambda: gu3)
    reduce_u.start()
    for j in range(LINES):
        gw.lent_line(j)
        gg.lent_line(j)

    small = {
        "y": links.message(lambda: (smy.at[0], smy.at[1], place.at(z, place.l2))),
        "x": links.message(lambda: (smx.at[0], smx.at[1], place.at(z, place.l3))),
        "w": links.message(lambda: (smw.at[0], smw.at[1], place.sibling)),
    }
    for k in range(1, nz):
        small[k] = links.copy(
            lambda k=k: (sm, smz.at[k - 1], place.at(place.around(k), l))
        )

    def small_z():
        for k in range(1, nz):
            small[k].wait_recv()
        total = jnp.zeros(sm.shape, F32)
        for source in range(nz):
            for k in range(nz):
                piece = sm[...] if k == 0 else smz[k - 1]
                total = total + jnp.where(place.around(nz - k) == source, piece, 0.0)
        smy[0] = total
        small["y"].start()

    def small_2():
        small["y"].wait_recv()
        smx[0] = smy[0] + smy[1]
        small["x"].start()

    def small_3():
        small["x"].wait_recv()
        smw[0] = smx[0] + smx[1]
        small["w"].start()

    def small_4():
        small["w"].wait_recv()
        total = smw[0] + smw[1]
        small_o[...] = jnp.where(c == 0, total[:, :half], total[:, half:])

    gathers = [Gather(place, links, lambda g=g: res.at[g], False) for g in range(2)]

    def weights_out(g):
        res[g, z, l] = scatters[g].total().astype(BF16)
        gathers[g].start()

    def tokens_out():
        grad = reduce_u.total()
        own = attn_s[pl.ds(0, rows), :]
        scale = row_scale(own)
        hat = own * scale
        lifted = grad * gain_a
        grad_x = scale * (lifted - hat * jnp.mean(lifted * hat, axis=-1, keepdims=True))
        at = pl.ds(pl.multiple_of(c * rows, rows), rows)
        grow_o[...] = grad_x + resid_s[at, :] + logit_s[at, :] * router

    timed = []

    def plan(steps, begin, end):
        gap = (end - begin) / max(len(steps) - 1, 1)
        timed.extend((begin + gap * i, step) for i, step in enumerate(steps))

    plan(scatters[0].steps(), -3, -1)
    plan([functools.partial(weights_out, 0)], -1, -1)
    plan([small_z], 1, 1)
    plan(scatters[1].steps(), 0, 4)
    plan([functools.partial(weights_out, 1)], 4, 4)
    plan(gathers[0].steps(), 1, 7)
    plan(reduce_u.steps(), 3, 11)
    plan(gathers[1].steps(), 6, 14)
    plan([small_2, small_3, small_4], 5, 11)
    plan([tokens_out], 12, 12)

    slots, part_ff = stage_u.shape[:2]
    hb = slots * part_ff
    blocks = ff // hb
    tile = total_rows // 2
    tiles = 2 * total_rows // tile
    points = (tiles + 2) * blocks
    spread = [[] for _ in range(points + 1)]
    for at, step in sorted(timed, key=lambda pair: pair[0]):
        if at < 0:
            step()
        else:
            spread[min(int(at), points)].append(step)

    def put(b, i, which, stage, out):
        at = pl.ds(pl.multiple_of(b * hb + i * part_ff, part_ff), part_ff)
        return pltpu.make_async_copy(stage.at[i], out.at[at, :], osem.at[which, i])

    def pumps(point, among):
        for j in among:
            if spread[j]:

                def go(steps=spread[j]):
                    for step in steps:
                        step()

                pl.when(point == j)(go)

    def ff_block(b, carry):
        cut = pl.ds(pl.multiple_of(b * hb, hb), hb)

        def ff_tile(t, carry):
            s, h = lax.div(t, 2), lax.rem(t, 2)
            at = pl.ds(pl.multiple_of(h * tile, tile), tile)
            zz = pl.ds(h * (nz // 2), nz // 2)
            act, slope = gelu_parts(mm(wall[s, zz].reshape(tile, width), wup[:, cut]))
            uall[s, zz, :, :, :hb] = act.astype(BF16).reshape(nz // 2, LINES, rows, hb)
            grad_act = mm(gall[s, zz].reshape(tile, width), wdown[cut, :], NT)
            grad_pre = (slope * grad_act).astype(BF16)
            for i in range(slots):
                gkv[i, s, at] = grad_pre[:, part_ff * i : part_ff * (i + 1)]
            pumps(b * (tiles + 2) + t, [i for i in range(points) if i % (tiles + 2) < tiles])
            return carry

        lax.fori_loop(0, tiles, ff_tile, 0)

        def flush(which, stage, out, lhs, rhs):
            for i in range(slots):
                pl.when(b >= 1)(lambda i=i: put(b - 1, i, which, stage, out).wait())
                stage[i] = mm(lhs(i), rhs[...].reshape(2 * total_rows, width), TN).astype(BF16)
                put(b, i, which, stage, out).start()

        flush(
            0, stage_d, gdown_o,
            lambda i: uall[:, :, :, :, part_ff * i : part_ff * (i + 1)].reshape(2 * total_rows, part_ff), gall,
        )
        pumps(b * (tiles + 2) + tiles, range(tiles, points, tiles + 2))
        flush(1, stage_u, gup_o, lambda i: gkv[i].reshape(2 * total_rows, part_ff), wall)
        pumps(b * (tiles + 2) + tiles + 1, range(tiles + 1, points, tiles + 2))
        return carry

    lax.fori_loop(0, blocks, ff_block, 0)
    for step in spread[points]:
        step()
    out_copy = pltpu.make_async_copy(res, res_o, osem.at[2, 0])
    out_copy.start()
    for i in range(slots):
        put(blocks - 1, i, 0, stage_d, gdown_o).wait()
        put(blocks - 1, i, 1, stage_u, gup_o).wait()
    links.drain()
    out_copy.wait()


def finish_kernel(
    tokens, cot, pick, rows, grow, small, res_h, gup_h, gdown_h,
    mixed_o, gtok_o, gain_a_o, gain_m_o, router_o, gqkv_o, gout_o, gup_o, gdown_o,
    res, gup, gdown, qkv_s, out_s, up_s, down_s, sem_in, sem_out,
):
    up_cuts = [slice(i * 384, (i + 1) * 384) for i in range(gup.shape[0] // 384)]
    down_cuts = [slice(i * 384, (i + 1) * 384) for i in range(gdown.shape[0] // 384)]
    loads, stores = [], []

    def load(src, dst):
        loads.append(pltpu.make_async_copy(src, dst, sem_in.at[len(loads)]))
        loads[-1].start()
        return loads[-1]

    def store(src, dst):
        stores.append(pltpu.make_async_copy(src, dst, sem_out.at[len(stores)]))
        stores[-1].start()

    downs = [load(gdown_h.at[cut], gdown.at[cut]) for cut in down_cuts]
    groups = [load(res_h.at[g], res.at[g]) for g in range(2)]
    ups = [load(gup_h.at[cut], gup.at[cut]) for cut in up_cuts]
    for cut, got in zip(down_cuts, downs):
        got.wait()
        down_s[cut] = gdown[cut].astype(F32)
        store(down_s.at[cut], gdown_o.at[cut])
    width = rows.shape[1]
    half = width // 2
    for got in groups:
        got.wait()
    for i in range(3):
        for unit in range(1, 4):
            cut = slice((unit - 1) * 128, unit * 128)
            qkv_s[i, :, cut] = res[unit // 2, :, :, unit % 2, i].reshape(width, 128).astype(F32)
        store(qkv_s.at[i], gqkv_o.at[i])
        value = res[0, :, :, 0, i].reshape(width, 128).astype(F32)
        out_s[:, 256 * i : 256 * i + 128] = value[:half]
        out_s[:, 256 * i + 128 : 256 * i + 256] = value[half:]
    store(out_s, gout_o)
    for cut, got in zip(up_cuts, ups):
        got.wait()
        up_s[:, cut] = gup[cut].astype(F32).T
        store(up_s.at[:, cut], gup_o.at[:, cut])
    chosen = mm(pick[...], jnp.ones(rows.shape, BF16), TN) > 0.5
    mixed_o[...] = jnp.where(chosen, mm(pick[...], rows[...], TN), tokens[...].astype(F32)).astype(BF16)
    grad = grow[...]
    hi = grad.astype(BF16)
    rest = grad - hi.astype(F32)
    mid = rest.astype(BF16)
    lo = (rest - mid.astype(F32)).astype(BF16)
    spread = mm(pick[...], hi, TN) + (mm(pick[...], mid, TN) + mm(pick[...], lo, TN))
    gtok_o[...] = (cot[...].astype(F32) + spread).astype(BF16)
    gain_a_o[...] = small[0:1].reshape(half)
    gain_m_o[...] = small[1:2].reshape(half)
    router_o[...] = small[2:3].reshape(half)
    for made in stores:
        made.wait()


def fused_body(
    tokens, cotangent, w_qkv, w_out, w_up, w_down, gain_attn, gain_mlp, router, picked, counts
):
    nseq = lax.axis_size("seq")
    nz = nseq // LINES
    rows = picked.shape[1] // nseq
    block, width = tokens.shape[1:]
    half, ff = w_out.shape[0], w_up.shape[1]
    pairs = half // 128
    total_rows = nseq * rows
    piece = width // nseq
    vm = pltpu.VMEM
    dma = pltpu.SemaphoreType.DMA
    wide = (2, nz, LINES, rows, width)
    heads = (2 * pairs, nz, LINES, rows, 128)
    both = (2 * rows, width)
    part = (2, 3, piece, 128)
    scratch = [
        vm((3, width, half), BF16), vm((half, width), BF16), vm((width, ff), BF16), vm((ff, width), BF16), dma((4,)),
        vm((2, 8, half), F32), vm(wide, BF16), vm(wide, BF16), vm(heads, BF16), vm(heads, BF16),
        vm((2 * pairs, 2 * rows, 128), BF16), vm((2, rows, total_rows), F32),
        vm((2 * pairs, 2 * rows, total_rows), F32), vm((2, rows, half), BF16),
        vm((2, rows, width), BF16), vm(both, F32), vm(both, F32), vm((2 * rows, 1), F32),
        vm(both, F32), vm(both, F32), vm(both, F32),
        vm(wide, BF16), vm(wide, BF16), vm((2 * rows, ff), F32), vm((2 * rows, ff), BF16), vm((2 * rows, ff), BF16),
        vm((2 * pairs, 2 * rows, 128), BF16), vm((pairs, 2, rows, 128), BF16), vm((pairs, 2, total_rows, 256), BF16),
        vm((nz, LINES, rows, width), BF16), vm((nz, 2, rows, width), BF16), vm((nz, rows, width), BF16),
        vm((nz - 1, rows, width), BF16),
        vm((2, nz, LINES, *part), BF16), vm((2, nz, 2, *part), BF16), vm((2, nz, *part), BF16),
        vm((2, nz - 1, *part), BF16), vm((2, nz, LINES, *part), BF16),
        vm((8, width), F32), vm((nz - 1, 8, width), F32), vm((2, 8, width), F32), vm((2, 8, width), F32),
        vm((2, 8, width), F32),
        vm((2, 256, width), BF16), vm((2, 256, width), BF16), dma((3, 2)),
        dma((MESSAGES,)), dma((MESSAGES,)),
    ]
    in_vmem = pl.BlockSpec(memory_space=pltpu.VMEM)
    in_hbm = pl.BlockSpec(memory_space=pl.ANY)
    in_smem = pl.BlockSpec(memory_space=pltpu.SMEM)
    shaped = jax.ShapeDtypeStruct
    pick, out_rows, grad_rows, res, grad_up, grad_down, small = pl.pallas_call(
        functools.partial(layer_kernel, nz),
        out_shape=(
            shaped((rows, block), BF16),
            shaped((rows, width), BF16),
            shaped((rows, width), F32),
            shaped((2, nz, LINES, *part), BF16),
            shaped((ff, width), BF16),
            shaped((ff, width), BF16),
            shaped((8, half), F32),
        ),
        in_specs=[in_vmem] * 3 + [in_smem] + [in_vmem] * 3 + [in_hbm] * 4,
        out_specs=(in_vmem, in_vmem, in_vmem, in_hbm, in_hbm, in_hbm, in_vmem),
        scratch_shapes=scratch,
        compiler_params=pltpu.CompilerParams(
            collective_id=0, has_side_effects=True, vmem_limit_bytes=VMEM_BYTES
        ),
        name="layer",
    )(
        tokens[0], cotangent[0], picked, counts,
        gain_attn, gain_mlp, router, w_qkv, w_out, w_up, w_down,
    )
    mixed, grad_tokens, gain_a, gain_m, grad_r, grad_qkv, grad_out, grad_up, grad_down = pl.pallas_call(
        finish_kernel,
        out_shape=(
            shaped((block, width), BF16),
            shaped((block, width), BF16),
            shaped((half,), F32),
            shaped((half,), F32),
            shaped((half,), F32),
            shaped((3, width, half), F32),
            shaped((half, width), F32),
            shaped((width, ff), F32),
            shaped((ff, width), F32),
        ),
        in_specs=[in_vmem] * 6 + [in_hbm] * 3,
        out_specs=(in_vmem,) * 5 + (in_hbm,) * 4,
        scratch_shapes=[
            vm((2, nz, LINES, *part), BF16), vm((ff, width), BF16), vm((ff, width), BF16),
            vm((3, width, half), F32), vm((half, width), F32), vm((width, ff), F32), vm((ff, width), F32),
            dma((16,)), dma((16,)),
        ],
        compiler_params=pltpu.CompilerParams(vmem_limit_bytes=VMEM_BYTES),
        name="finish",
    )(tokens[0], cotangent[0], pick, out_rows, grad_rows, small, res, grad_up, grad_down)
    return (
        mixed[None], grad_tokens[None], grad_qkv, grad_out, grad_up, grad_down, gain_a, gain_m, grad_r,
    )


def body(tokens, *rest):
    nseq, cores = lax.axis_size("seq"), lax.axis_size("wa")
    fits = nseq == 4 * LINES and cores == 2 and rest[-2].shape[1] == nseq * CAP
    return (fused_body if fits else spread_body)(tokens, *rest)


CAP = 80


def norm_rows(value, gain):
    scale = lax.rsqrt(jnp.mean(value * value, axis=-1, keepdims=True) + EPS)
    return (value * scale * gain, scale)


def norm_back(value, scale, gain, grad_out):
    normed = value * scale
    weighted = grad_out * gain
    grad_value = scale * (weighted - normed * jnp.mean(weighted * normed, axis=-1, keepdims=True))
    return (grad_value, normed)


def gelu_back(pre, grad):
    unused, pull = jax.vjp(lambda value: jax.nn.gelu(value, approximate=True), pre)
    return pull(grad)[0]


def spread_body(
    tokens, cotangent, w_qkv, w_out, w_up, w_down, gain_attn, gain_mlp, router, picked, counts
):
    f32 = jnp.float32
    bf16 = jnp.bfloat16
    nseq = lax.axis_size("seq")
    me = lax.axis_index("seq")
    side = lax.axis_index("wa")
    slots = jnp.arange(CAP, dtype=jnp.int32)
    own_rows = lax.dynamic_slice(picked, (side, me * CAP), (1, CAP))[0]
    x_own = jnp.take(tokens[0], own_rows, axis=0)
    dy_own = jnp.take(cotangent[0], own_rows, axis=0).astype(f32)
    x_rows, g_attn, g_mlp, w_router = (
        lax.all_gather(x_own[None], "wa", axis=0, tiled=True),
        lax.all_gather(gain_attn, "wa", axis=0, tiled=True),
        lax.all_gather(gain_mlp, "wa", axis=0, tiled=True),
        lax.all_gather(router, "wa", axis=0, tiled=True),
    )
    qkv_w, out_w, up_w, down_w = (w_qkv, w_out, w_up, w_down)
    streams = jnp.arange(lax.axis_size("wa"))
    stream_picked = jnp.take(picked, streams, axis=0)
    stream_counts = jnp.take(counts, streams, axis=0)
    key_index = jnp.arange(nseq * CAP, dtype=jnp.int32)
    key_device = key_index // CAP
    key_pos = stream_picked * nseq + key_device[None, :]
    key_live = (key_index % CAP)[None, :] < jnp.take(stream_counts, key_device, axis=1)
    query_index = me * CAP + slots
    query_pos = lax.dynamic_slice_in_dim(key_pos, me * CAP, CAP, 1)
    own_live = (slots < counts[side, me]).astype(f32)
    gains_a = g_attn.astype(f32)
    gains_m = g_mlp.astype(f32)
    x_keep = x_own.astype(f32)
    weight = jax.nn.sigmoid(jnp.dot(x_own, w_router, preferred_element_type=f32))
    x_wide = x_rows.astype(f32)
    normed_a, scale_a = norm_rows(x_wide, gains_a)
    u_rows = normed_a.astype(bf16)
    qkv = jnp.einsum("srd,cde->csre", u_rows, qkv_w, preferred_element_type=f32).astype(bf16)
    query = qkv[0]
    local_kv = qkv[1:]
    batch = query.shape[0]
    heads = query.shape[-1] // HD
    factor = HD ** (-0.5)
    split_q = query.reshape(batch, CAP, heads, HD)
    kv_all = lax.all_gather(local_kv, "seq", axis=2, tiled=True)
    block = 8 * CAP
    nblock = kv_all.shape[2] // block

    def block_of(start):
        keys_b = lax.dynamic_slice_in_dim(kv_all[0], start, block, 1).reshape(
            batch, block, heads, HD
        )
        vals_b = lax.dynamic_slice_in_dim(kv_all[1], start, block, 1).reshape(
            batch, block, heads, HD
        )
        k_pos = lax.dynamic_slice_in_dim(key_pos, start, block, 1)
        k_live = lax.dynamic_slice_in_dim(key_live, start, block, 1)
        k_index = start + jnp.arange(block, dtype=jnp.int32)
        allowed = (k_pos[:, None, :] <= query_pos[:, :, None]) & (
            k_live[:, None, :] | (k_index[None, None, :] == query_index[None, :, None])
        )
        raw = jnp.einsum("sqhd,skhd->shqk", split_q, keys_b, preferred_element_type=f32) * factor
        return (keys_b, vals_b, allowed, jnp.where(allowed[:, None], raw, NEG))

    def max_sum(number, carry):
        top, total = carry
        unused_k, unused_v, allowed, scores = block_of(number * block)
        new_top = jnp.maximum(top, jnp.max(scores, axis=-1, keepdims=True))
        expd = jnp.where(allowed[:, None], jnp.exp(scores - new_top), 0.0)
        return (new_top, total * jnp.exp(top - new_top) + jnp.sum(expd, axis=-1, keepdims=True))

    top_start = jnp.full((batch, heads, CAP, 1), NEG, f32)
    top, total = lax.fori_loop(
        0, nblock, max_sum, (top_start, jnp.zeros((batch, heads, CAP, 1), f32))
    )
    lse = top + jnp.log(total)

    def weigh(number, acc):
        unused_k, vals_b, allowed, scores = block_of(number * block)
        probs_low = jnp.exp(scores - lse).astype(bf16)
        return acc + jnp.einsum("shqk,skhd->sqhd", probs_low, vals_b, preferred_element_type=f32)

    acc = lax.fori_loop(0, nblock, weigh, jnp.zeros((batch, CAP, heads, HD), f32))
    attended = acc.reshape(query.shape).astype(bf16)
    attn_part = jnp.einsum("sqe,ed->sqd", attended, out_w, preferred_element_type=f32)
    attn_own = lax.psum_scatter(attn_part, "wa", scatter_dimension=0, tiled=True)[0]
    resid = x_keep + attn_own
    normed_m, scale_m = norm_rows(resid, gains_m)
    w_own = normed_m.astype(bf16)
    w_rows = lax.all_gather(w_own[None], "wa", axis=0, tiled=True)
    pre = jnp.einsum("srd,df->srf", w_rows, up_w, preferred_element_type=f32)
    act = jax.nn.gelu(pre, approximate=True).astype(bf16)
    mlp_part = jnp.einsum("srf,fd->srd", act, down_w, preferred_element_type=f32)
    mlp_own = lax.psum_scatter(
        mlp_part.astype(jnp.bfloat16), "wa", scatter_dimension=0, tiled=True
    ).astype(jnp.float32)[0]
    branch = attn_own + mlp_own
    lift = (weight * own_live)[:, None]
    out_rows = (x_keep + lift * branch).astype(bf16)
    mixed_out = tokens.at[0, own_rows].set(out_rows)
    grad_branch = dy_own * lift
    grad_logit = jnp.sum(dy_own * branch, axis=-1) * own_live * weight * (1.0 - weight)
    grad_router = jnp.dot(grad_logit, x_keep, precision=lax.Precision.HIGHEST)
    grad_m = grad_branch.astype(bf16)
    grad_m_rows = lax.all_gather(grad_m[None], "wa", axis=0, tiled=True)
    grad_down = jnp.einsum("srf,srd->fd", act, grad_m_rows, preferred_element_type=f32)
    grad_act = jnp.einsum("srd,fd->srf", grad_m_rows, down_w, preferred_element_type=f32)
    grad_pre = gelu_back(pre, grad_act).astype(bf16)
    grad_up = jnp.einsum("srd,srf->df", w_rows, grad_pre, preferred_element_type=f32)
    grad_w_part = jnp.einsum("srf,df->srd", grad_pre, up_w, preferred_element_type=f32)
    grad_w_own = lax.psum_scatter(grad_w_part, "wa", scatter_dimension=0, tiled=True)[0]
    grad_resid, hat_m = norm_back(resid, scale_m, gains_m, grad_w_own)
    grad_gain_m = jnp.sum(grad_w_own * hat_m, axis=0)
    grad_a = (grad_branch + grad_resid).astype(bf16)
    grad_a_rows = lax.all_gather(grad_a[None], "wa", axis=0, tiled=True)
    grad_out = jnp.einsum("sqe,sqd->ed", attended, grad_a_rows, preferred_element_type=f32)
    grad_attended = jnp.einsum(
        "sqd,ed->sqe", grad_a_rows, out_w, preferred_element_type=f32
    ).astype(bf16)
    split_do = grad_attended.reshape(batch, CAP, heads, HD)

    def delta_step(number, delta):
        unused_k, vals_b, allowed, scores = block_of(number * block)
        probs = jnp.exp(scores - lse)
        grad_probs = jnp.einsum("sqhd,skhd->shqk", split_do, vals_b, preferred_element_type=f32)
        return delta + jnp.sum(grad_probs * probs, axis=-1, keepdims=True)

    delta = lax.fori_loop(0, nblock, delta_step, jnp.zeros((batch, heads, CAP, 1), f32))

    def grad_step(number, carry):
        grad_query, holder = carry
        start = number * block
        keys_b, vals_b, allowed, scores = block_of(start)
        probs = jnp.exp(scores - lse)
        grad_probs = jnp.einsum("sqhd,skhd->shqk", split_do, vals_b, preferred_element_type=f32)
        grad_scores = (probs * (grad_probs - delta)).astype(bf16)
        grad_query = (
            grad_query
            + jnp.einsum("shqk,skhd->sqhd", grad_scores, keys_b, preferred_element_type=f32)
            * factor
        )
        grad_keys = (
            jnp.einsum("shqk,sqhd->skhd", grad_scores, split_q, preferred_element_type=f32) * factor
        )
        grad_values = jnp.einsum(
            "shqk,sqhd->skhd", probs.astype(bf16), split_do, preferred_element_type=f32
        )
        paired = jnp.stack([grad_keys, grad_values]).reshape(2, batch, block, heads * HD)
        holder = lax.dynamic_update_slice_in_dim(holder, paired, start, 2)
        return (grad_query, holder)

    grad_query, holder = lax.fori_loop(
        0,
        nblock,
        grad_step,
        (jnp.zeros((batch, CAP, heads, HD), f32), jnp.zeros(kv_all.shape, f32)),
    )
    kv_total = lax.psum_scatter(holder.astype(bf16), "seq", scatter_dimension=2, tiled=True)
    grad_qkv_rows = jnp.concatenate(
        [grad_query.reshape(query.shape)[None].astype(bf16), kv_total.astype(bf16)], axis=0
    )
    grad_qkv = jnp.einsum("srd,csre->cde", u_rows, grad_qkv_rows, preferred_element_type=f32)
    grad_u_part = jnp.einsum("csre,cde->srd", grad_qkv_rows, qkv_w, preferred_element_type=f32)
    part_gain_a = jnp.sum(grad_u_part * (x_wide * scale_a), axis=(0, 1))
    grad_u_all, grad_gain_a, grad_gain_m, grad_router = (
        lax.psum_scatter(
            grad_u_part.astype(jnp.bfloat16), "wa", scatter_dimension=0, tiled=True
        ).astype(jnp.float32),
        lax.psum_scatter(
            part_gain_a.astype(jnp.bfloat16), "wa", scatter_dimension=0, tiled=True
        ).astype(jnp.float32),
        lax.psum_scatter(
            grad_gain_m.astype(jnp.bfloat16), "wa", scatter_dimension=0, tiled=True
        ).astype(jnp.float32),
        lax.psum_scatter(
            grad_router.astype(jnp.bfloat16), "wa", scatter_dimension=0, tiled=True
        ).astype(jnp.float32),
    )
    grad_u_own = grad_u_all[0]
    grad_x_norm, unused = norm_back(x_keep, scale_a[side], gains_a, grad_u_own)
    grad_rows = grad_x_norm + grad_resid + grad_logit[:, None] * w_router.astype(f32)[None, :]
    grad_tokens = cotangent.astype(f32).at[0, own_rows].add(grad_rows).astype(bf16)
    shares = (grad_qkv, grad_out, grad_up, grad_down, grad_gain_a, grad_gain_m, grad_router)
    large = lax.psum(tuple(share.astype(bf16) for share in shares[:4]), "seq")
    small = lax.psum(shares[4:], "seq")
    summed = tuple(part.astype(f32) for part in large) + small
    return (
        mixed_out,
        grad_tokens,
        summed[0],
        summed[1],
        summed[2],
        summed[3],
        summed[4],
        summed[5],
        summed[6],
    )


def solution(mesh):
    return jax.shard_map(
        body,
        mesh=mesh,
        in_specs=(
            P("wa", "seq", None),
            P("wa", "seq", None),
            P(None, None, "wa"),
            P("wa", None),
            P(None, "wa"),
            P("wa", None),
            P("wa"),
            P("wa"),
            P("wa"),
            P(),
            P(),
        ),
        out_specs=(
            P("wa", "seq", None),
            P("wa", "seq", None),
            P(None, None, "wa"),
            P("wa", None),
            P(None, "wa"),
            P("wa", None),
            P("wa"),
            P("wa"),
            P("wa"),
        ),
        check_vma=False,
    )
```

```python
import functools

import jax
import jax.numpy as jnp
from jax import lax
from jax.experimental import pallas as pl
from jax.experimental.pallas import tpu as pltpu
from jax.sharding import PartitionSpec as P

HD = 64
EPS = 1e-05
NEG = -1e30
FAR = 1e9
LINES = 4
MESSAGES = 420
VMEM_BYTES = 64 << 20
EARLY_ROWS = 48
COTANGENT_AT = 1
POINTS = {"x": 0, "a": 8, "p": 14, "b": 20, "v": 27, "u": 31, "h": 36, "z": 54}
SCHEDULE = (
    (0, 16, 21, 7, 15, 1, 2, 24, 22, 17, 18),
    (23, 26, 5, 3),
    (8, 6, 19, 4, 10, 27, 20),
    (9, 25),
    (30,),
    (33, 45, 51, 37, 11, 31),
    (28, 13, 52, 14, 29, 12),
    (46,),
    (56, 34, 38, 32, 48),
    (41, 49, 53),
    (35, 39),
    (),
    (47,),
    (36, 40, 42),
    (50, 57),
    (54, 55),
    (43,),
    (44,),
    (59,),
    (60, 63),
    (82, 75, 58, 67, 61, 81),
    (64, 83, 71, 68),
    (62,),
    (86, 78, 65),
    (155, 69, 76, 77, 79),
    (150, 154, 157, 156, 80),
    (72, 152),
    (151, 153, 70),
    (73, 87, 85),
    (),
    (66, 84),
    (),
    (168, 88, 163, 162),
    (166,),
    (),
    (167, 169, 158, 164, 159, 89, 165, 74),
    (160,),
    (171, 161),
    (188, 174),
    (170, 176),
    (186, 172),
    (179, 178),
    (181, 90, 175, 105, 91, 177, 180),
    (111, 189, 173, 187),
    (97, 106, 93, 112, 94),
    (107, 182, 98, 113, 92),
    (136, 135, 120, 108, 183, 121, 123, 95, 190, 109),
    (99, 184, 115, 116, 127),
    (114, 96),
    (142, 102, 117, 100, 128, 125),
    (141, 131, 118, 144, 185),
    (122, 137, 133, 129, 101),
    (110, 191, 126, 124, 103),
    (143, 146, 145, 132, 130, 134, 139, 138),
    (140, 192, 148, 147, 149, 119, 104),
)
MESH = pl.DeviceIdType.MESH
F32 = jnp.float32
BF16 = jnp.bfloat16
NN = (((1,), (0,)), ((), ()))
NT = (((1,), (1,)), ((), ()))
TN = (((0,), (0,)), ((), ()))
GELU_A = 0.7978845608028654
GELU_B = 0.044715


def mm(a, b, dims=NN):
    return lax.dot_general(a, b, dims, preferred_element_type=F32)


def gelu_parts(pre):
    square = pre * pre
    t = jnp.tanh(GELU_A * pre * (1.0 + GELU_B * square))
    half = 0.5 * (1.0 + t)
    slope = half + 0.5 * pre * (1.0 - t * t) * (GELU_A * (1.0 + 3.0 * GELU_B * square))
    return pre * half, slope


def row_scale(value):
    return lax.rsqrt(jnp.mean(value * value, axis=-1, keepdims=True) + EPS)


class Message:
    def __init__(self, links, i, ends):
        self.links, self.i, self.ends = links, i, ends

    def make(self):
        src, dst, device = self.ends()
        return pltpu.make_async_remote_copy(
            src_ref=src,
            dst_ref=dst,
            send_sem=self.links.send.at[self.i],
            recv_sem=self.links.recv.at[self.i],
            device_id=device,
            device_id_type=MESH,
        )

    def start(self):
        self.make().start()
        self.links.pending.append(self)
        return self

    def wait_recv(self):
        self.make().wait_recv()

    def wait_send(self):
        self.links.forget(self)
        self.make().wait_send()

    def wait(self):
        self.wait_send()
        self.wait_recv()


class Links:
    def __init__(self, send, recv):
        self.send, self.recv, self.used, self.pending = send, recv, 0, []

    def many(self, count):
        self.used += count
        return self.used - count

    def numbered(self, i, ends):
        return Message(self, i, ends)

    def forget(self, what):
        self.pending = [other for other in self.pending if other is not what]

    def message(self, ends):
        return self.numbered(self.many(1), ends)

    def copy(self, ends):
        return self.message(ends).start()

    def drain(self):
        for message in list(self.pending):
            message.wait_send()


class Place:
    def __init__(self, nz):
        self.me, self.c = lax.axis_index("seq"), lax.axis_index("wa")
        self.nz = nz
        self.z, self.l = lax.div(self.me, LINES), lax.rem(self.me, LINES)
        y, x = lax.div(self.l, 2), lax.rem(self.l, 2)
        over_y, over_x = self.l + 2 - 4 * y, self.l + 1 - 2 * x
        self.l2 = over_y * (1 - self.c) + over_x * self.c
        self.l3 = over_x * (1 - self.c) + over_y * self.c
        self.l23 = 3 - self.l
        self.sibling = (self.me, 1 - self.c)
        near = [sorted(range(nz), key=lambda other: abs(other - here)) for here in range(nz)]
        self.sources = []
        for i in range(nz):
            source = near[0][i] + 0 * self.z
            for here in range(1, nz):
                source = jnp.where(self.z == here, near[here][i], source)
            self.sources.append(source)

    def turn(self, i):
        return self.sources[i]

    def around(self, k):
        return lax.rem(self.z + k, self.nz)

    def at(self, z, line):
        return (z * LINES + line, self.c)


class Chain:
    def __init__(self, place, links, shard):
        self.p, self.links, self.shard = place, links, shard
        self.i = links.many(2 * place.nz)

    def hop(self, source, to, down, hops):
        i = self.i + down * self.p.nz + hops
        return self.links.numbered(
            i, lambda: (self.shard(source), self.shard(source), self.p.at(to, self.p.l))
        )

    def start(self):
        p = self.p
        pl.when(p.z + 1 < p.nz)(lambda: self.hop(p.z, p.z + 1, 0, 1).make().start())
        pl.when(p.z > 0)(lambda: self.hop(p.z, p.z - 1, 1, 1).make().start())
        self.links.pending.append(self)

    def arrive(self, i):
        p = self.p
        source = p.turn(i)
        down = jnp.where(source > p.z, 1, 0)
        hops = jnp.where(source > p.z, source - p.z, p.z - source)
        self.hop(source, p.z, down, hops).wait_recv()
        on = p.z + 1 - 2 * down
        pl.when((on >= 0) & (on < p.nz))(lambda: self.hop(source, on, down, hops + 1).make().start())

    def wait_send(self):
        p = self.p
        self.links.forget(self)
        for hops in range(1, p.nz):
            up = (p.z + 1 < p.nz) & (p.z >= hops - 1)
            down = (p.z > 0) & (p.z + hops - 1 < p.nz)
            pl.when(up)(lambda: self.hop(p.z, p.z, 0, hops).make().wait_send())
            pl.when(down)(lambda: self.hop(p.z, p.z, 1, hops).make().wait_send())


class Gather:
    def __init__(self, place, links, buf, lend, own=False, early=True, cut=None):
        self.p = p = place
        self.early = early
        lines = (p.l, p.l2, p.l3, p.l23)

        def at(source, line):
            ref = buf().at[source, line]
            return ref if cut is None else ref.at[cut]

        def message(j, i, device):
            def ends():
                shard = at(p.turn(i), lines[j])
                return shard, shard, device()

            return links.message(ends)

        over = range(p.nz)
        self.second = {i: message(0, i, lambda: p.at(p.z, p.l2)) for i in (over if early else (0,))}
        self.third = {(j, i): message(j, i, lambda: p.at(p.z, p.l3)) for j in range(2) for i in over}
        self.chains = [Chain(place, links, lambda s, j=j: at(s, lines[j])) for j in range(1 if early else 2)]
        keys = [(j, i) for j in range(4) for i in over if j or i or own] if lend else []
        self.lent = {key: message(*key, lambda: p.sibling) for key in keys}
        self.waited = set()
        self.all = [*self.second.values(), *self.third.values(), *self.lent.values(), *self.chains]

    def wait_sent(self):
        for message in self.all:
            message.wait_send()

    def hand_over(self, *key):
        if key in self.lent:
            self.lent[key].start()

    def start(self):
        self.chains[0].start()
        self.second[0].start()
        self.third[0, 0].start()
        self.hand_over(0, 0)

    def over_z(self, j, i):
        self.chains[j].arrive(i)
        self.third[j, i].start()
        if self.early:
            self.second[i].start()
        self.hand_over(j, i)

    def over_second(self, i):
        self.second[i].wait_recv()
        if not self.early:
            self.chains[1].start()
        self.third[1, i].start()
        self.hand_over(1, i)

    def over_third(self, j, i):
        self.third[j, i].wait_recv()
        self.hand_over(2 + j, i)

    def lent_own(self):
        self.waited.add((0, 0))
        self.lent[0, 0].wait_recv()

    def lent_line(self, j):
        for i in range(self.p.nz):
            if (j, i) in self.lent and (j, i) not in self.waited:
                self.waited.add((j, i))
                self.lent[j, i].wait_recv()

    def steps(self):
        part, over = functools.partial, range(self.p.nz)
        out = [part(self.over_z, j, i) for j in range(len(self.chains)) for i in over[1:]]
        out += [part(self.over_second, i) for i in self.second]
        return out + [part(self.over_third, j, i) for j, i in self.third]


def two_ways(place, links, buf, lend, own=False, cuts=(None, None)):
    return [
        Gather(place, links, buf, lend, own, early=early, cut=cut) for early, cut in zip((True, False), cuts)
    ]


class Scatter:
    def __init__(self, place, links, acc, got1, got2, got3):
        self.p = p = place
        self.acc, self.got1, self.got2, self.got3 = acc, got1, got2, got3
        self.order = (2, 1, 3, 0) if p.nz == 4 else (*range(1, p.nz), 0)

        def one(o, j, line):
            return lambda: (acc().at[p.around(o), line], got1().at[p.around(o), j], p.at(p.z, p.l3))

        def two(o):
            return lambda: (acc().at[p.around(o), p.l2], got2().at[p.around(o)], p.at(p.z, p.l2))

        def three(o):
            return lambda: (acc().at[p.around(o), p.l], got3().at[o - 1], p.at(p.around(o), p.l))

        self.m1 = {
            (j, o): links.message(one(o, j, line)) for o in self.order for j, line in ((0, p.l23), (1, p.l3))
        }
        self.m2 = {o: links.message(two(o)) for o in self.order}
        self.m3 = {o: links.message(three(o)) for o in range(1, p.nz)}

    def add(self, z, line, got):
        acc = self.acc()
        acc[z, line] = (acc[z, line].astype(F32) + got.astype(F32)).astype(BF16)

    def start(self):
        for message in self.m1.values():
            message.start()

    def far(self, o):
        p, zz = self.p, self.p.around(o)
        self.m1[0, o].wait_recv()
        self.add(zz, p.l2, self.got1()[zz, 0])
        self.m2[o].start()

    def near(self, o):
        p, zz = self.p, self.p.around(o)
        self.m1[1, o].wait_recv()
        self.add(zz, p.l, self.got1()[zz, 1])

    def along(self, o):
        p, zz = self.p, self.p.around(o)
        self.m2[o].wait_recv()
        if o:
            self.add(zz, p.l, self.got2()[zz])
            self.m3[o].start()

    def total(self):
        p = self.p
        total = self.acc()[p.z, p.l].astype(F32) + self.got2()[p.z].astype(F32)
        for o in range(1, p.nz):
            self.m3[o].wait_recv()
            total = total + self.got3()[o - 1].astype(F32)
        return total

    def steps(self):
        return [functools.partial(step, o) for step in (self.far, self.near, self.along) for o in self.order]


def layer_kernel(
    nz,
    tokens_h, cot_h, picked, counts, gain_a_r, gain_m_r, router_r, wqkv_h, wout_h, wup_h, wdown_h,
    pick_o, rows_o, grow_o, res_o, gup_o, gdown_o, small_o,
    tokens, cot, wqkv, wout, wup, wdown, wsem,
    gvec, xall, uall, kall, vall, qst, bias, probs, att,
    dy_s, attn_s, resid_s, logit_s, part, got_a, got_m,
    wall, gall, pre_s, act_s, gpre_s, dost, gq, gkv,
    gsib, gu1, gu2, gu3, share, sh1, sh2, sh3, res,
    sm, smz, smy, smx, smw, stage_u, stage_d, osem,
    send, recv,
):
    place = Place(nz)
    links = Links(send, recv)
    c, l, z = place.c, place.l, place.z
    other = 1 - c
    rows, width = grow_o.shape
    both = 2 * rows
    block = tokens.shape[0]
    half = wout.shape[0]
    pairs = half // 128
    nseq = nz * LINES
    total_rows = nseq * rows
    ff = wup.shape[1]

    barrier = pltpu.get_barrier_semaphore()
    peers = [place.at(z, place.l2), place.at(z, place.l3), place.sibling]
    for peer in peers:
        pl.semaphore_signal(barrier, inc=1, device_id=peer, device_id_type=MESH)

    def greet(on):
        pl.semaphore_signal(barrier, inc=1, device_id=place.at(on, l), device_id_type=MESH)

    pl.when(z + 1 < nz)(lambda: greet(z + 1))
    pl.when(z > 0)(lambda: greet(z - 1))
    loads = [
        pltpu.make_async_copy(h, v, wsem.at[i])
        for i, (h, v) in enumerate(
            ((tokens_h, tokens), (cot_h, cot), (wqkv_h, wqkv), (wout_h, wout), (wup_h, wup), (wdown_h, wdown))
        )
    ]
    for load in loads[:2]:
        load.start()

    cuts = (pl.ds(0, EARLY_ROWS), pl.ds(EARLY_ROWS, rows - EARLY_ROWS))
    gx = two_ways(place, links, lambda: xall.at[c], True, True, cuts)
    gw = two_ways(place, links, lambda: wall.at[c], True, False, cuts)
    gg = two_ways(place, links, lambda: gall.at[c], True, True, cuts)
    scatters = [
        Scatter(
            place, links, lambda g=g: share.at[g], lambda g=g: sh1.at[g], lambda g=g: sh2.at[g], lambda g=g: sh3.at[g]
        )
        for g in range(2)
    ]
    gathers = [two_ways(place, links, lambda g=g: res.at[g], False, False, (0, 1)) for g in range(2)]
    reduce_u = Scatter(place, links, lambda: xall.at[c], lambda: gu1, lambda: gu2, lambda: gu3)
    small = {
        "y": links.message(lambda: (smy.at[0], smy.at[1], place.at(z, place.l2))),
        "x": links.message(lambda: (smx.at[0], smx.at[1], place.at(z, place.l3))),
        "w": links.message(lambda: (smw.at[0], smw.at[1], place.sibling)),
    }
    for k in range(1, nz):
        small[k] = links.message(lambda k=k: (sm, smz.at[k - 1], place.at(place.around(k), l)))

    def begin(flows):
        for flow in flows:
            flow.start()

    def small_z():
        for k in range(1, nz):
            small[k].wait_recv()
        total = jnp.zeros(sm.shape, F32)
        for source in range(nz):
            for k in range(nz):
                piece = sm[...] if k == 0 else smz[k - 1]
                total = total + jnp.where(place.around(nz - k) == source, piece, 0.0)
        smy[0] = total
        small["y"].start()

    def small_2():
        small["y"].wait_recv()
        smx[0] = smy[0] + smy[1]
        small["x"].start()

    def small_3():
        small["x"].wait_recv()
        smw[0] = smx[0] + smx[1]
        small["w"].start()

    def small_4():
        small["w"].wait_recv()
        total = smw[0] + smw[1]
        small_o[...] = jnp.where(c == 0, total[:, :half], total[:, half:])

    def weights_out(g):
        res[g, z, l] = scatters[g].total().astype(BF16)
        begin(gathers[g])

    def tokens_out():
        grad = reduce_u.total()
        own = attn_s[pl.ds(0, rows), :]
        scale = row_scale(own)
        hat = own * scale
        lifted = grad * gain_a
        grad_x = scale * (lifted - hat * jnp.mean(lifted * hat, axis=-1, keepdims=True))
        at = pl.ds(pl.multiple_of(c * rows, rows), rows)
        grow_o[...] = grad_x + resid_s[at, :] + logit_s[at, :] * router

    slots, part_ff = stage_u.shape[:2]
    hb = slots * part_ff
    blocks = ff // hb
    tile = total_rows // 2
    tiles = 2 * total_rows // tile
    per_block = tiles + 2
    steps = [step for flows in (gx, gg, gw, *gathers) for flow in flows for step in flow.steps()]
    steps += [step for scatter in (*scatters, reduce_u) for step in scatter.steps()]
    steps += [functools.partial(weights_out, g) for g in range(2)]
    steps += [small_z, small_2, small_3, small_4, tokens_out]
    left = set(range(len(steps)))

    def pump(kind, j):
        for i in SCHEDULE[POINTS[kind] + j]:
            left.remove(i)
            steps[i]()

    def pump_in(index, kind, among):
        for j in among:
            if SCHEDULE[POINTS[kind] + j]:
                pl.when(index == j)(functools.partial(pump, kind, j))

    itself = lax.broadcasted_iota(jnp.int32, (rows, total_rows), 1) == (
        lax.broadcasted_iota(jnp.int32, (rows, total_rows), 0) + place.me * rows
    )
    picked_f = picked[...].astype(F32)
    own_index = [
        jnp.sum(jnp.where(itself, picked_f[s : s + 1], 0.0), axis=-1, keepdims=True) for s in range(2)
    ]
    own_row = jnp.where(c == 0, own_index[0], own_index[1])
    pick = jnp.where(
        lax.broadcasted_iota(jnp.int32, (rows, block), 1).astype(F32) == own_row, 1.0, 0.0
    ).astype(BF16)
    pick_o[...] = pick
    loads[0].wait()
    xall[c, z, l] = mm(pick, tokens[...]).astype(BF16)
    gvec[c] = jnp.zeros(gvec.shape[1:], F32)
    for i, ref in enumerate((gain_a_r, gain_m_r, router_r)):
        gvec[c, i : i + 1] = ref[...].astype(F32).reshape(1, half)
    pl.semaphore_wait(barrier, len(peers) + jnp.where(z + 1 < nz, 1, 0) + jnp.where(z > 0, 1, 0))

    begin(gx)
    for load in loads[2:]:
        load.start()
    vec_copy = links.copy(lambda: (gvec.at[c], gvec.at[c], place.sibling))
    loads[1].wait()
    gall[c, z, l] = mm(pick, cot[...]).astype(BF16)

    lane = lax.broadcasted_iota(jnp.int32, (2, total_rows), 1)
    stream = lax.broadcasted_iota(jnp.int32, (2, total_rows), 0)

    def place_keys(d, carry):
        until = d * rows + jnp.where(stream == 0, counts[0, d], counts[1, d])
        mine = (lane >= d * rows) & (lane < until)
        return jnp.where(mine, picked_f * nseq + d.astype(F32), carry)

    kpos = lax.fori_loop(0, nseq, place_keys, jnp.full((2, total_rows), FAR, F32))
    for s in range(2):
        near = kpos[s : s + 1] <= own_index[s] * nseq + place.me.astype(F32)
        bias[s] = jnp.where(near | itself, 0.0, NEG)
    slot = lax.broadcasted_iota(jnp.int32, (both, 1), 0)
    first = slot < rows
    own_live = jnp.where(
        slot - jnp.where(first, 0, rows) < jnp.where(first, counts[0, place.me], counts[1, place.me]), 1.0, 0.0
    )
    on_core = jnp.where(first, (1 - c).astype(F32), c.astype(F32))
    vec_copy.wait_recv()
    vectors = jnp.concatenate([gvec[0], gvec[1]], axis=1)
    gain_a, gain_m, router = vectors[0:1], vectors[1:2], vectors[2:3]
    loads[2].wait()

    def project(s, line):
        def norm(zz, carry):
            value = xall[s, zz, line].astype(F32)
            uall[s, zz, line] = (value * row_scale(value) * gain_a).astype(BF16)
            return carry

        lax.fori_loop(0, nz, norm, 0)
        u = jnp.concatenate([uall[s, zz, line] for zz in range(nz)], axis=0)
        for j, out in ((1, kall), (2, vall)):
            value = mm(u, wqkv[j]).astype(BF16)
            for p in range(pairs):
                for zz in range(nz):
                    out[s * pairs + p, zz, line] = value[
                        zz * rows : (zz + 1) * rows, p * 128 : (p + 1) * 128
                    ]

    def arrive(j):
        pump("x", j)
        if j % 2:
            for flow in gx:
                flow.lent_line(j // 2)
        if j == COTANGENT_AT:
            begin(gg)

    def take_line(j, carry):
        for i in range(8):
            pl.when(j == i)(functools.partial(arrive, i))
        mine = lax.rem(j, 2) == 0
        step = lax.div(j, 2)
        one, two = jnp.where(mine, place.l2, place.l3), jnp.where(mine, place.l3, place.l2)
        line = jnp.where(
            step == 0, l, jnp.where(step == 1, one, jnp.where(step == 2, two, place.l23))
        )
        project(jnp.where(mine, c, other), line)
        return carry

    lax.fori_loop(0, 8, take_line, 0)
    low = lax.broadcasted_iota(jnp.int32, (rows, 128), 1) < HD

    def stacked(value, s, p):
        piece = value[s * rows : (s + 1) * rows, p * 128 : (p + 1) * 128]
        zero = jnp.zeros_like(piece)
        return jnp.concatenate([jnp.where(low, piece, zero), jnp.where(low, zero, piece)], axis=0)

    own_u = uall[:, z, l].reshape(both, width)
    query = mm(own_u, wqkv[0]).astype(BF16) * jnp.asarray(HD ** (-0.5), BF16)
    for s in range(2):
        for p in range(pairs):
            qst[s * pairs + p] = stacked(query, s, p)

    def attend(i, carry):
        s, p = lax.div(i, pairs), lax.rem(i, pairs)
        keys = kall[i].reshape(total_rows, 128)
        vals = vall[i].reshape(total_rows, 128)
        hide = bias[s]
        raw = mm(qst[i], keys, NT) + jnp.concatenate([hide, hide], axis=0)
        expd = jnp.exp(raw - jnp.max(raw, axis=-1, keepdims=True))
        prob = expd * (1.0 / jnp.sum(expd, axis=-1, keepdims=True))
        probs[i] = prob
        out = mm(prob.astype(BF16), vals)
        at = pl.multiple_of(p * 128, 128)
        att[s, :, pl.ds(at, 128)] = jnp.where(low, out[:rows], out[rows:]).astype(BF16)
        pump_in(i, "a", range(2 * pairs))
        return carry

    lax.fori_loop(0, 2 * pairs, attend, 0)
    loads[3].wait()
    part[...] = mm(att[...].reshape(both, half), wout[...])
    swap = links.copy(lambda: (part, got_a, place.sibling))
    x_both = xall[:, z, l].reshape(both, width).astype(F32)
    pump("p", 0)
    weight = jax.nn.sigmoid(jnp.sum(x_both * router, axis=-1, keepdims=True))
    lift = weight * own_live
    for flow in gg:
        flow.lent_own()
    swap.wait()
    attn = part[...] + got_a[...]
    attn_s[...] = attn
    resid = x_both + attn
    resid_s[...] = resid
    w_both = (resid * row_scale(resid) * gain_m).astype(BF16)
    wall[:, z, l] = w_both.reshape(2, rows, width)
    begin(gw)
    for load in loads[4:]:
        load.wait()

    fb = 384
    for b in range(ff // fb):
        cut = slice(b * fb, (b + 1) * fb)
        pre = mm(w_both, wup[:, cut])
        pre_s[:, cut] = pre
        act_s[:, cut] = gelu_parts(pre)[0].astype(BF16)
    pump("p", 1)
    part[...] = mm(act_s[...], wdown[...])
    swap = links.copy(lambda: (part, got_m, place.sibling))
    pump("p", 2)
    swap.wait()
    branch = attn_s[...] + (part[...] + got_m[...])
    x_both = xall[:, z, l].reshape(both, width).astype(F32)
    dy_both = gall[:, z, l].reshape(both, width).astype(F32)
    grad_branch = dy_both * lift
    g_both = grad_branch.astype(BF16)
    attn_s[...] = x_both + lift * branch
    rows_o[...] = attn_s[pl.ds(pl.multiple_of(c * rows, rows), rows), :].astype(BF16)
    grad_logit = (
        jnp.sum(dy_both * branch, axis=-1, keepdims=True) * own_live * weight * (1.0 - weight)
    )
    logit_s[...] = grad_logit
    sm[...] = jnp.zeros_like(sm)
    sm[2:3] = jnp.sum(grad_logit * on_core * x_both, axis=0, keepdims=True)
    pump("p", 3)
    for b in range(ff // fb):
        cut = slice(b * fb, (b + 1) * fb)
        grad_act = mm(g_both, wdown[cut, :], NT)
        gpre_s[:, cut] = (gelu_parts(pre_s[:, cut])[1] * grad_act).astype(BF16)
    pump("p", 4)
    part[...] = mm(gpre_s[...], wup[...], NT)
    swap = links.copy(lambda: (part, got_a, place.sibling))
    pump("p", 5)
    swap.wait()
    grad_w = part[...] + got_a[...]
    resid = resid_s[...]
    scale_m = row_scale(resid)
    hat = resid * scale_m
    sm[1:2] = jnp.sum(grad_w * on_core * hat, axis=0, keepdims=True)
    lifted = grad_w * gain_m
    grad_resid = scale_m * (lifted - hat * jnp.mean(lifted * hat, axis=-1, keepdims=True))
    resid_s[...] = grad_resid
    ga_both = (gall[:, z, l].reshape(both, width).astype(F32) * lift + grad_resid).astype(BF16)
    attended = att[...].reshape(both, half)
    piece = width // nseq
    grad_o = mm(attended, ga_both, TN).astype(BF16)
    for i in range(3):
        value = jnp.concatenate(
            [grad_o[:, 256 * i : 256 * i + 128], grad_o[:, 256 * i + 128 : 256 * i + 256]], axis=0
        )
        share[0, :, :, 0, i] = value.reshape(nz, LINES, piece, 128)
    grad_att = mm(ga_both, wout[...], NT).astype(BF16)
    for s in range(2):
        for p in range(pairs):
            dost[s * pairs + p] = stacked(grad_att, s, p)

    def attend_back(s, p):
        i = s * pairs + p
        keys = kall[i].reshape(total_rows, 128)
        vals = vall[i].reshape(total_rows, 128)
        prob = probs[i]
        grad_p = mm(dost[i], vals, NT)
        delta = jnp.sum(grad_p * prob, axis=-1, keepdims=True)
        grad_s = (prob * (grad_p - delta)).astype(BF16)
        out = mm(grad_s, keys) * HD ** (-0.5)
        gq[p, s] = jnp.where(low, out[:rows], out[rows:]).astype(BF16)
        gkv[p, s, :, :128] = mm(grad_s, qst[i], TN).astype(BF16)
        gkv[p, s, :, 128:] = mm(prob.astype(BF16), dost[i], TN).astype(BF16)

    def share_pair(p):
        group, unit = lax.div(p + 1, 2), lax.rem(p + 1, 2)
        grad_q = mm(uall[:, z, l].reshape(both, width), gq[p].reshape(both, 128), TN)
        share[group, :, :, unit, 0] = grad_q.astype(BF16).reshape(nz, LINES, piece, 128)
        span = width // 2

        def half_of(h, carry):
            at = pl.ds(pl.multiple_of(h * span, span), span)
            value = mm(uall[0, :, :, :, at].reshape(total_rows, span), gkv[p, 0], TN)
            value = value + mm(uall[1, :, :, :, at].reshape(total_rows, span), gkv[p, 1], TN)
            value = value.astype(BF16)
            zs = pl.ds(h * (nz // 2), nz // 2)
            for j in range(2):
                share[group, zs, :, unit, 1 + j] = value[:, 128 * j : 128 * (j + 1)].reshape(
                    nz // 2, LINES, piece, 128
                )
            return carry

        lax.fori_loop(0, 2, half_of, 0)

    def back(i, carry):
        p, s = lax.div(i, 2), lax.rem(i, 2)
        attend_back(s, p)
        pl.when(s == 1)(lambda: share_pair(p))
        pl.when(i == 1)(scatters[0].start)
        pl.when(i == 2 * pairs - 1)(scatters[1].start)
        pump_in(i, "b", range(2 * pairs))
        return carry

    lax.fori_loop(0, 2 * pairs, back, 0)
    for flow in gx:
        flow.wait_sent()

    pump("b", 6)
    for flow in gg:
        for j in range(LINES):
            flow.lent_line(j)
        flow.wait_sent()

    def weigh(i, carry):
        s, zz = lax.div(i, nz), lax.rem(i, nz)
        for line in range(LINES):
            gate = jax.nn.sigmoid(jnp.sum(xall[s, zz, line].astype(F32) * router, axis=-1, keepdims=True))
            alive = lax.broadcasted_iota(jnp.int32, (rows, 1), 0) < counts[s, zz * LINES + line]
            gall[s, zz, line] = (gall[s, zz, line].astype(F32) * jnp.where(alive, gate, 0.0)).astype(BF16)
        return carry

    lax.fori_loop(0, 2 * nz, weigh, 0)

    own_gq = jnp.concatenate([gq[p].reshape(both, 128) for p in range(pairs)], axis=1)
    part[...] = mm(own_gq, wqkv[0], NT)

    def grad_u(s, zz):
        at = pl.ds(pl.multiple_of(zz * (LINES * rows), LINES * rows), LINES * rows)
        gk = jnp.concatenate([gkv[p, s, at, :128] for p in range(pairs)], axis=1)
        gv = jnp.concatenate([gkv[p, s, at, 128:] for p in range(pairs)], axis=1)
        return mm(gk, wqkv[1], NT) + mm(gv, wqkv[2], NT)

    def part_of(s):
        return part[pl.ds(pl.multiple_of(s * rows, rows), rows), :]

    def theirs(j, carry):
        zz = place.around(j + 1)
        xall[other, zz] = grad_u(other, zz).astype(BF16).reshape(LINES, rows, width)
        pump_in(j, "v", range(nz))
        return carry

    lax.fori_loop(0, nz, theirs, 0)
    xall[other, z, l] = (xall[other, z, l].astype(F32) + part_of(other)).astype(BF16)
    lent = [
        links.copy(
            lambda j=j: (xall.at[other, place.around(j + 1)], gsib.at[place.around(j + 1)], place.sibling)
        )
        for j in range(nz)
    ]

    def ours(j, gain_total):
        zz = place.around(j + 1)
        value = grad_u(c, zz).reshape(LINES, rows, width)
        for i in range(nz):
            pl.when(j == i)(lent[i].wait_recv)
        value = value + gsib[zz].astype(F32)
        rows_x = xall[c, zz].astype(F32)
        hat = rows_x * row_scale(rows_x)
        xall[c, zz] = value.astype(BF16)
        pump_in(j, "u", range(nz))
        return gain_total + jnp.sum(value * hat, axis=(0, 1)).reshape(1, width)

    x_own = xall[c, z, l].astype(F32)
    gain_total = jnp.sum(part_of(c) * (x_own * row_scale(x_own)), axis=0, keepdims=True)
    attn_s[pl.ds(0, rows), :] = x_own
    gain_total = lax.fori_loop(0, nz, ours, gain_total)
    xall[c, z, l] = (xall[c, z, l].astype(F32) + part_of(c)).astype(BF16)
    sm[0:1] = gain_total
    reduce_u.start()
    for k in range(1, nz):
        small[k].start()
    pump("u", nz)
    for flow in gw:
        for j in range(LINES):
            flow.lent_line(j)

    def put(b, i, which, stage, out):
        at = pl.ds(pl.multiple_of(b * hb + i * part_ff, part_ff), part_ff)
        return pltpu.make_async_copy(stage.at[i], out.at[at, :], osem.at[which, i])

    def ff_block(b, carry):
        cut = pl.ds(pl.multiple_of(b * hb, hb), hb)

        def ff_tile(t, carry):
            s, h = lax.div(t, 2), lax.rem(t, 2)
            at = pl.ds(pl.multiple_of(h * tile, tile), tile)
            zz = pl.ds(h * (nz // 2), nz // 2)
            act, slope = gelu_parts(mm(wall[s, zz].reshape(tile, width), wup[:, cut]))
            uall[s, zz, :, :, :hb] = act.astype(BF16).reshape(nz // 2, LINES, rows, hb)
            grad_act = mm(gall[s, zz].reshape(tile, width), wdown[cut, :], NT)
            grad_pre = (slope * grad_act).astype(BF16)
            for i in range(slots):
                gkv[i, s, at] = grad_pre[:, part_ff * i : part_ff * (i + 1)]
            pump_in(b * per_block + t, "h", [j for j in range(per_block * blocks) if j % per_block < tiles])
            return carry

        lax.fori_loop(0, tiles, ff_tile, 0)

        def flush(which, stage, out, lhs, rhs):
            value = mm(lhs, rhs[...].reshape(2 * total_rows, width), TN).astype(BF16)
            for i in range(slots):
                pl.when(b >= 1)(lambda i=i: put(b - 1, i, which, stage, out).wait())
                stage[i] = value[i * part_ff : (i + 1) * part_ff]
                put(b, i, which, stage, out).start()

        flush(0, stage_d, gdown_o, uall[:, :, :, :, :hb].reshape(2 * total_rows, hb), gall)
        pump_in(b * per_block + tiles, "h", range(tiles, per_block * blocks, per_block))
        slopes = [gkv[i].reshape(2 * total_rows, part_ff) for i in range(slots)]
        flush(1, stage_u, gup_o, jnp.concatenate(slopes, axis=1), wall)
        pump_in(b * per_block + tiles + 1, "h", range(tiles + 1, per_block * blocks, per_block))
        return carry

    lax.fori_loop(0, blocks, ff_block, 0)
    pump("z", 0)
    assert not left
    out_copy = pltpu.make_async_copy(res, res_o, osem.at[2, 0])
    out_copy.start()
    for i in range(slots):
        put(blocks - 1, i, 0, stage_d, gdown_o).wait()
        put(blocks - 1, i, 1, stage_u, gup_o).wait()
    links.drain()
    out_copy.wait()


def finish_kernel(
    tokens, cot, pick, rows, grow, small, res_h, gup_h, gdown_h,
    mixed_o, gtok_o, gain_a_o, gain_m_o, router_o, gqkv_o, gout_o, gup_o, gdown_o,
    res, gup, gdown, qkv_s, out_s, up_s, down_s, sem_in, sem_out,
):
    up_cuts = [slice(i * 384, (i + 1) * 384) for i in range(gup.shape[0] // 384)]
    down_cuts = [slice(i * 384, (i + 1) * 384) for i in range(gdown.shape[0] // 384)]
    loads, stores = [], []

    def load(src, dst):
        loads.append(pltpu.make_async_copy(src, dst, sem_in.at[len(loads)]))
        loads[-1].start()
        return loads[-1]

    def store(src, dst):
        stores.append(pltpu.make_async_copy(src, dst, sem_out.at[len(stores)]))
        stores[-1].start()

    downs = [load(gdown_h.at[cut], gdown.at[cut]) for cut in down_cuts]
    groups = [load(res_h.at[g], res.at[g]) for g in range(2)]
    ups = [load(gup_h.at[cut], gup.at[cut]) for cut in up_cuts]
    for cut, got in zip(down_cuts, downs):
        got.wait()
        down_s[cut] = gdown[cut].astype(F32)
        store(down_s.at[cut], gdown_o.at[cut])
    width = rows.shape[1]
    half = width // 2
    for got in groups:
        got.wait()
    for i in range(3):
        for unit in range(1, 4):
            cut = slice((unit - 1) * 128, unit * 128)
            qkv_s[i, :, cut] = res[unit // 2, :, :, unit % 2, i].reshape(width, 128).astype(F32)
        store(qkv_s.at[i], gqkv_o.at[i])
        value = res[0, :, :, 0, i].reshape(width, 128).astype(F32)
        out_s[:, 256 * i : 256 * i + 128] = value[:half]
        out_s[:, 256 * i + 128 : 256 * i + 256] = value[half:]
    store(out_s, gout_o)
    for cut, got in zip(up_cuts, ups):
        got.wait()
        up_s[:, cut] = gup[cut].astype(F32).T
        store(up_s.at[:, cut], gup_o.at[:, cut])
    chosen = mm(pick[...], jnp.ones(rows.shape, BF16), TN) > 0.5
    mixed_o[...] = jnp.where(chosen, mm(pick[...], rows[...], TN), tokens[...].astype(F32)).astype(BF16)
    grad = grow[...]
    hi = grad.astype(BF16)
    rest = grad - hi.astype(F32)
    mid = rest.astype(BF16)
    lo = (rest - mid.astype(F32)).astype(BF16)
    spread = mm(pick[...], hi, TN) + (mm(pick[...], mid, TN) + mm(pick[...], lo, TN))
    gtok_o[...] = (cot[...].astype(F32) + spread).astype(BF16)
    gain_a_o[...] = small[0:1].reshape(half)
    gain_m_o[...] = small[1:2].reshape(half)
    router_o[...] = small[2:3].reshape(half)
    for made in stores:
        made.wait()


def fused_body(
    tokens, cotangent, w_qkv, w_out, w_up, w_down, gain_attn, gain_mlp, router, picked, counts
):
    nseq = lax.axis_size("seq")
    nz = nseq // LINES
    rows = picked.shape[1] // nseq
    block, width = tokens.shape[1:]
    half, ff = w_out.shape[0], w_up.shape[1]
    pairs = half // 128
    total_rows = nseq * rows
    piece = width // nseq
    vm = pltpu.VMEM
    dma = pltpu.SemaphoreType.DMA
    wide = (2, nz, LINES, rows, width)
    heads = (2 * pairs, nz, LINES, rows, 128)
    both = (2 * rows, width)
    part = (2, 3, piece, 128)
    scratch = [
        vm((block, width), BF16), vm((block, width), BF16),
        vm((3, width, half), BF16), vm((half, width), BF16), vm((width, ff), BF16), vm((ff, width), BF16), dma((6,)),
        vm((2, 8, half), F32), vm(wide, BF16), vm(wide, BF16), vm(heads, BF16), vm(heads, BF16),
        vm((2 * pairs, 2 * rows, 128), BF16), vm((2, rows, total_rows), F32),
        vm((2 * pairs, 2 * rows, total_rows), F32), vm((2, rows, half), BF16),
        vm((8, 128), F32), vm(both, F32), vm(both, F32), vm((2 * rows, 1), F32),
        vm(both, F32), vm(both, F32), vm(both, F32),
        vm(wide, BF16), vm(wide, BF16), vm((2 * rows, ff), F32), vm((2 * rows, ff), BF16), vm((2 * rows, ff), BF16),
        vm((2 * pairs, 2 * rows, 128), BF16), vm((pairs, 2, rows, 128), BF16), vm((pairs, 2, total_rows, 256), BF16),
        vm((nz, LINES, rows, width), BF16), vm((nz, 2, rows, width), BF16), vm((nz, rows, width), BF16),
        vm((nz - 1, rows, width), BF16),
        vm((2, nz, LINES, *part), BF16), vm((2, nz, 2, *part), BF16), vm((2, nz, *part), BF16),
        vm((2, nz - 1, *part), BF16), vm((2, nz, LINES, *part), BF16),
        vm((8, width), F32), vm((nz - 1, 8, width), F32), vm((2, 8, width), F32), vm((2, 8, width), F32),
        vm((2, 8, width), F32),
        vm((2, 256, width), BF16), vm((2, 256, width), BF16), dma((3, 2)),
        dma((MESSAGES,)), dma((MESSAGES,)),
    ]
    in_vmem = pl.BlockSpec(memory_space=pltpu.VMEM)
    in_hbm = pl.BlockSpec(memory_space=pl.ANY)
    in_smem = pl.BlockSpec(memory_space=pltpu.SMEM)
    shaped = jax.ShapeDtypeStruct
    pick, out_rows, grad_rows, res, grad_up, grad_down, small = pl.pallas_call(
        functools.partial(layer_kernel, nz),
        out_shape=(
            shaped((rows, block), BF16),
            shaped((rows, width), BF16),
            shaped((rows, width), F32),
            shaped((2, nz, LINES, *part), BF16),
            shaped((ff, width), BF16),
            shaped((ff, width), BF16),
            shaped((8, half), F32),
        ),
        in_specs=[in_hbm] * 2 + [in_vmem, in_smem] + [in_vmem] * 3 + [in_hbm] * 4,
        out_specs=(in_vmem, in_vmem, in_vmem, in_hbm, in_hbm, in_hbm, in_vmem),
        scratch_shapes=scratch,
        compiler_params=pltpu.CompilerParams(
            collective_id=0, has_side_effects=True, vmem_limit_bytes=VMEM_BYTES
        ),
        name="layer",
    )(
        tokens[0], cotangent[0], picked, counts,
        gain_attn, gain_mlp, router, w_qkv, w_out, w_up, w_down,
    )
    mixed, grad_tokens, gain_a, gain_m, grad_r, grad_qkv, grad_out, grad_up, grad_down = pl.pallas_call(
        finish_kernel,
        out_shape=(
            shaped((block, width), BF16),
            shaped((block, width), BF16),
            shaped((half,), F32),
            shaped((half,), F32),
            shaped((half,), F32),
            shaped((3, width, half), F32),
            shaped((half, width), F32),
            shaped((width, ff), F32),
            shaped((ff, width), F32),
        ),
        in_specs=[in_vmem] * 6 + [in_hbm] * 3,
        out_specs=(in_vmem,) * 5 + (in_hbm,) * 4,
        scratch_shapes=[
            vm((2, nz, LINES, *part), BF16), vm((ff, width), BF16), vm((ff, width), BF16),
            vm((3, width, half), F32), vm((half, width), F32), vm((width, ff), F32), vm((ff, width), F32),
            dma((16,)), dma((16,)),
        ],
        compiler_params=pltpu.CompilerParams(vmem_limit_bytes=VMEM_BYTES),
        name="finish",
    )(tokens[0], cotangent[0], pick, out_rows, grad_rows, small, res, grad_up, grad_down)
    return (
        mixed[None], grad_tokens[None], grad_qkv, grad_out, grad_up, grad_down, gain_a, gain_m, grad_r,
    )


def body(tokens, *rest):
    nseq, cores = lax.axis_size("seq"), lax.axis_size("wa")
    fits = nseq == 4 * LINES and cores == 2 and rest[-2].shape[1] == nseq * CAP
    return (fused_body if fits else spread_body)(tokens, *rest)


CAP = 80


def norm_rows(value, gain):
    scale = lax.rsqrt(jnp.mean(value * value, axis=-1, keepdims=True) + EPS)
    return (value * scale * gain, scale)


def norm_back(value, scale, gain, grad_out):
    normed = value * scale
    weighted = grad_out * gain
    grad_value = scale * (weighted - normed * jnp.mean(weighted * normed, axis=-1, keepdims=True))
    return (grad_value, normed)


def gelu_back(pre, grad):
    unused, pull = jax.vjp(lambda value: jax.nn.gelu(value, approximate=True), pre)
    return pull(grad)[0]


def spread_body(
    tokens, cotangent, w_qkv, w_out, w_up, w_down, gain_attn, gain_mlp, router, picked, counts
):
    f32 = jnp.float32
    bf16 = jnp.bfloat16
    nseq = lax.axis_size("seq")
    me = lax.axis_index("seq")
    side = lax.axis_index("wa")
    slots = jnp.arange(CAP, dtype=jnp.int32)
    own_rows = lax.dynamic_slice(picked, (side, me * CAP), (1, CAP))[0]
    x_own = jnp.take(tokens[0], own_rows, axis=0)
    dy_own = jnp.take(cotangent[0], own_rows, axis=0).astype(f32)
    x_rows, g_attn, g_mlp, w_router = (
        lax.all_gather(x_own[None], "wa", axis=0, tiled=True),
        lax.all_gather(gain_attn, "wa", axis=0, tiled=True),
        lax.all_gather(gain_mlp, "wa", axis=0, tiled=True),
        lax.all_gather(router, "wa", axis=0, tiled=True),
    )
    qkv_w, out_w, up_w, down_w = (w_qkv, w_out, w_up, w_down)
    streams = jnp.arange(lax.axis_size("wa"))
    stream_picked = jnp.take(picked, streams, axis=0)
    stream_counts = jnp.take(counts, streams, axis=0)
    key_index = jnp.arange(nseq * CAP, dtype=jnp.int32)
    key_device = key_index // CAP
    key_pos = stream_picked * nseq + key_device[None, :]
    key_live = (key_index % CAP)[None, :] < jnp.take(stream_counts, key_device, axis=1)
    query_index = me * CAP + slots
    query_pos = lax.dynamic_slice_in_dim(key_pos, me * CAP, CAP, 1)
    own_live = (slots < counts[side, me]).astype(f32)
    gains_a = g_attn.astype(f32)
    gains_m = g_mlp.astype(f32)
    x_keep = x_own.astype(f32)
    weight = jax.nn.sigmoid(jnp.dot(x_own, w_router, preferred_element_type=f32))
    x_wide = x_rows.astype(f32)
    normed_a, scale_a = norm_rows(x_wide, gains_a)
    u_rows = normed_a.astype(bf16)
    qkv = jnp.einsum("srd,cde->csre", u_rows, qkv_w, preferred_element_type=f32).astype(bf16)
    query = qkv[0]
    local_kv = qkv[1:]
    batch = query.shape[0]
    heads = query.shape[-1] // HD
    factor = HD ** (-0.5)
    split_q = query.reshape(batch, CAP, heads, HD)
    kv_all = lax.all_gather(local_kv, "seq", axis=2, tiled=True)
    block = 8 * CAP
    nblock = kv_all.shape[2] // block

    def block_of(start):
        keys_b = lax.dynamic_slice_in_dim(kv_all[0], start, block, 1).reshape(
            batch, block, heads, HD
        )
        vals_b = lax.dynamic_slice_in_dim(kv_all[1], start, block, 1).reshape(
            batch, block, heads, HD
        )
        k_pos = lax.dynamic_slice_in_dim(key_pos, start, block, 1)
        k_live = lax.dynamic_slice_in_dim(key_live, start, block, 1)
        k_index = start + jnp.arange(block, dtype=jnp.int32)
        allowed = (k_pos[:, None, :] <= query_pos[:, :, None]) & (
            k_live[:, None, :] | (k_index[None, None, :] == query_index[None, :, None])
        )
        raw = jnp.einsum("sqhd,skhd->shqk", split_q, keys_b, preferred_element_type=f32) * factor
        return (keys_b, vals_b, allowed, jnp.where(allowed[:, None], raw, NEG))

    def max_sum(number, carry):
        top, total = carry
        unused_k, unused_v, allowed, scores = block_of(number * block)
        new_top = jnp.maximum(top, jnp.max(scores, axis=-1, keepdims=True))
        expd = jnp.where(allowed[:, None], jnp.exp(scores - new_top), 0.0)
        return (new_top, total * jnp.exp(top - new_top) + jnp.sum(expd, axis=-1, keepdims=True))

    top_start = jnp.full((batch, heads, CAP, 1), NEG, f32)
    top, total = lax.fori_loop(
        0, nblock, max_sum, (top_start, jnp.zeros((batch, heads, CAP, 1), f32))
    )
    lse = top + jnp.log(total)

    def weigh(number, acc):
        unused_k, vals_b, allowed, scores = block_of(number * block)
        probs_low = jnp.exp(scores - lse).astype(bf16)
        return acc + jnp.einsum("shqk,skhd->sqhd", probs_low, vals_b, preferred_element_type=f32)

    acc = lax.fori_loop(0, nblock, weigh, jnp.zeros((batch, CAP, heads, HD), f32))
    attended = acc.reshape(query.shape).astype(bf16)
    attn_part = jnp.einsum("sqe,ed->sqd", attended, out_w, preferred_element_type=f32)
    attn_own = lax.psum_scatter(attn_part, "wa", scatter_dimension=0, tiled=True)[0]
    resid = x_keep + attn_own
    normed_m, scale_m = norm_rows(resid, gains_m)
    w_own = normed_m.astype(bf16)
    w_rows = lax.all_gather(w_own[None], "wa", axis=0, tiled=True)
    pre = jnp.einsum("srd,df->srf", w_rows, up_w, preferred_element_type=f32)
    act = jax.nn.gelu(pre, approximate=True).astype(bf16)
    mlp_part = jnp.einsum("srf,fd->srd", act, down_w, preferred_element_type=f32)
    mlp_own = lax.psum_scatter(
        mlp_part.astype(jnp.bfloat16), "wa", scatter_dimension=0, tiled=True
    ).astype(jnp.float32)[0]
    branch = attn_own + mlp_own
    lift = (weight * own_live)[:, None]
    out_rows = (x_keep + lift * branch).astype(bf16)
    mixed_out = tokens.at[0, own_rows].set(out_rows)
    grad_branch = dy_own * lift
    grad_logit = jnp.sum(dy_own * branch, axis=-1) * own_live * weight * (1.0 - weight)
    grad_router = jnp.dot(grad_logit, x_keep, precision=lax.Precision.HIGHEST)
    grad_m = grad_branch.astype(bf16)
    grad_m_rows = lax.all_gather(grad_m[None], "wa", axis=0, tiled=True)
    grad_down = jnp.einsum("srf,srd->fd", act, grad_m_rows, preferred_element_type=f32)
    grad_act = jnp.einsum("srd,fd->srf", grad_m_rows, down_w, preferred_element_type=f32)
    grad_pre = gelu_back(pre, grad_act).astype(bf16)
    grad_up = jnp.einsum("srd,srf->df", w_rows, grad_pre, preferred_element_type=f32)
    grad_w_part = jnp.einsum("srf,df->srd", grad_pre, up_w, preferred_element_type=f32)
    grad_w_own = lax.psum_scatter(grad_w_part, "wa", scatter_dimension=0, tiled=True)[0]
    grad_resid, hat_m = norm_back(resid, scale_m, gains_m, grad_w_own)
    grad_gain_m = jnp.sum(grad_w_own * hat_m, axis=0)
    grad_a = (grad_branch + grad_resid).astype(bf16)
    grad_a_rows = lax.all_gather(grad_a[None], "wa", axis=0, tiled=True)
    grad_out = jnp.einsum("sqe,sqd->ed", attended, grad_a_rows, preferred_element_type=f32)
    grad_attended = jnp.einsum(
        "sqd,ed->sqe", grad_a_rows, out_w, preferred_element_type=f32
    ).astype(bf16)
    split_do = grad_attended.reshape(batch, CAP, heads, HD)

    def delta_step(number, delta):
        unused_k, vals_b, allowed, scores = block_of(number * block)
        probs = jnp.exp(scores - lse)
        grad_probs = jnp.einsum("sqhd,skhd->shqk", split_do, vals_b, preferred_element_type=f32)
        return delta + jnp.sum(grad_probs * probs, axis=-1, keepdims=True)

    delta = lax.fori_loop(0, nblock, delta_step, jnp.zeros((batch, heads, CAP, 1), f32))

    def grad_step(number, carry):
        grad_query, holder = carry
        start = number * block
        keys_b, vals_b, allowed, scores = block_of(start)
        probs = jnp.exp(scores - lse)
        grad_probs = jnp.einsum("sqhd,skhd->shqk", split_do, vals_b, preferred_element_type=f32)
        grad_scores = (probs * (grad_probs - delta)).astype(bf16)
        grad_query = (
            grad_query
            + jnp.einsum("shqk,skhd->sqhd", grad_scores, keys_b, preferred_element_type=f32)
            * factor
        )
        grad_keys = (
            jnp.einsum("shqk,sqhd->skhd", grad_scores, split_q, preferred_element_type=f32) * factor
        )
        grad_values = jnp.einsum(
            "shqk,sqhd->skhd", probs.astype(bf16), split_do, preferred_element_type=f32
        )
        paired = jnp.stack([grad_keys, grad_values]).reshape(2, batch, block, heads * HD)
        holder = lax.dynamic_update_slice_in_dim(holder, paired, start, 2)
        return (grad_query, holder)

    grad_query, holder = lax.fori_loop(
        0,
        nblock,
        grad_step,
        (jnp.zeros((batch, CAP, heads, HD), f32), jnp.zeros(kv_all.shape, f32)),
    )
    kv_total = lax.psum_scatter(holder.astype(bf16), "seq", scatter_dimension=2, tiled=True)
    grad_qkv_rows = jnp.concatenate(
        [grad_query.reshape(query.shape)[None].astype(bf16), kv_total.astype(bf16)], axis=0
    )
    grad_qkv = jnp.einsum("srd,csre->cde", u_rows, grad_qkv_rows, preferred_element_type=f32)
    grad_u_part = jnp.einsum("csre,cde->srd", grad_qkv_rows, qkv_w, preferred_element_type=f32)
    part_gain_a = jnp.sum(grad_u_part * (x_wide * scale_a), axis=(0, 1))
    grad_u_all, grad_gain_a, grad_gain_m, grad_router = (
        lax.psum_scatter(
            grad_u_part.astype(jnp.bfloat16), "wa", scatter_dimension=0, tiled=True
        ).astype(jnp.float32),
        lax.psum_scatter(
            part_gain_a.astype(jnp.bfloat16), "wa", scatter_dimension=0, tiled=True
        ).astype(jnp.float32),
        lax.psum_scatter(
            grad_gain_m.astype(jnp.bfloat16), "wa", scatter_dimension=0, tiled=True
        ).astype(jnp.float32),
        lax.psum_scatter(
            grad_router.astype(jnp.bfloat16), "wa", scatter_dimension=0, tiled=True
        ).astype(jnp.float32),
    )
    grad_u_own = grad_u_all[0]
    grad_x_norm, unused = norm_back(x_keep, scale_a[side], gains_a, grad_u_own)
    grad_rows = grad_x_norm + grad_resid + grad_logit[:, None] * w_router.astype(f32)[None, :]
    grad_tokens = cotangent.astype(f32).at[0, own_rows].add(grad_rows).astype(bf16)
    shares = (grad_qkv, grad_out, grad_up, grad_down, grad_gain_a, grad_gain_m, grad_router)
    large = lax.psum(tuple(share.astype(bf16) for share in shares[:4]), "seq")
    small = lax.psum(shares[4:], "seq")
    summed = tuple(part.astype(f32) for part in large) + small
    return (
        mixed_out,
        grad_tokens,
        summed[0],
        summed[1],
        summed[2],
        summed[3],
        summed[4],
        summed[5],
        summed[6],
    )


def solution(mesh):
    return jax.shard_map(
        body,
        mesh=mesh,
        in_specs=(
            P("wa", "seq", None),
            P("wa", "seq", None),
            P(None, None, "wa"),
            P("wa", None),
            P(None, "wa"),
            P("wa", None),
            P("wa"),
            P("wa"),
            P("wa"),
            P(),
            P(),
        ),
        out_specs=(
            P("wa", "seq", None),
            P("wa", "seq", None),
            P(None, None, "wa"),
            P("wa", None),
            P(None, "wa"),
            P("wa", None),
            P("wa"),
            P("wa"),
            P("wa"),
        ),
        check_vma=False,
    )
```

```python
import functools

import jax
import jax.numpy as jnp
from jax import lax
from jax.experimental import pallas as pl
from jax.experimental.pallas import tpu as pltpu
from jax.sharding import PartitionSpec as P

HD = 64
EPS = 1e-05
NEG = -1e30
FAR = 1e9
LINES = 4
MESSAGES = 420
VMEM_BYTES = 64 << 20
EARLY_ROWS = 48
COTANGENT_AT = 1
POINTS = {"x": 0, "a": 8, "p": 14, "b": 20, "v": 27, "u": 31, "h": 36, "z": 54}
SCHEDULE = (
    (3, 0, 21, 1, 15, 22, 16, 2, 18, 7, 17),
    (),
    (19, 4, 5, 6, 20, 8),
    (10, 24, 9, 23, 25),
    (11, 30, 33, 27),
    (52, 51, 37, 26, 45),
    (28, 14, 31, 29, 12, 13),
    (46,),
    (38, 41, 34),
    (32, 53),
    (56, 49, 48, 35),
    (54,),
    (47,),
    (42,),
    (50, 39, 36),
    (40, 55),
    (57, 43),
    (44,),
    (58,),
    (67, 61, 59, 60),
    (63, 75, 81),
    (65, 82),
    (62, 76, 64, 78, 71),
    (83, 69, 77, 154, 86, 68, 155),
    (),
    (151,),
    (79, 156, 152),
    (72, 84),
    (150, 153, 80, 73, 66),
    (),
    (),
    (85, 163, 157, 162, 166, 87),
    (70, 168),
    (),
    (),
    (74, 164, 159, 89, 165, 158, 88),
    (188, 169, 160, 161, 167),
    (170,),
    (171, 178),
    (174, 179),
    (186, 176, 175),
    (177, 172),
    (181, 189, 173, 90, 105, 180),
    (111, 187, 91),
    (93, 106, 97),
    (182, 94, 98),
    (113, 108, 120, 109, 123, 190, 112, 107),
    (135, 121, 92, 127, 141, 114, 116, 185),
    (136, 99, 184, 191, 128, 131, 183),
    (95, 115, 142, 102),
    (100, 117, 96, 124, 125, 146, 122, 144, 129),
    (118, 110, 143),
    (101, 138, 137, 139, 104, 103, 126, 133),
    (130, 119),
    (140, 132, 192, 147, 134, 145, 149, 148),
)
MESH = pl.DeviceIdType.MESH
F32 = jnp.float32
BF16 = jnp.bfloat16
NN = (((1,), (0,)), ((), ()))
NT = (((1,), (1,)), ((), ()))
TN = (((0,), (0,)), ((), ()))
GELU_A = 0.7978845608028654
GELU_B = 0.044715


def mm(a, b, dims=NN):
    return lax.dot_general(a, b, dims, preferred_element_type=F32)


def gelu_parts(pre):
    square = pre * pre
    t = jnp.tanh(GELU_A * pre * (1.0 + GELU_B * square))
    half = 0.5 * (1.0 + t)
    slope = half + 0.5 * pre * (1.0 - t * t) * (GELU_A * (1.0 + 3.0 * GELU_B * square))
    return pre * half, slope


def row_scale(value):
    return lax.rsqrt(jnp.mean(value * value, axis=-1, keepdims=True) + EPS)


class Message:
    def __init__(self, links, i, ends):
        self.links, self.i, self.ends = links, i, ends

    def make(self):
        src, dst, device = self.ends()
        return pltpu.make_async_remote_copy(
            src_ref=src,
            dst_ref=dst,
            send_sem=self.links.send.at[self.i],
            recv_sem=self.links.recv.at[self.i],
            device_id=device,
            device_id_type=MESH,
        )

    def start(self):
        self.make().start()
        self.links.pending.append(self)
        return self

    def wait_recv(self):
        self.make().wait_recv()

    def wait_send(self):
        self.links.forget(self)
        self.make().wait_send()

    def wait(self):
        self.wait_send()
        self.wait_recv()


class Links:
    def __init__(self, send, recv):
        self.send, self.recv, self.used, self.pending = send, recv, 0, []

    def many(self, count):
        self.used += count
        return self.used - count

    def numbered(self, i, ends):
        return Message(self, i, ends)

    def forget(self, what):
        self.pending = [other for other in self.pending if other is not what]

    def message(self, ends):
        return self.numbered(self.many(1), ends)

    def copy(self, ends):
        return self.message(ends).start()

    def drain(self):
        for message in list(self.pending):
            message.wait_send()


class Place:
    def __init__(self, nz):
        self.me, self.c = lax.axis_index("seq"), lax.axis_index("wa")
        self.nz = nz
        self.z, self.l = lax.div(self.me, LINES), lax.rem(self.me, LINES)
        y, x = lax.div(self.l, 2), lax.rem(self.l, 2)
        over_y, over_x = self.l + 2 - 4 * y, self.l + 1 - 2 * x
        self.l2 = over_y * (1 - self.c) + over_x * self.c
        self.l3 = over_x * (1 - self.c) + over_y * self.c
        self.l23 = 3 - self.l
        self.sibling = (self.me, 1 - self.c)
        near = [sorted(range(nz), key=lambda other: abs(other - here)) for here in range(nz)]
        self.sources = []
        for i in range(nz):
            source = near[0][i] + 0 * self.z
            for here in range(1, nz):
                source = jnp.where(self.z == here, near[here][i], source)
            self.sources.append(source)

    def turn(self, i):
        return self.sources[i]

    def around(self, k):
        return lax.rem(self.z + k, self.nz)

    def at(self, z, line):
        return (z * LINES + line, self.c)


class Chain:
    def __init__(self, place, links, shard):
        self.p, self.links, self.shard = place, links, shard
        self.i = links.many(2 * place.nz)

    def hop(self, source, to, down, hops):
        i = self.i + down * self.p.nz + hops
        return self.links.numbered(
            i, lambda: (self.shard(source), self.shard(source), self.p.at(to, self.p.l))
        )

    def start(self):
        p = self.p
        pl.when(p.z + 1 < p.nz)(lambda: self.hop(p.z, p.z + 1, 0, 1).make().start())
        pl.when(p.z > 0)(lambda: self.hop(p.z, p.z - 1, 1, 1).make().start())
        self.links.pending.append(self)

    def arrive(self, i):
        p = self.p
        source = p.turn(i)
        down = jnp.where(source > p.z, 1, 0)
        hops = jnp.where(source > p.z, source - p.z, p.z - source)
        self.hop(source, p.z, down, hops).wait_recv()
        on = p.z + 1 - 2 * down
        pl.when((on >= 0) & (on < p.nz))(lambda: self.hop(source, on, down, hops + 1).make().start())

    def wait_send(self):
        p = self.p
        self.links.forget(self)
        for hops in range(1, p.nz):
            up = (p.z + 1 < p.nz) & (p.z >= hops - 1)
            down = (p.z > 0) & (p.z + hops - 1 < p.nz)
            pl.when(up)(lambda: self.hop(p.z, p.z, 0, hops).make().wait_send())
            pl.when(down)(lambda: self.hop(p.z, p.z, 1, hops).make().wait_send())


class Gather:
    def __init__(self, place, links, buf, lend, own=False, early=True, cut=None):
        self.p = p = place
        self.early = early
        lines = (p.l, p.l2, p.l3, p.l23)

        def at(source, line):
            ref = buf().at[source, line]
            return ref if cut is None else ref.at[cut]

        def message(j, i, device):
            def ends():
                shard = at(p.turn(i), lines[j])
                return shard, shard, device()

            return links.message(ends)

        over = range(p.nz)
        self.second = {i: message(0, i, lambda: p.at(p.z, p.l2)) for i in (over if early else (0,))}
        self.third = {(j, i): message(j, i, lambda: p.at(p.z, p.l3)) for j in range(2) for i in over}
        self.chains = [Chain(place, links, lambda s, j=j: at(s, lines[j])) for j in range(1 if early else 2)]
        keys = [(j, i) for j in range(4) for i in over if j or i or own] if lend else []
        self.lent = {key: message(*key, lambda: p.sibling) for key in keys}
        self.waited = set()
        self.all = [*self.second.values(), *self.third.values(), *self.lent.values(), *self.chains]

    def wait_sent(self):
        for message in self.all:
            message.wait_send()

    def hand_over(self, *key):
        if key in self.lent:
            self.lent[key].start()

    def start(self):
        self.chains[0].start()
        self.second[0].start()
        self.third[0, 0].start()
        self.hand_over(0, 0)

    def over_z(self, j, i):
        self.chains[j].arrive(i)
        self.third[j, i].start()
        if self.early:
            self.second[i].start()
        self.hand_over(j, i)

    def over_second(self, i):
        self.second[i].wait_recv()
        if not self.early:
            self.chains[1].start()
        self.third[1, i].start()
        self.hand_over(1, i)

    def over_third(self, j, i):
        self.third[j, i].wait_recv()
        self.hand_over(2 + j, i)

    def lent_own(self):
        self.waited.add((0, 0))
        self.lent[0, 0].wait_recv()

    def lent_line(self, j):
        for i in range(self.p.nz):
            if (j, i) in self.lent and (j, i) not in self.waited:
                self.waited.add((j, i))
                self.lent[j, i].wait_recv()

    def steps(self):
        part, over = functools.partial, range(self.p.nz)
        out = [part(self.over_z, j, i) for j in range(len(self.chains)) for i in over[1:]]
        out += [part(self.over_second, i) for i in self.second]
        return out + [part(self.over_third, j, i) for j, i in self.third]


def two_ways(place, links, buf, lend, own=False, cuts=(None, None)):
    return [
        Gather(place, links, buf, lend, own, early=early, cut=cut) for early, cut in zip((True, False), cuts)
    ]


class Scatter:
    def __init__(self, place, links, acc, got1, got2, got3):
        self.p = p = place
        self.acc, self.got1, self.got2, self.got3 = acc, got1, got2, got3
        self.order = (2, 1, 3, 0) if p.nz == 4 else (*range(1, p.nz), 0)

        def one(o, j, line):
            return lambda: (acc().at[p.around(o), line], got1().at[p.around(o), j], p.at(p.z, p.l3))

        def two(o):
            return lambda: (acc().at[p.around(o), p.l2], got2().at[p.around(o)], p.at(p.z, p.l2))

        def three(o):
            return lambda: (acc().at[p.around(o), p.l], got3().at[o - 1], p.at(p.around(o), p.l))

        self.m1 = {
            (j, o): links.message(one(o, j, line)) for o in self.order for j, line in ((0, p.l23), (1, p.l3))
        }
        self.m2 = {o: links.message(two(o)) for o in self.order}
        self.m3 = {o: links.message(three(o)) for o in range(1, p.nz)}

    def add(self, z, line, got):
        acc = self.acc()
        acc[z, line] = (acc[z, line].astype(F32) + got.astype(F32)).astype(BF16)

    def start(self):
        for message in self.m1.values():
            message.start()

    def far(self, o):
        p, zz = self.p, self.p.around(o)
        self.m1[0, o].wait_recv()
        self.add(zz, p.l2, self.got1()[zz, 0])
        self.m2[o].start()

    def near(self, o):
        p, zz = self.p, self.p.around(o)
        self.m1[1, o].wait_recv()
        self.add(zz, p.l, self.got1()[zz, 1])

    def along(self, o):
        p, zz = self.p, self.p.around(o)
        self.m2[o].wait_recv()
        if o:
            self.add(zz, p.l, self.got2()[zz])
            self.m3[o].start()

    def total(self):
        p = self.p
        total = self.acc()[p.z, p.l].astype(F32) + self.got2()[p.z].astype(F32)
        for o in range(1, p.nz):
            self.m3[o].wait_recv()
            total = total + self.got3()[o - 1].astype(F32)
        return total

    def steps(self):
        return [functools.partial(step, o) for step in (self.far, self.near, self.along) for o in self.order]


def layer_kernel(
    nz,
    tokens_h, cot_h, picked, counts, gain_a_r, gain_m_r, router_r, wqkv_h, wout_h, wup_h, wdown_h,
    pick_o, rows_o, grow_o, res_o, gup_o, gdown_o, small_o,
    tokens, cot, wqkv, wout, wup, wdown, wsem,
    gvec, xall, uall, kall, vall, qst, bias, probs, att,
    dy_s, attn_s, resid_s, logit_s, part, got_a, got_m,
    wall, gall, pre_s, act_s, gpre_s, dost, gq, gkv,
    gsib, gu1, gu2, gu3, share, sh1, sh2, sh3, res,
    sm, smz, smy, smx, smw, stage_u, stage_d, osem,
    send, recv,
):
    place = Place(nz)
    links = Links(send, recv)
    c, l, z = place.c, place.l, place.z
    other = 1 - c
    rows, width = grow_o.shape
    both = 2 * rows
    block = tokens.shape[0]
    pairs = wout.shape[0] // 128
    nseq = nz * LINES
    total_rows = nseq * rows
    ff = wup.shape[1]

    barrier = pltpu.get_barrier_semaphore()
    peers = [place.at(z, place.l2), place.at(z, place.l3), place.sibling]
    for peer in peers:
        pl.semaphore_signal(barrier, inc=1, device_id=peer, device_id_type=MESH)

    def greet(on):
        pl.semaphore_signal(barrier, inc=1, device_id=place.at(on, l), device_id_type=MESH)

    pl.when(z + 1 < nz)(lambda: greet(z + 1))
    pl.when(z > 0)(lambda: greet(z - 1))
    half = wout.shape[0]
    pairs_of = [(tokens_h, tokens), (cot_h, cot)]
    pairs_of += [(wqkv_h.at[i], wqkv.at[:, i * half : (i + 1) * half]) for i in range(3)]
    pairs_of += [(wout_h, wout), (wup_h, wup), (wdown_h, wdown)]
    loads = [pltpu.make_async_copy(h, v, wsem.at[i]) for i, (h, v) in enumerate(pairs_of)]
    for load in loads[:2]:
        load.start()

    cuts = (pl.ds(0, EARLY_ROWS), pl.ds(EARLY_ROWS, rows - EARLY_ROWS))
    gx = two_ways(place, links, lambda: xall.at[c], True, True, cuts)
    gw = two_ways(place, links, lambda: wall.at[c], True, False, cuts)
    gg = two_ways(place, links, lambda: gall.at[c], True, True, cuts)
    scatters = [
        Scatter(
            place, links, lambda g=g: share.at[g], lambda g=g: sh1.at[g], lambda g=g: sh2.at[g], lambda g=g: sh3.at[g]
        )
        for g in range(2)
    ]
    gathers = [two_ways(place, links, lambda g=g: res.at[g], False, False, (0, 1)) for g in range(2)]
    reduce_u = Scatter(place, links, lambda: xall.at[c], lambda: gu1, lambda: gu2, lambda: gu3)
    small = {
        "y": links.message(lambda: (smy.at[0], smy.at[1], place.at(z, place.l2))),
        "x": links.message(lambda: (smx.at[0], smx.at[1], place.at(z, place.l3))),
        "w": links.message(lambda: (smw.at[0], smw.at[1], place.sibling)),
    }
    for k in range(1, nz):
        small[k] = links.message(lambda k=k: (sm, smz.at[k - 1], place.at(place.around(k), l)))

    def begin(flows):
        for flow in flows:
            flow.start()

    def small_z():
        for k in range(1, nz):
            small[k].wait_recv()
        total = jnp.zeros(sm.shape, F32)
        for source in range(nz):
            for k in range(nz):
                piece = sm[...] if k == 0 else smz[k - 1]
                total = total + jnp.where(place.around(nz - k) == source, piece, 0.0)
        smy[0] = total
        small["y"].start()

    def small_2():
        small["y"].wait_recv()
        smx[0] = smy[0] + smy[1]
        small["x"].start()

    def small_3():
        small["x"].wait_recv()
        smw[0] = smx[0] + smx[1]
        small["w"].start()

    def small_4():
        small["w"].wait_recv()
        total = smw[0] + smw[1]
        small_o[...] = jnp.where(c == 0, total[:, :half], total[:, half:])

    def weights_out(g):
        res[g, z, l] = scatters[g].total().astype(BF16)
        begin(gathers[g])

    def tokens_out():
        grad = reduce_u.total()
        own = attn_s[pl.ds(0, rows), :]
        scale = row_scale(own)
        hat = own * scale
        lifted = grad * gain_a
        grad_x = scale * (lifted - hat * jnp.mean(lifted * hat, axis=-1, keepdims=True))
        at = pl.ds(pl.multiple_of(c * rows, rows), rows)
        grow_o[...] = grad_x + resid_s[at, :] + logit_s[at, :] * router

    slots, part_ff = stage_u.shape[:2]
    hb = slots * part_ff
    blocks = ff // hb
    tile = total_rows // 2
    tiles = 2 * total_rows // tile
    per_block = tiles + 2
    steps = [step for flows in (gx, gg, gw, *gathers) for flow in flows for step in flow.steps()]
    steps += [step for scatter in (*scatters, reduce_u) for step in scatter.steps()]
    steps += [functools.partial(weights_out, g) for g in range(2)]
    steps += [small_z, small_2, small_3, small_4, tokens_out]
    left = set(range(len(steps)))

    def pump(kind, j):
        for i in SCHEDULE[POINTS[kind] + j]:
            left.remove(i)
            steps[i]()

    def pump_in(index, kind, among):
        for j in among:
            if SCHEDULE[POINTS[kind] + j]:
                pl.when(index == j)(functools.partial(pump, kind, j))

    itself = lax.broadcasted_iota(jnp.int32, (rows, total_rows), 1) == (
        lax.broadcasted_iota(jnp.int32, (rows, total_rows), 0) + place.me * rows
    )
    picked_f = picked[...].astype(F32)
    own_index = [
        jnp.sum(jnp.where(itself, picked_f[s : s + 1], 0.0), axis=-1, keepdims=True) for s in range(2)
    ]
    own_row = jnp.where(c == 0, own_index[0], own_index[1])
    pick = jnp.where(
        lax.broadcasted_iota(jnp.int32, (rows, block), 1).astype(F32) == own_row, 1.0, 0.0
    ).astype(BF16)
    pick_o[...] = pick
    loads[0].wait()
    xall[c, z, l] = mm(pick, tokens[...]).astype(BF16)
    gvec[c] = jnp.zeros(gvec.shape[1:], F32)
    for i, ref in enumerate((gain_a_r, gain_m_r, router_r)):
        gvec[c, i : i + 1] = ref[...].astype(F32).reshape(1, half)
    pl.semaphore_wait(barrier, len(peers) + jnp.where(z + 1 < nz, 1, 0) + jnp.where(z > 0, 1, 0))

    begin(gx)
    for load in loads[2:]:
        load.start()
    vec_copy = links.copy(lambda: (gvec.at[c], gvec.at[c], place.sibling))
    loads[1].wait()
    gall[c, z, l] = mm(pick, cot[...]).astype(BF16)

    lane = lax.broadcasted_iota(jnp.int32, (2, total_rows), 1)
    stream = lax.broadcasted_iota(jnp.int32, (2, total_rows), 0)

    def place_keys(d, carry):
        until = d * rows + jnp.where(stream == 0, counts[0, d], counts[1, d])
        mine = (lane >= d * rows) & (lane < until)
        return jnp.where(mine, picked_f * nseq + d.astype(F32), carry)

    kpos = lax.fori_loop(0, nseq, place_keys, jnp.full((2, total_rows), FAR, F32))
    for s in range(2):
        near = kpos[s : s + 1] <= own_index[s] * nseq + place.me.astype(F32)
        bias[s] = jnp.where(near | itself, 0.0, NEG)
    slot = lax.broadcasted_iota(jnp.int32, (both, 1), 0)
    first = slot < rows
    own_live = jnp.where(
        slot - jnp.where(first, 0, rows) < jnp.where(first, counts[0, place.me], counts[1, place.me]), 1.0, 0.0
    )
    on_core = jnp.where(first, (1 - c).astype(F32), c.astype(F32))
    vec_copy.wait_recv()
    vectors = jnp.concatenate([gvec[0], gvec[1]], axis=1)
    gain_a, gain_m, router = vectors[0:1], vectors[1:2], vectors[2:3]
    for load in loads[2:5]:
        load.wait()

    def project(s, line):
        def norm(zz, carry):
            value = xall[s, zz, line].astype(F32)
            uall[s, zz, line] = (value * row_scale(value) * gain_a).astype(BF16)
            return carry

        lax.fori_loop(0, nz, norm, 0)
        u = jnp.concatenate([uall[s, zz, line] for zz in range(nz)], axis=0)
        value = mm(u, wqkv[:, half:]).astype(BF16)
        for j, out in enumerate((kall, vall)):
            for p in range(pairs):
                at = j * half + p * 128
                for zz in range(nz):
                    out[s * pairs + p, zz, line] = value[zz * rows : (zz + 1) * rows, at : at + 128]

    def arrive(j):
        pump("x", j)
        if j % 2:
            for flow in gx:
                flow.lent_line(j // 2)
        if j == COTANGENT_AT:
            begin(gg)

    def take_line(j, carry):
        for i in range(8):
            pl.when(j == i)(functools.partial(arrive, i))
        mine = lax.rem(j, 2) == 0
        step = lax.div(j, 2)
        one, two = jnp.where(mine, place.l2, place.l3), jnp.where(mine, place.l3, place.l2)
        line = jnp.where(
            step == 0, l, jnp.where(step == 1, one, jnp.where(step == 2, two, place.l23))
        )
        project(jnp.where(mine, c, other), line)
        return carry

    lax.fori_loop(0, 8, take_line, 0)
    low = lax.broadcasted_iota(jnp.int32, (rows, 128), 1) < HD

    def stacked(value, s, p):
        piece = value[s * rows : (s + 1) * rows, p * 128 : (p + 1) * 128]
        zero = jnp.zeros_like(piece)
        return jnp.concatenate([jnp.where(low, piece, zero), jnp.where(low, zero, piece)], axis=0)

    own_u = uall[:, z, l].reshape(both, width)
    query = mm(own_u, wqkv[:, :half]).astype(BF16) * jnp.asarray(HD ** (-0.5), BF16)
    for s in range(2):
        for p in range(pairs):
            qst[s * pairs + p] = stacked(query, s, p)

    def attend(i, carry):
        s, p = lax.div(i, pairs), lax.rem(i, pairs)
        keys = kall[i].reshape(total_rows, 128)
        vals = vall[i].reshape(total_rows, 128)
        hide = bias[s]
        raw = mm(qst[i], keys, NT) + jnp.concatenate([hide, hide], axis=0)
        expd = jnp.exp(raw - jnp.max(raw, axis=-1, keepdims=True))
        prob = expd * (1.0 / jnp.sum(expd, axis=-1, keepdims=True))
        probs[i] = prob
        out = mm(prob.astype(BF16), vals)
        at = pl.multiple_of(p * 128, 128)
        att[s, :, pl.ds(at, 128)] = jnp.where(low, out[:rows], out[rows:]).astype(BF16)
        pump_in(i, "a", range(2 * pairs))
        return carry

    lax.fori_loop(0, 2 * pairs, attend, 0)
    loads[5].wait()
    part[...] = mm(att[...].reshape(both, half), wout[...])
    swap = links.copy(lambda: (part, got_a, place.sibling))
    x_both = xall[:, z, l].reshape(both, width).astype(F32)
    pump("p", 0)
    weight = jax.nn.sigmoid(jnp.sum(x_both * router, axis=-1, keepdims=True))
    lift = weight * own_live
    for flow in gg:
        flow.lent_own()
    swap.wait()
    attn = part[...] + got_a[...]
    attn_s[...] = attn
    resid = x_both + attn
    resid_s[...] = resid
    w_both = (resid * row_scale(resid) * gain_m).astype(BF16)
    wall[:, z, l] = w_both.reshape(2, rows, width)
    begin(gw)
    for load in loads[6:]:
        load.wait()

    fb = 512
    for b in range(ff // fb):
        cut = slice(b * fb, (b + 1) * fb)
        pre = mm(w_both, wup[:, cut])
        pre_s[:, cut] = pre
        act_s[:, cut] = gelu_parts(pre)[0].astype(BF16)
    pump("p", 1)
    part[...] = mm(act_s[...], wdown[...])
    swap = links.copy(lambda: (part, got_m, place.sibling))
    pump("p", 2)
    swap.wait()
    branch = attn_s[...] + (part[...] + got_m[...])
    x_both = xall[:, z, l].reshape(both, width).astype(F32)
    dy_both = gall[:, z, l].reshape(both, width).astype(F32)
    grad_branch = dy_both * lift
    g_both = grad_branch.astype(BF16)
    attn_s[...] = x_both + lift * branch
    rows_o[...] = attn_s[pl.ds(pl.multiple_of(c * rows, rows), rows), :].astype(BF16)
    grad_logit = (
        jnp.sum(dy_both * branch, axis=-1, keepdims=True) * own_live * weight * (1.0 - weight)
    )
    logit_s[...] = grad_logit
    sm[...] = jnp.zeros_like(sm)
    sm[2:3] = jnp.sum(grad_logit * on_core * x_both, axis=0, keepdims=True)
    pump("p", 3)
    for b in range(ff // fb):
        cut = slice(b * fb, (b + 1) * fb)
        grad_act = mm(g_both, wdown[cut, :], NT)
        gpre_s[:, cut] = (gelu_parts(pre_s[:, cut])[1] * grad_act).astype(BF16)
    pump("p", 4)
    part[...] = mm(gpre_s[...], wup[...], NT)
    swap = links.copy(lambda: (part, got_a, place.sibling))
    pump("p", 5)
    swap.wait()
    grad_w = part[...] + got_a[...]
    resid = resid_s[...]
    scale_m = row_scale(resid)
    hat = resid * scale_m
    sm[1:2] = jnp.sum(grad_w * on_core * hat, axis=0, keepdims=True)
    lifted = grad_w * gain_m
    grad_resid = scale_m * (lifted - hat * jnp.mean(lifted * hat, axis=-1, keepdims=True))
    resid_s[...] = grad_resid
    ga_both = (gall[:, z, l].reshape(both, width).astype(F32) * lift + grad_resid).astype(BF16)
    attended = att[...].reshape(both, half)
    piece = width // nseq
    grad_o = mm(attended, ga_both, TN).astype(BF16)
    for i in range(3):
        value = jnp.concatenate(
            [grad_o[:, 256 * i : 256 * i + 128], grad_o[:, 256 * i + 128 : 256 * i + 256]], axis=0
        )
        share[0, :, :, 0, i] = value.reshape(nz, LINES, piece, 128)
    grad_att = mm(ga_both, wout[...], NT).astype(BF16)
    for s in range(2):
        for p in range(pairs):
            dost[s * pairs + p] = stacked(grad_att, s, p)

    def attend_back(s, p):
        i = s * pairs + p
        keys = kall[i].reshape(total_rows, 128)
        vals = vall[i].reshape(total_rows, 128)
        prob = probs[i]
        grad_p = mm(dost[i], vals, NT)
        delta = jnp.sum(grad_p * prob, axis=-1, keepdims=True)
        grad_s = (prob * (grad_p - delta)).astype(BF16)
        out = mm(grad_s, keys) * HD ** (-0.5)
        gq[p, s] = jnp.where(low, out[:rows], out[rows:]).astype(BF16)
        gkv[p, s, :, :128] = mm(grad_s, qst[i], TN).astype(BF16)
        gkv[p, s, :, 128:] = mm(prob.astype(BF16), dost[i], TN).astype(BF16)

    def share_pair(p):
        group, unit = lax.div(p + 1, 2), lax.rem(p + 1, 2)
        grad_q = mm(uall[:, z, l].reshape(both, width), gq[p].reshape(both, 128), TN)
        share[group, :, :, unit, 0] = grad_q.astype(BF16).reshape(nz, LINES, piece, 128)
        span = width // 2

        def half_of(h, carry):
            at = pl.ds(pl.multiple_of(h * span, span), span)
            value = mm(uall[0, :, :, :, at].reshape(total_rows, span), gkv[p, 0], TN)
            value = value + mm(uall[1, :, :, :, at].reshape(total_rows, span), gkv[p, 1], TN)
            value = value.astype(BF16)
            zs = pl.ds(h * (nz // 2), nz // 2)
            for j in range(2):
                share[group, zs, :, unit, 1 + j] = value[:, 128 * j : 128 * (j + 1)].reshape(
                    nz // 2, LINES, piece, 128
                )
            return carry

        lax.fori_loop(0, 2, half_of, 0)

    def back(i, carry):
        p, s = lax.div(i, 2), lax.rem(i, 2)
        attend_back(s, p)
        pl.when(s == 1)(lambda: share_pair(p))
        pl.when(i == 1)(scatters[0].start)
        pl.when(i == 2 * pairs - 1)(scatters[1].start)
        pump_in(i, "b", range(2 * pairs))
        return carry

    lax.fori_loop(0, 2 * pairs, back, 0)
    for flow in gx:
        flow.wait_sent()

    pump("b", 6)
    for flow in gg:
        for j in range(LINES):
            flow.lent_line(j)
        flow.wait_sent()

    def weigh(i, carry):
        s, zz = lax.div(i, nz), lax.rem(i, nz)
        for line in range(LINES):
            gate = jax.nn.sigmoid(jnp.sum(xall[s, zz, line].astype(F32) * router, axis=-1, keepdims=True))
            alive = lax.broadcasted_iota(jnp.int32, (rows, 1), 0) < counts[s, zz * LINES + line]
            gall[s, zz, line] = (gall[s, zz, line].astype(F32) * jnp.where(alive, gate, 0.0)).astype(BF16)
        return carry

    lax.fori_loop(0, 2 * nz, weigh, 0)

    own_gq = jnp.concatenate([gq[p].reshape(both, 128) for p in range(pairs)], axis=1)
    part[...] = mm(own_gq, wqkv[:, :half], NT)

    def grad_u(s, j):
        size = 2 * LINES * rows
        at = pl.ds(pl.multiple_of(j * size, size), size)
        parts = [gkv[p, s, at, cut] for cut in (slice(0, 128), slice(128, 256)) for p in range(pairs)]
        return mm(jnp.concatenate(parts, axis=1), wqkv[:, half:], NT).reshape(2, LINES, rows, width)

    def part_of(s):
        return part[pl.ds(pl.multiple_of(s * rows, rows), rows), :]

    def theirs(j, carry):
        xall[other, pl.ds(2 * j, 2)] = grad_u(other, j).astype(BF16)
        pump_in(j, "v", range(nz // 2))
        return carry

    lax.fori_loop(0, nz // 2, theirs, 0)
    xall[other, z, l] = (xall[other, z, l].astype(F32) + part_of(other)).astype(BF16)
    lent = [
        links.copy(lambda j=j: (xall.at[other, pl.ds(2 * j, 2)], gsib.at[pl.ds(2 * j, 2)], place.sibling))
        for j in range(nz // 2)
    ]

    def ours(j, gain_total):
        value = grad_u(c, j)
        for i in range(nz // 2):
            pl.when(j == i)(lent[i].wait_recv)
        at = pl.ds(2 * j, 2)
        value = value + gsib[at].astype(F32)
        rows_x = xall[c, at].astype(F32)
        hat = rows_x * row_scale(rows_x)
        xall[c, at] = value.astype(BF16)
        pump_in(j, "u", range(nz // 2))
        return gain_total + jnp.sum(value * hat, axis=(0, 1, 2)).reshape(1, width)

    x_own = xall[c, z, l].astype(F32)
    gain_total = jnp.sum(part_of(c) * (x_own * row_scale(x_own)), axis=0, keepdims=True)
    attn_s[pl.ds(0, rows), :] = x_own
    gain_total = lax.fori_loop(0, nz // 2, ours, gain_total)
    xall[c, z, l] = (xall[c, z, l].astype(F32) + part_of(c)).astype(BF16)
    sm[0:1] = gain_total
    reduce_u.start()
    for k in range(1, nz):
        small[k].start()
    pump("u", nz)
    for flow in gw:
        for j in range(LINES):
            flow.lent_line(j)

    def put(b, i, which, stage, out):
        at = pl.ds(pl.multiple_of(b * hb + i * part_ff, part_ff), part_ff)
        return pltpu.make_async_copy(stage.at[i], out.at[at, :], osem.at[which, i])

    def ff_block(b, carry):
        cut = pl.ds(pl.multiple_of(b * hb, hb), hb)

        def ff_tile(t, carry):
            s, h = lax.div(t, 2), lax.rem(t, 2)
            at = pl.ds(pl.multiple_of(h * tile, tile), tile)
            zz = pl.ds(h * (nz // 2), nz // 2)
            act, slope = gelu_parts(mm(wall[s, zz].reshape(tile, width), wup[:, cut]))
            uall[s, zz, :, :, :hb] = act.astype(BF16).reshape(nz // 2, LINES, rows, hb)
            grad_act = mm(gall[s, zz].reshape(tile, width), wdown[cut, :], NT)
            grad_pre = (slope * grad_act).astype(BF16)
            for i in range(slots):
                gkv[i, s, at] = grad_pre[:, part_ff * i : part_ff * (i + 1)]
            pump_in(b * per_block + t, "h", [j for j in range(per_block * blocks) if j % per_block < tiles])
            return carry

        lax.fori_loop(0, tiles, ff_tile, 0)

        @pl.when(b >= 1)
        def _():
            for i in range(slots):
                put(b - 1, i, 0, stage_d, gdown_o).wait()
                put(b - 1, i, 1, stage_u, gup_o).wait()

        def flush(which, stage, out, lhs, rhs):
            value = mm(lhs, rhs[...].reshape(2 * total_rows, width), TN).astype(BF16)
            for i in range(slots):
                stage[i] = value[i * part_ff : (i + 1) * part_ff]
            for i in range(slots):
                put(b, i, which, stage, out).start()

        flush(0, stage_d, gdown_o, uall[:, :, :, :, :hb].reshape(2 * total_rows, hb), gall)
        pump_in(b * per_block + tiles, "h", range(tiles, per_block * blocks, per_block))
        slopes = [gkv[i].reshape(2 * total_rows, part_ff) for i in range(slots)]
        flush(1, stage_u, gup_o, jnp.concatenate(slopes, axis=1), wall)
        pump_in(b * per_block + tiles + 1, "h", range(tiles + 1, per_block * blocks, per_block))
        return carry

    lax.fori_loop(0, blocks, ff_block, 0)
    pump("z", 0)
    assert not left
    out_copy = pltpu.make_async_copy(res, res_o, osem.at[2, 0])
    out_copy.start()
    for i in range(slots):
        put(blocks - 1, i, 0, stage_d, gdown_o).wait()
        put(blocks - 1, i, 1, stage_u, gup_o).wait()
    links.drain()
    out_copy.wait()


def finish_kernel(
    tokens, cot, pick, rows, grow, small, res_h, gup_h, gdown_h,
    mixed_o, gtok_o, gain_a_o, gain_m_o, router_o, gqkv_o, gout_o, gup_o, gdown_o,
    res, gup, gdown, qkv_s, out_s, up_s, down_s, sem_in, sem_out,
):
    up_cuts = [slice(i * 384, (i + 1) * 384) for i in range(gup.shape[0] // 384)]
    down_cuts = [slice(i * 384, (i + 1) * 384) for i in range(gdown.shape[0] // 384)]
    loads, stores = [], []

    def load(src, dst):
        loads.append(pltpu.make_async_copy(src, dst, sem_in.at[len(loads)]))
        loads[-1].start()
        return loads[-1]

    def store(src, dst):
        stores.append(pltpu.make_async_copy(src, dst, sem_out.at[len(stores)]))
        stores[-1].start()

    downs = [load(gdown_h.at[cut], gdown.at[cut]) for cut in down_cuts]
    groups = [load(res_h.at[g], res.at[g]) for g in range(2)]
    ups = [load(gup_h.at[cut], gup.at[cut]) for cut in up_cuts]
    for cut, got in zip(down_cuts, downs):
        got.wait()
        down_s[cut] = gdown[cut].astype(F32)
        store(down_s.at[cut], gdown_o.at[cut])
    width = rows.shape[1]
    half = width // 2
    for got in groups:
        got.wait()
    for i in range(3):
        for unit in range(1, 4):
            cut = slice((unit - 1) * 128, unit * 128)
            qkv_s[i, :, cut] = res[unit // 2, :, :, unit % 2, i].reshape(width, 128).astype(F32)
        store(qkv_s.at[i], gqkv_o.at[i])
        value = res[0, :, :, 0, i].reshape(width, 128).astype(F32)
        out_s[:, 256 * i : 256 * i + 128] = value[:half]
        out_s[:, 256 * i + 128 : 256 * i + 256] = value[half:]
    store(out_s, gout_o)
    for cut, got in zip(up_cuts, ups):
        got.wait()
        up_s[:, cut] = gup[cut].astype(F32).T
        store(up_s.at[:, cut], gup_o.at[:, cut])
    chosen = mm(pick[...], jnp.ones(rows.shape, BF16), TN) > 0.5
    mixed_o[...] = jnp.where(chosen, mm(pick[...], rows[...], TN), tokens[...].astype(F32)).astype(BF16)
    grad = grow[...]
    hi = grad.astype(BF16)
    rest = grad - hi.astype(F32)
    mid = rest.astype(BF16)
    lo = (rest - mid.astype(F32)).astype(BF16)
    spread = mm(pick[...], hi, TN) + (mm(pick[...], mid, TN) + mm(pick[...], lo, TN))
    gtok_o[...] = (cot[...].astype(F32) + spread).astype(BF16)
    gain_a_o[...] = small[0:1].reshape(half)
    gain_m_o[...] = small[1:2].reshape(half)
    router_o[...] = small[2:3].reshape(half)
    for made in stores:
        made.wait()


def fused_body(
    tokens, cotangent, w_qkv, w_out, w_up, w_down, gain_attn, gain_mlp, router, picked, counts
):
    nseq = lax.axis_size("seq")
    nz = nseq // LINES
    rows = picked.shape[1] // nseq
    block, width = tokens.shape[1:]
    half, ff = w_out.shape[0], w_up.shape[1]
    pairs = half // 128
    total_rows = nseq * rows
    piece = width // nseq
    vm = pltpu.VMEM
    dma = pltpu.SemaphoreType.DMA
    wide = (2, nz, LINES, rows, width)
    heads = (2 * pairs, nz, LINES, rows, 128)
    both = (2 * rows, width)
    part = (2, 3, piece, 128)
    scratch = [
        vm((block, width), BF16), vm((block, width), BF16),
        vm((width, 3 * half), BF16), vm((half, width), BF16), vm((width, ff), BF16), vm((ff, width), BF16), dma((8,)),
        vm((2, 8, half), F32), vm(wide, BF16), vm(wide, BF16), vm(heads, BF16), vm(heads, BF16),
        vm((2 * pairs, 2 * rows, 128), BF16), vm((2, rows, total_rows), F32),
        vm((2 * pairs, 2 * rows, total_rows), F32), vm((2, rows, half), BF16),
        vm((8, 128), F32), vm(both, F32), vm(both, F32), vm((2 * rows, 1), F32),
        vm(both, F32), vm(both, F32), vm(both, F32),
        vm(wide, BF16), vm(wide, BF16), vm((2 * rows, ff), F32), vm((2 * rows, ff), BF16), vm((2 * rows, ff), BF16),
        vm((2 * pairs, 2 * rows, 128), BF16), vm((pairs, 2, rows, 128), BF16), vm((pairs, 2, total_rows, 256), BF16),
        vm((nz, LINES, rows, width), BF16), vm((nz, 2, rows, width), BF16), vm((nz, rows, width), BF16),
        vm((nz - 1, rows, width), BF16),
        vm((2, nz, LINES, *part), BF16), vm((2, nz, 2, *part), BF16), vm((2, nz, *part), BF16),
        vm((2, nz - 1, *part), BF16), vm((2, nz, LINES, *part), BF16),
        vm((8, width), F32), vm((nz - 1, 8, width), F32), vm((2, 8, width), F32), vm((2, 8, width), F32),
        vm((2, 8, width), F32),
        vm((2, 256, width), BF16), vm((2, 256, width), BF16), dma((3, 2)),
        dma((MESSAGES,)), dma((MESSAGES,)),
    ]
    in_vmem = pl.BlockSpec(memory_space=pltpu.VMEM)
    in_hbm = pl.BlockSpec(memory_space=pl.ANY)
    in_smem = pl.BlockSpec(memory_space=pltpu.SMEM)
    shaped = jax.ShapeDtypeStruct
    pick, out_rows, grad_rows, res, grad_up, grad_down, small = pl.pallas_call(
        functools.partial(layer_kernel, nz),
        out_shape=(
            shaped((rows, block), BF16),
            shaped((rows, width), BF16),
            shaped((rows, width), F32),
            shaped((2, nz, LINES, *part), BF16),
            shaped((ff, width), BF16),
            shaped((ff, width), BF16),
            shaped((8, half), F32),
        ),
        in_specs=[in_hbm] * 2 + [in_vmem, in_smem] + [in_vmem] * 3 + [in_hbm] * 4,
        out_specs=(in_vmem, in_vmem, in_vmem, in_hbm, in_hbm, in_hbm, in_vmem),
        scratch_shapes=scratch,
        compiler_params=pltpu.CompilerParams(
            collective_id=0, has_side_effects=True, vmem_limit_bytes=VMEM_BYTES
        ),
        name="layer",
    )(
        tokens[0], cotangent[0], picked, counts,
        gain_attn, gain_mlp, router, w_qkv, w_out, w_up, w_down,
    )
    mixed, grad_tokens, gain_a, gain_m, grad_r, grad_qkv, grad_out, grad_up, grad_down = pl.pallas_call(
        finish_kernel,
        out_shape=(
            shaped((block, width), BF16),
            shaped((block, width), BF16),
            shaped((half,), F32),
            shaped((half,), F32),
            shaped((half,), F32),
            shaped((3, width, half), F32),
            shaped((half, width), F32),
            shaped((width, ff), F32),
            shaped((ff, width), F32),
        ),
        in_specs=[in_vmem] * 6 + [in_hbm] * 3,
        out_specs=(in_vmem,) * 5 + (in_hbm,) * 4,
        scratch_shapes=[
            vm((2, nz, LINES, *part), BF16), vm((ff, width), BF16), vm((ff, width), BF16),
            vm((3, width, half), F32), vm((half, width), F32), vm((width, ff), F32), vm((ff, width), F32),
            dma((16,)), dma((16,)),
        ],
        compiler_params=pltpu.CompilerParams(vmem_limit_bytes=VMEM_BYTES),
        name="finish",
    )(tokens[0], cotangent[0], pick, out_rows, grad_rows, small, res, grad_up, grad_down)
    return (
        mixed[None], grad_tokens[None], grad_qkv, grad_out, grad_up, grad_down, gain_a, gain_m, grad_r,
    )


def body(tokens, *rest):
    nseq, cores = lax.axis_size("seq"), lax.axis_size("wa")
    fits = nseq == 4 * LINES and cores == 2 and rest[-2].shape[1] == nseq * CAP
    return (fused_body if fits else spread_body)(tokens, *rest)


CAP = 80


def norm_rows(value, gain):
    scale = lax.rsqrt(jnp.mean(value * value, axis=-1, keepdims=True) + EPS)
    return (value * scale * gain, scale)


def norm_back(value, scale, gain, grad_out):
    normed = value * scale
    weighted = grad_out * gain
    grad_value = scale * (weighted - normed * jnp.mean(weighted * normed, axis=-1, keepdims=True))
    return (grad_value, normed)


def gelu_back(pre, grad):
    unused, pull = jax.vjp(lambda value: jax.nn.gelu(value, approximate=True), pre)
    return pull(grad)[0]


def spread_body(
    tokens, cotangent, w_qkv, w_out, w_up, w_down, gain_attn, gain_mlp, router, picked, counts
):
    f32 = jnp.float32
    bf16 = jnp.bfloat16
    nseq = lax.axis_size("seq")
    me = lax.axis_index("seq")
    side = lax.axis_index("wa")
    slots = jnp.arange(CAP, dtype=jnp.int32)
    own_rows = lax.dynamic_slice(picked, (side, me * CAP), (1, CAP))[0]
    x_own = jnp.take(tokens[0], own_rows, axis=0)
    dy_own = jnp.take(cotangent[0], own_rows, axis=0).astype(f32)
    x_rows, g_attn, g_mlp, w_router = (
        lax.all_gather(x_own[None], "wa", axis=0, tiled=True),
        lax.all_gather(gain_attn, "wa", axis=0, tiled=True),
        lax.all_gather(gain_mlp, "wa", axis=0, tiled=True),
        lax.all_gather(router, "wa", axis=0, tiled=True),
    )
    qkv_w, out_w, up_w, down_w = (w_qkv, w_out, w_up, w_down)
    streams = jnp.arange(lax.axis_size("wa"))
    stream_picked = jnp.take(picked, streams, axis=0)
    stream_counts = jnp.take(counts, streams, axis=0)
    key_index = jnp.arange(nseq * CAP, dtype=jnp.int32)
    key_device = key_index // CAP
    key_pos = stream_picked * nseq + key_device[None, :]
    key_live = (key_index % CAP)[None, :] < jnp.take(stream_counts, key_device, axis=1)
    query_index = me * CAP + slots
    query_pos = lax.dynamic_slice_in_dim(key_pos, me * CAP, CAP, 1)
    own_live = (slots < counts[side, me]).astype(f32)
    gains_a = g_attn.astype(f32)
    gains_m = g_mlp.astype(f32)
    x_keep = x_own.astype(f32)
    weight = jax.nn.sigmoid(jnp.dot(x_own, w_router, preferred_element_type=f32))
    x_wide = x_rows.astype(f32)
    normed_a, scale_a = norm_rows(x_wide, gains_a)
    u_rows = normed_a.astype(bf16)
    qkv = jnp.einsum("srd,cde->csre", u_rows, qkv_w, preferred_element_type=f32).astype(bf16)
    query = qkv[0]
    local_kv = qkv[1:]
    batch = query.shape[0]
    heads = query.shape[-1] // HD
    factor = HD ** (-0.5)
    split_q = query.reshape(batch, CAP, heads, HD)
    kv_all = lax.all_gather(local_kv, "seq", axis=2, tiled=True)
    block = 8 * CAP
    nblock = kv_all.shape[2] // block

    def block_of(start):
        keys_b = lax.dynamic_slice_in_dim(kv_all[0], start, block, 1).reshape(
            batch, block, heads, HD
        )
        vals_b = lax.dynamic_slice_in_dim(kv_all[1], start, block, 1).reshape(
            batch, block, heads, HD
        )
        k_pos = lax.dynamic_slice_in_dim(key_pos, start, block, 1)
        k_live = lax.dynamic_slice_in_dim(key_live, start, block, 1)
        k_index = start + jnp.arange(block, dtype=jnp.int32)
        allowed = (k_pos[:, None, :] <= query_pos[:, :, None]) & (
            k_live[:, None, :] | (k_index[None, None, :] == query_index[None, :, None])
        )
        raw = jnp.einsum("sqhd,skhd->shqk", split_q, keys_b, preferred_element_type=f32) * factor
        return (keys_b, vals_b, allowed, jnp.where(allowed[:, None], raw, NEG))

    def max_sum(number, carry):
        top, total = carry
        unused_k, unused_v, allowed, scores = block_of(number * block)
        new_top = jnp.maximum(top, jnp.max(scores, axis=-1, keepdims=True))
        expd = jnp.where(allowed[:, None], jnp.exp(scores - new_top), 0.0)
        return (new_top, total * jnp.exp(top - new_top) + jnp.sum(expd, axis=-1, keepdims=True))

    top_start = jnp.full((batch, heads, CAP, 1), NEG, f32)
    top, total = lax.fori_loop(
        0, nblock, max_sum, (top_start, jnp.zeros((batch, heads, CAP, 1), f32))
    )
    lse = top + jnp.log(total)

    def weigh(number, acc):
        unused_k, vals_b, allowed, scores = block_of(number * block)
        probs_low = jnp.exp(scores - lse).astype(bf16)
        return acc + jnp.einsum("shqk,skhd->sqhd", probs_low, vals_b, preferred_element_type=f32)

    acc = lax.fori_loop(0, nblock, weigh, jnp.zeros((batch, CAP, heads, HD), f32))
    attended = acc.reshape(query.shape).astype(bf16)
    attn_part = jnp.einsum("sqe,ed->sqd", attended, out_w, preferred_element_type=f32)
    attn_own = lax.psum_scatter(attn_part, "wa", scatter_dimension=0, tiled=True)[0]
    resid = x_keep + attn_own
    normed_m, scale_m = norm_rows(resid, gains_m)
    w_own = normed_m.astype(bf16)
    w_rows = lax.all_gather(w_own[None], "wa", axis=0, tiled=True)
    pre = jnp.einsum("srd,df->srf", w_rows, up_w, preferred_element_type=f32)
    act = jax.nn.gelu(pre, approximate=True).astype(bf16)
    mlp_part = jnp.einsum("srf,fd->srd", act, down_w, preferred_element_type=f32)
    mlp_own = lax.psum_scatter(
        mlp_part.astype(jnp.bfloat16), "wa", scatter_dimension=0, tiled=True
    ).astype(jnp.float32)[0]
    branch = attn_own + mlp_own
    lift = (weight * own_live)[:, None]
    out_rows = (x_keep + lift * branch).astype(bf16)
    mixed_out = tokens.at[0, own_rows].set(out_rows)
    grad_branch = dy_own * lift
    grad_logit = jnp.sum(dy_own * branch, axis=-1) * own_live * weight * (1.0 - weight)
    grad_router = jnp.dot(grad_logit, x_keep, precision=lax.Precision.HIGHEST)
    grad_m = grad_branch.astype(bf16)
    grad_m_rows = lax.all_gather(grad_m[None], "wa", axis=0, tiled=True)
    grad_down = jnp.einsum("srf,srd->fd", act, grad_m_rows, preferred_element_type=f32)
    grad_act = jnp.einsum("srd,fd->srf", grad_m_rows, down_w, preferred_element_type=f32)
    grad_pre = gelu_back(pre, grad_act).astype(bf16)
    grad_up = jnp.einsum("srd,srf->df", w_rows, grad_pre, preferred_element_type=f32)
    grad_w_part = jnp.einsum("srf,df->srd", grad_pre, up_w, preferred_element_type=f32)
    grad_w_own = lax.psum_scatter(grad_w_part, "wa", scatter_dimension=0, tiled=True)[0]
    grad_resid, hat_m = norm_back(resid, scale_m, gains_m, grad_w_own)
    grad_gain_m = jnp.sum(grad_w_own * hat_m, axis=0)
    grad_a = (grad_branch + grad_resid).astype(bf16)
    grad_a_rows = lax.all_gather(grad_a[None], "wa", axis=0, tiled=True)
    grad_out = jnp.einsum("sqe,sqd->ed", attended, grad_a_rows, preferred_element_type=f32)
    grad_attended = jnp.einsum(
        "sqd,ed->sqe", grad_a_rows, out_w, preferred_element_type=f32
    ).astype(bf16)
    split_do = grad_attended.reshape(batch, CAP, heads, HD)

    def delta_step(number, delta):
        unused_k, vals_b, allowed, scores = block_of(number * block)
        probs = jnp.exp(scores - lse)
        grad_probs = jnp.einsum("sqhd,skhd->shqk", split_do, vals_b, preferred_element_type=f32)
        return delta + jnp.sum(grad_probs * probs, axis=-1, keepdims=True)

    delta = lax.fori_loop(0, nblock, delta_step, jnp.zeros((batch, heads, CAP, 1), f32))

    def grad_step(number, carry):
        grad_query, holder = carry
        start = number * block
        keys_b, vals_b, allowed, scores = block_of(start)
        probs = jnp.exp(scores - lse)
        grad_probs = jnp.einsum("sqhd,skhd->shqk", split_do, vals_b, preferred_element_type=f32)
        grad_scores = (probs * (grad_probs - delta)).astype(bf16)
        grad_query = (
            grad_query
            + jnp.einsum("shqk,skhd->sqhd", grad_scores, keys_b, preferred_element_type=f32)
            * factor
        )
        grad_keys = (
            jnp.einsum("shqk,sqhd->skhd", grad_scores, split_q, preferred_element_type=f32) * factor
        )
        grad_values = jnp.einsum(
            "shqk,sqhd->skhd", probs.astype(bf16), split_do, preferred_element_type=f32
        )
        paired = jnp.stack([grad_keys, grad_values]).reshape(2, batch, block, heads * HD)
        holder = lax.dynamic_update_slice_in_dim(holder, paired, start, 2)
        return (grad_query, holder)

    grad_query, holder = lax.fori_loop(
        0,
        nblock,
        grad_step,
        (jnp.zeros((batch, CAP, heads, HD), f32), jnp.zeros(kv_all.shape, f32)),
    )
    kv_total = lax.psum_scatter(holder.astype(bf16), "seq", scatter_dimension=2, tiled=True)
    grad_qkv_rows = jnp.concatenate(
        [grad_query.reshape(query.shape)[None].astype(bf16), kv_total.astype(bf16)], axis=0
    )
    grad_qkv = jnp.einsum("srd,csre->cde", u_rows, grad_qkv_rows, preferred_element_type=f32)
    grad_u_part = jnp.einsum("csre,cde->srd", grad_qkv_rows, qkv_w, preferred_element_type=f32)
    part_gain_a = jnp.sum(grad_u_part * (x_wide * scale_a), axis=(0, 1))
    grad_u_all, grad_gain_a, grad_gain_m, grad_router = (
        lax.psum_scatter(
            grad_u_part.astype(jnp.bfloat16), "wa", scatter_dimension=0, tiled=True
        ).astype(jnp.float32),
        lax.psum_scatter(
            part_gain_a.astype(jnp.bfloat16), "wa", scatter_dimension=0, tiled=True
        ).astype(jnp.float32),
        lax.psum_scatter(
            grad_gain_m.astype(jnp.bfloat16), "wa", scatter_dimension=0, tiled=True
        ).astype(jnp.float32),
        lax.psum_scatter(
            grad_router.astype(jnp.bfloat16), "wa", scatter_dimension=0, tiled=True
        ).astype(jnp.float32),
    )
    grad_u_own = grad_u_all[0]
    grad_x_norm, unused = norm_back(x_keep, scale_a[side], gains_a, grad_u_own)
    grad_rows = grad_x_norm + grad_resid + grad_logit[:, None] * w_router.astype(f32)[None, :]
    grad_tokens = cotangent.astype(f32).at[0, own_rows].add(grad_rows).astype(bf16)
    shares = (grad_qkv, grad_out, grad_up, grad_down, grad_gain_a, grad_gain_m, grad_router)
    large = lax.psum(tuple(share.astype(bf16) for share in shares[:4]), "seq")
    small = lax.psum(shares[4:], "seq")
    summed = tuple(part.astype(f32) for part in large) + small
    return (
        mixed_out,
        grad_tokens,
        summed[0],
        summed[1],
        summed[2],
        summed[3],
        summed[4],
        summed[5],
        summed[6],
    )


def solution(mesh):
    return jax.shard_map(
        body,
        mesh=mesh,
        in_specs=(
            P("wa", "seq", None),
            P("wa", "seq", None),
            P(None, None, "wa"),
            P("wa", None),
            P(None, "wa"),
            P("wa", None),
            P("wa"),
            P("wa"),
            P("wa"),
            P(),
            P(),
        ),
        out_specs=(
            P("wa", "seq", None),
            P("wa", "seq", None),
            P(None, None, "wa"),
            P("wa", None),
            P(None, "wa"),
            P("wa", None),
            P("wa"),
            P("wa"),
            P("wa"),
        ),
        check_vma=False,
    )
```

```python
import functools

import jax
import jax.numpy as jnp
from jax import lax
from jax.experimental import pallas as pl
from jax.experimental.pallas import tpu as pltpu
from jax.sharding import PartitionSpec as P

HD = 64
EPS = 1e-05
NEG = -1e30
FAR = 1e9
LINES = 4
MESSAGES = 420
VMEM_BYTES = 64 << 20
EARLY_ROWS = 48
COTANGENT_AT = 1
POINTS = {"x": 0, "a": 8, "p": 14, "b": 20, "v": 27, "u": 31, "h": 36, "z": 54}
SCHEDULE = (
    (3, 0, 1, 15, 21, 16, 2, 17, 11, 4),
    (18, 19, 26, 9),
    (7, 5, 24, 6, 23, 20),
    (22, 10, 25, 8),
    (27, 30),
    (51, 12, 33, 45),
    (29, 13, 28, 14),
    (52, 37, 31),
    (41, 56, 34),
    (46,),
    (32, 48),
    (38, 53),
    (35, 49),
    (42,),
    (39, 47, 54),
    (36,),
    (),
    (40, 57),
    (50, 43, 55),
    (63, 61, 60, 58),
    (75, 81, 82, 44),
    (62, 69, 65),
    (67, 76, 64, 78, 59, 71, 79),
    (68, 86, 154, 151),
    (77, 150),
    (153, 156, 83),
    (152,),
    (80, 157),
    (88, 66, 70, 73, 155),
    (),
    (),
    (87, 158),
    (162, 84, 85, 72),
    (),
    (),
    (164, 159, 163, 89, 168, 166, 193, 194, 195, 167, 74, 196),
    (160, 170, 169, 161),
    (165, 171, 188, 174),
    (172,),
    (175,),
    (186, 178),
    (177, 180, 176),
    (189,),
    (90, 105, 173, 187, 179),
    (111, 181, 97),
    (93, 106, 182, 91, 112),
    (107, 190, 94, 120, 135, 185, 108, 109),
    (123, 136, 141, 121, 92, 98, 127),
    (113, 116, 99, 142),
    (115, 124, 184, 191, 183),
    (101, 118, 102, 110, 128, 144, 122),
    (114, 95, 143, 96, 138, 129),
    (131, 125, 139, 100, 126, 119),
    (147, 146, 103),
    (137, 140, 133, 192, 117, 148, 130, 132, 145, 134, 104, 149),
)
MESH = pl.DeviceIdType.MESH
F32 = jnp.float32
BF16 = jnp.bfloat16
NN = (((1,), (0,)), ((), ()))
NT = (((1,), (1,)), ((), ()))
TN = (((0,), (0,)), ((), ()))
GELU_A = 0.7978845608028654
GELU_B = 0.044715


def mm(a, b, dims=NN):
    return lax.dot_general(a, b, dims, preferred_element_type=F32)


def gelu_parts(pre):
    square = pre * pre
    t = jnp.tanh(GELU_A * pre * (1.0 + GELU_B * square))
    half = 0.5 * (1.0 + t)
    slope = half + 0.5 * pre * (1.0 - t * t) * (GELU_A * (1.0 + 3.0 * GELU_B * square))
    return pre * half, slope


def row_scale(value):
    return lax.rsqrt(jnp.mean(value * value, axis=-1, keepdims=True) + EPS)


class Message:
    def __init__(self, links, i, ends):
        self.links, self.i, self.ends = links, i, ends

    def make(self):
        src, dst, device = self.ends()
        return pltpu.make_async_remote_copy(
            src_ref=src,
            dst_ref=dst,
            send_sem=self.links.send.at[self.i],
            recv_sem=self.links.recv.at[self.i],
            device_id=device,
            device_id_type=MESH,
        )

    def start(self):
        self.make().start()
        self.links.pending.append(self)
        return self

    def wait_recv(self):
        self.make().wait_recv()

    def wait_send(self):
        self.links.forget(self)
        self.make().wait_send()

    def wait(self):
        self.wait_send()
        self.wait_recv()


class Links:
    def __init__(self, send, recv):
        self.send, self.recv, self.used, self.pending = send, recv, 0, []

    def many(self, count):
        self.used += count
        return self.used - count

    def numbered(self, i, ends):
        return Message(self, i, ends)

    def forget(self, what):
        self.pending = [other for other in self.pending if other is not what]

    def message(self, ends):
        return self.numbered(self.many(1), ends)

    def copy(self, ends):
        return self.message(ends).start()

    def drain(self):
        for message in list(self.pending):
            message.wait_send()


class Place:
    def __init__(self, nz):
        self.me, self.c = lax.axis_index("seq"), lax.axis_index("wa")
        self.nz = nz
        self.z, self.l = lax.div(self.me, LINES), lax.rem(self.me, LINES)
        y, x = lax.div(self.l, 2), lax.rem(self.l, 2)
        over_y, over_x = self.l + 2 - 4 * y, self.l + 1 - 2 * x
        self.l2 = over_y * (1 - self.c) + over_x * self.c
        self.l3 = over_x * (1 - self.c) + over_y * self.c
        self.l23 = 3 - self.l
        self.sibling = (self.me, 1 - self.c)
        near = [sorted(range(nz), key=lambda other: abs(other - here)) for here in range(nz)]
        self.sources = []
        for i in range(nz):
            source = near[0][i] + 0 * self.z
            for here in range(1, nz):
                source = jnp.where(self.z == here, near[here][i], source)
            self.sources.append(source)

    def turn(self, i):
        return self.sources[i]

    def around(self, k):
        return lax.rem(self.z + k, self.nz)

    def at(self, z, line):
        return (z * LINES + line, self.c)


class Chain:
    def __init__(self, place, links, shard):
        self.p, self.links, self.shard = place, links, shard
        self.i = links.many(2 * place.nz)

    def hop(self, source, to, down, hops):
        i = self.i + down * self.p.nz + hops
        return self.links.numbered(
            i, lambda: (self.shard(source), self.shard(source), self.p.at(to, self.p.l))
        )

    def start(self):
        p = self.p
        pl.when(p.z + 1 < p.nz)(lambda: self.hop(p.z, p.z + 1, 0, 1).make().start())
        pl.when(p.z > 0)(lambda: self.hop(p.z, p.z - 1, 1, 1).make().start())
        self.links.pending.append(self)

    def arrive(self, i):
        p = self.p
        source = p.turn(i)
        down = jnp.where(source > p.z, 1, 0)
        hops = jnp.where(source > p.z, source - p.z, p.z - source)
        self.hop(source, p.z, down, hops).wait_recv()
        on = p.z + 1 - 2 * down
        pl.when((on >= 0) & (on < p.nz))(lambda: self.hop(source, on, down, hops + 1).make().start())

    def wait_send(self):
        p = self.p
        self.links.forget(self)
        for hops in range(1, p.nz):
            up = (p.z + 1 < p.nz) & (p.z >= hops - 1)
            down = (p.z > 0) & (p.z + hops - 1 < p.nz)
            pl.when(up)(lambda: self.hop(p.z, p.z, 0, hops).make().wait_send())
            pl.when(down)(lambda: self.hop(p.z, p.z, 1, hops).make().wait_send())


class Gather:
    def __init__(self, place, links, buf, lend, own=False, early=True, cut=None):
        self.p = p = place
        self.early = early
        lines = (p.l, p.l2, p.l3, p.l23)

        def at(source, line):
            ref = buf().at[source, line]
            return ref if cut is None else ref.at[cut]

        def message(j, i, device):
            def ends():
                shard = at(p.turn(i), lines[j])
                return shard, shard, device()

            return links.message(ends)

        over = range(p.nz)
        self.second = {i: message(0, i, lambda: p.at(p.z, p.l2)) for i in (over if early else (0,))}
        self.third = {(j, i): message(j, i, lambda: p.at(p.z, p.l3)) for j in range(2) for i in over}
        self.chains = [Chain(place, links, lambda s, j=j: at(s, lines[j])) for j in range(1 if early else 2)]
        keys = [(j, i) for j in range(4) for i in over if j or i or own] if lend else []
        self.lent = {key: message(*key, lambda: p.sibling) for key in keys}
        self.waited = set()
        self.all = [*self.second.values(), *self.third.values(), *self.lent.values(), *self.chains]

    def wait_sent(self):
        for message in self.all:
            message.wait_send()

    def hand_over(self, *key):
        if key in self.lent:
            self.lent[key].start()

    def start(self):
        self.chains[0].start()
        self.second[0].start()
        self.third[0, 0].start()
        self.hand_over(0, 0)

    def over_z(self, j, i):
        self.chains[j].arrive(i)
        self.third[j, i].start()
        if self.early:
            self.second[i].start()
        self.hand_over(j, i)

    def over_second(self, i):
        self.second[i].wait_recv()
        if not self.early:
            self.chains[1].start()
        self.third[1, i].start()
        self.hand_over(1, i)

    def over_third(self, j, i):
        self.third[j, i].wait_recv()
        self.hand_over(2 + j, i)

    def lent_own(self):
        self.waited.add((0, 0))
        self.lent[0, 0].wait_recv()

    def lent_line(self, j):
        for i in range(self.p.nz):
            if (j, i) in self.lent and (j, i) not in self.waited:
                self.waited.add((j, i))
                self.lent[j, i].wait_recv()

    def steps(self):
        part, over = functools.partial, range(self.p.nz)
        out = [part(self.over_z, j, i) for j in range(len(self.chains)) for i in over[1:]]
        out += [part(self.over_second, i) for i in self.second]
        return out + [part(self.over_third, j, i) for j, i in self.third]


def two_ways(place, links, buf, lend, own=False, cuts=(None, None)):
    return [
        Gather(place, links, buf, lend, own, early=early, cut=cut) for early, cut in zip((True, False), cuts)
    ]


class Scatter:
    def __init__(self, place, links, acc, got1, got2, got3):
        self.p = p = place
        self.acc, self.got1, self.got2, self.got3 = acc, got1, got2, got3
        self.order = (2, 1, 3, 0) if p.nz == 4 else (*range(1, p.nz), 0)

        def one(o, j, line):
            return lambda: (acc().at[p.around(o), line], got1().at[p.around(o), j], p.at(p.z, p.l3))

        def two(o):
            return lambda: (acc().at[p.around(o), p.l2], got2().at[p.around(o)], p.at(p.z, p.l2))

        def three(o):
            return lambda: (acc().at[p.around(o), p.l], got3().at[o - 1], p.at(p.around(o), p.l))

        self.m1 = {
            (j, o): links.message(one(o, j, line)) for o in self.order for j, line in ((0, p.l23), (1, p.l3))
        }
        self.m2 = {o: links.message(two(o)) for o in self.order}
        self.m3 = {o: links.message(three(o)) for o in range(1, p.nz)}

    def add(self, z, line, got):
        acc = self.acc()
        acc[z, line] = (acc[z, line].astype(F32) + got.astype(F32)).astype(BF16)

    def launch(self, o):
        for j in range(2):
            self.m1[j, o].start()

    def start(self):
        for o in self.order:
            self.launch(o)

    def far(self, o):
        p, zz = self.p, self.p.around(o)
        self.m1[0, o].wait_recv()
        self.add(zz, p.l2, self.got1()[zz, 0])
        self.m2[o].start()

    def near(self, o):
        p, zz = self.p, self.p.around(o)
        self.m1[1, o].wait_recv()
        self.add(zz, p.l, self.got1()[zz, 1])

    def along(self, o):
        p, zz = self.p, self.p.around(o)
        self.m2[o].wait_recv()
        if o:
            self.add(zz, p.l, self.got2()[zz])
            self.m3[o].start()

    def total(self):
        p = self.p
        total = self.acc()[p.z, p.l].astype(F32) + self.got2()[p.z].astype(F32)
        for o in range(1, p.nz):
            self.m3[o].wait_recv()
            total = total + self.got3()[o - 1].astype(F32)
        return total

    def steps(self):
        return [functools.partial(step, o) for step in (self.far, self.near, self.along) for o in self.order]


def layer_kernel(
    nz,
    tokens_h, cot_h, picked, counts, gain_a_r, gain_m_r, router_r, wqkv_h, wout_h, wup_h, wdown_h,
    pick_o, rows_o, grow_o, res_o, gup_o, gdown_o, small_o,
    tokens, cot, wqkv, wout, wup, wdown, wsem,
    gvec, xall, uall, kall, vall, qst, bias, probs, att,
    dy_s, attn_s, resid_s, logit_s, part, got_a, got_m,
    wall, gall, pre_s, act_s, gpre_s, dost, gq, gkv,
    gsib, gu1, gu2, gu3, share, sh1, sh2, sh3, res,
    sm, smz, smy, smx, smw, stage_u, stage_d, osem,
    send, recv,
):
    place = Place(nz)
    links = Links(send, recv)
    c, l, z = place.c, place.l, place.z
    other = 1 - c
    rows, width = grow_o.shape
    both = 2 * rows
    block = tokens.shape[0]
    pairs = wout.shape[0] // 128
    nseq = nz * LINES
    total_rows = nseq * rows
    ff = wup.shape[1]

    barrier = pltpu.get_barrier_semaphore()
    peers = [place.at(z, place.l2), place.at(z, place.l3), place.sibling]
    for peer in peers:
        pl.semaphore_signal(barrier, inc=1, device_id=peer, device_id_type=MESH)

    def greet(on):
        pl.semaphore_signal(barrier, inc=1, device_id=place.at(on, l), device_id_type=MESH)

    pl.when(z + 1 < nz)(lambda: greet(z + 1))
    pl.when(z > 0)(lambda: greet(z - 1))
    half = wout.shape[0]
    pairs_of = [(tokens_h, tokens), (cot_h, cot)]
    pairs_of += [(wqkv_h.at[i], wqkv.at[:, i * half : (i + 1) * half]) for i in range(3)]
    pairs_of += [(wout_h, wout), (wup_h, wup), (wdown_h, wdown)]
    loads = [pltpu.make_async_copy(h, v, wsem.at[i]) for i, (h, v) in enumerate(pairs_of)]
    for load in loads[:2]:
        load.start()

    cuts = (pl.ds(0, EARLY_ROWS), pl.ds(EARLY_ROWS, rows - EARLY_ROWS))
    gx = two_ways(place, links, lambda: xall.at[c], True, True, cuts)
    gw = two_ways(place, links, lambda: wall.at[c], True, False, cuts)
    gg = two_ways(place, links, lambda: gall.at[c], True, True, cuts)
    scatters = [
        Scatter(
            place, links, lambda g=g: share.at[g], lambda g=g: sh1.at[g], lambda g=g: sh2.at[g], lambda g=g: sh3.at[g]
        )
        for g in range(2)
    ]
    gathers = [two_ways(place, links, lambda g=g: res.at[g], False, False, (0, 1)) for g in range(2)]
    reduce_u = Scatter(place, links, lambda: xall.at[c], lambda: gu1, lambda: gu2, lambda: gu3)
    small = {
        "y": links.message(lambda: (smy.at[0], smy.at[1], place.at(z, place.l2))),
        "x": links.message(lambda: (smx.at[0], smx.at[1], place.at(z, place.l3))),
        "w": links.message(lambda: (smw.at[0], smw.at[1], place.sibling)),
    }
    for k in range(1, nz):
        small[k] = links.message(lambda k=k: (sm, smz.at[k - 1], place.at(place.around(k), l)))

    def begin(flows):
        for flow in flows:
            flow.start()

    def small_z():
        for k in range(1, nz):
            small[k].wait_recv()
        total = jnp.zeros(sm.shape, F32)
        for source in range(nz):
            for k in range(nz):
                piece = sm[...] if k == 0 else smz[k - 1]
                total = total + jnp.where(place.around(nz - k) == source, piece, 0.0)
        smy[0] = total
        small["y"].start()

    def small_2():
        small["y"].wait_recv()
        smx[0] = smy[0] + smy[1]
        small["x"].start()

    def small_3():
        small["x"].wait_recv()
        smw[0] = smx[0] + smx[1]
        small["w"].start()

    def small_4():
        small["w"].wait_recv()
        total = smw[0] + smw[1]
        small_o[...] = jnp.where(c == 0, total[:, :half], total[:, half:])

    def weights_out(g):
        res[g, z, l] = scatters[g].total().astype(BF16)
        begin(gathers[g])

    def tokens_out():
        grad = reduce_u.total()
        own = attn_s[pl.ds(0, rows), :]
        scale = row_scale(own)
        hat = own * scale
        lifted = grad * gain_a
        grad_x = scale * (lifted - hat * jnp.mean(lifted * hat, axis=-1, keepdims=True))
        at = pl.ds(pl.multiple_of(c * rows, rows), rows)
        grow_o[...] = grad_x + resid_s[at, :] + logit_s[at, :] * router

    slots, part_ff = stage_u.shape[:2]
    hb = slots * part_ff
    blocks = ff // hb
    tile = total_rows // 2
    tiles = 2 * total_rows // tile
    per_block = tiles + 2
    steps = [step for flows in (gx, gg, gw, *gathers) for flow in flows for step in flow.steps()]
    steps += [step for scatter in (*scatters, reduce_u) for step in scatter.steps()]
    steps += [functools.partial(weights_out, g) for g in range(2)]
    steps += [small_z, small_2, small_3, small_4, tokens_out]
    steps += [functools.partial(reduce_u.launch, o) for o in reduce_u.order]
    left = set(range(len(steps)))

    def pump(kind, j):
        for i in SCHEDULE[POINTS[kind] + j]:
            left.remove(i)
            steps[i]()

    def pump_in(index, kind, among):
        for j in among:
            if SCHEDULE[POINTS[kind] + j]:
                pl.when(index == j)(functools.partial(pump, kind, j))

    itself = lax.broadcasted_iota(jnp.int32, (rows, total_rows), 1) == (
        lax.broadcasted_iota(jnp.int32, (rows, total_rows), 0) + place.me * rows
    )
    picked_f = picked[...].astype(F32)
    own_index = [
        jnp.sum(jnp.where(itself, picked_f[s : s + 1], 0.0), axis=-1, keepdims=True) for s in range(2)
    ]
    own_row = jnp.where(c == 0, own_index[0], own_index[1])
    pick = jnp.where(
        lax.broadcasted_iota(jnp.int32, (rows, block), 1).astype(F32) == own_row, 1.0, 0.0
    ).astype(BF16)
    pick_o[...] = pick
    loads[0].wait()
    xall[c, z, l] = mm(pick, tokens[...]).astype(BF16)
    gvec[c] = jnp.zeros(gvec.shape[1:], F32)
    for i, ref in enumerate((gain_a_r, gain_m_r, router_r)):
        gvec[c, i : i + 1] = ref[...].astype(F32).reshape(1, half)
    pl.semaphore_wait(barrier, len(peers) + jnp.where(z + 1 < nz, 1, 0) + jnp.where(z > 0, 1, 0))

    begin(gx)
    for load in loads[2:]:
        load.start()
    vec_copy = links.copy(lambda: (gvec.at[c], gvec.at[c], place.sibling))
    loads[1].wait()
    gall[c, z, l] = mm(pick, cot[...]).astype(BF16)

    lane = lax.broadcasted_iota(jnp.int32, (2, total_rows), 1)
    stream = lax.broadcasted_iota(jnp.int32, (2, total_rows), 0)

    def place_keys(d, carry):
        until = d * rows + jnp.where(stream == 0, counts[0, d], counts[1, d])
        mine = (lane >= d * rows) & (lane < until)
        return jnp.where(mine, picked_f * nseq + d.astype(F32), carry)

    kpos = lax.fori_loop(0, nseq, place_keys, jnp.full((2, total_rows), FAR, F32))
    for s in range(2):
        near = kpos[s : s + 1] <= own_index[s] * nseq + place.me.astype(F32)
        bias[s] = jnp.where(near | itself, 0.0, NEG)
    slot = lax.broadcasted_iota(jnp.int32, (both, 1), 0)
    first = slot < rows
    own_live = jnp.where(
        slot - jnp.where(first, 0, rows) < jnp.where(first, counts[0, place.me], counts[1, place.me]), 1.0, 0.0
    )
    on_core = jnp.where(first, (1 - c).astype(F32), c.astype(F32))
    vec_copy.wait_recv()
    vectors = jnp.concatenate([gvec[0], gvec[1]], axis=1)
    gain_a, gain_m, router = vectors[0:1], vectors[1:2], vectors[2:3]
    for load in loads[2:5]:
        load.wait()

    def project(s, line):
        def norm(zz, carry):
            value = xall[s, zz, line].astype(F32)
            uall[s, zz, line] = (value * row_scale(value) * gain_a).astype(BF16)
            return carry

        lax.fori_loop(0, nz, norm, 0)
        u = jnp.concatenate([uall[s, zz, line] for zz in range(nz)], axis=0)
        value = mm(u, wqkv[:, half:]).astype(BF16)
        for j, out in enumerate((kall, vall)):
            for p in range(pairs):
                at = j * half + p * 128
                for zz in range(nz):
                    out[s * pairs + p, zz, line] = value[zz * rows : (zz + 1) * rows, at : at + 128]

    def arrive(j):
        pump("x", j)
        if j % 2:
            for flow in gx:
                flow.lent_line(j // 2)
        if j == COTANGENT_AT:
            begin(gg)

    def take_line(j, carry):
        for i in range(8):
            pl.when(j == i)(functools.partial(arrive, i))
        mine = lax.rem(j, 2) == 0
        step = lax.div(j, 2)
        one, two = jnp.where(mine, place.l2, place.l3), jnp.where(mine, place.l3, place.l2)
        line = jnp.where(
            step == 0, l, jnp.where(step == 1, one, jnp.where(step == 2, two, place.l23))
        )
        project(jnp.where(mine, c, other), line)
        return carry

    lax.fori_loop(0, 8, take_line, 0)
    low = lax.broadcasted_iota(jnp.int32, (rows, 128), 1) < HD

    def stacked(value, s, p):
        piece = value[s * rows : (s + 1) * rows, p * 128 : (p + 1) * 128]
        zero = jnp.zeros_like(piece)
        return jnp.concatenate([jnp.where(low, piece, zero), jnp.where(low, zero, piece)], axis=0)

    own_u = uall[:, z, l].reshape(both, width)
    query = mm(own_u, wqkv[:, :half]).astype(BF16) * jnp.asarray(HD ** (-0.5), BF16)
    for s in range(2):
        for p in range(pairs):
            qst[s * pairs + p] = stacked(query, s, p)

    def attend(i, carry):
        s, p = lax.div(i, pairs), lax.rem(i, pairs)
        keys = kall[i].reshape(total_rows, 128)
        vals = vall[i].reshape(total_rows, 128)
        hide = bias[s]
        raw = mm(qst[i], keys, NT) + jnp.concatenate([hide, hide], axis=0)
        expd = jnp.exp(raw - jnp.max(raw, axis=-1, keepdims=True))
        prob = expd * (1.0 / jnp.sum(expd, axis=-1, keepdims=True))
        probs[i] = prob
        out = mm(prob.astype(BF16), vals)
        at = pl.multiple_of(p * 128, 128)
        att[s, :, pl.ds(at, 128)] = jnp.where(low, out[:rows], out[rows:]).astype(BF16)
        pump_in(i, "a", range(2 * pairs))
        return carry

    lax.fori_loop(0, 2 * pairs, attend, 0)
    loads[5].wait()
    part[...] = mm(att[...].reshape(both, half), wout[...])
    swap = links.copy(lambda: (part, got_a, place.sibling))
    x_both = xall[:, z, l].reshape(both, width).astype(F32)
    pump("p", 0)
    weight = jax.nn.sigmoid(jnp.sum(x_both * router, axis=-1, keepdims=True))
    lift = weight * own_live
    for flow in gg:
        flow.lent_own()
    swap.wait()
    attn = part[...] + got_a[...]
    attn_s[...] = attn
    resid = x_both + attn
    resid_s[...] = resid
    w_both = (resid * row_scale(resid) * gain_m).astype(BF16)
    wall[:, z, l] = w_both.reshape(2, rows, width)
    begin(gw)
    for load in loads[6:]:
        load.wait()

    fb = 512
    for b in range(ff // fb):
        cut = slice(b * fb, (b + 1) * fb)
        pre = mm(w_both, wup[:, cut])
        pre_s[:, cut] = pre
        act_s[:, cut] = gelu_parts(pre)[0].astype(BF16)
    pump("p", 1)
    part[...] = mm(act_s[...], wdown[...])
    swap = links.copy(lambda: (part, got_m, place.sibling))
    pump("p", 2)
    swap.wait()
    branch = attn_s[...] + (part[...] + got_m[...])
    x_both = xall[:, z, l].reshape(both, width).astype(F32)
    dy_both = gall[:, z, l].reshape(both, width).astype(F32)
    grad_branch = dy_both * lift
    g_both = grad_branch.astype(BF16)
    attn_s[...] = x_both + lift * branch
    rows_o[...] = attn_s[pl.ds(pl.multiple_of(c * rows, rows), rows), :].astype(BF16)
    grad_logit = (
        jnp.sum(dy_both * branch, axis=-1, keepdims=True) * own_live * weight * (1.0 - weight)
    )
    logit_s[...] = grad_logit
    sm[...] = jnp.zeros_like(sm)
    sm[2:3] = jnp.sum(grad_logit * on_core * x_both, axis=0, keepdims=True)
    pump("p", 3)
    for b in range(ff // fb):
        cut = slice(b * fb, (b + 1) * fb)
        grad_act = mm(g_both, wdown[cut, :], NT)
        gpre_s[:, cut] = (gelu_parts(pre_s[:, cut])[1] * grad_act).astype(BF16)
    pump("p", 4)
    part[...] = mm(gpre_s[...], wup[...], NT)
    swap = links.copy(lambda: (part, got_a, place.sibling))
    pump("p", 5)
    swap.wait()
    grad_w = part[...] + got_a[...]
    resid = resid_s[...]
    scale_m = row_scale(resid)
    hat = resid * scale_m
    sm[1:2] = jnp.sum(grad_w * on_core * hat, axis=0, keepdims=True)
    lifted = grad_w * gain_m
    grad_resid = scale_m * (lifted - hat * jnp.mean(lifted * hat, axis=-1, keepdims=True))
    resid_s[...] = grad_resid
    ga_both = (gall[:, z, l].reshape(both, width).astype(F32) * lift + grad_resid).astype(BF16)
    attended = att[...].reshape(both, half)
    piece = width // nseq
    grad_o = mm(attended, ga_both, TN).astype(BF16)
    for i in range(3):
        value = jnp.concatenate(
            [grad_o[:, 256 * i : 256 * i + 128], grad_o[:, 256 * i + 128 : 256 * i + 256]], axis=0
        )
        share[0, :, :, 0, i] = value.reshape(nz, LINES, piece, 128)
    grad_att = mm(ga_both, wout[...], NT).astype(BF16)
    for s in range(2):
        for p in range(pairs):
            dost[s * pairs + p] = stacked(grad_att, s, p)

    def attend_back(s, p):
        i = s * pairs + p
        keys = kall[i].reshape(total_rows, 128)
        vals = vall[i].reshape(total_rows, 128)
        prob = probs[i]
        grad_p = mm(dost[i], vals, NT)
        delta = jnp.sum(grad_p * prob, axis=-1, keepdims=True)
        grad_s = (prob * (grad_p - delta)).astype(BF16)
        out = mm(grad_s, keys) * HD ** (-0.5)
        gq[p, s] = jnp.where(low, out[:rows], out[rows:]).astype(BF16)
        gkv[p, s, :, :128] = mm(grad_s, qst[i], TN).astype(BF16)
        gkv[p, s, :, 128:] = mm(prob.astype(BF16), dost[i], TN).astype(BF16)

    def share_pair(p):
        group, unit = lax.div(p + 1, 2), lax.rem(p + 1, 2)
        grad_q = mm(uall[:, z, l].reshape(both, width), gq[p].reshape(both, 128), TN)
        share[group, :, :, unit, 0] = grad_q.astype(BF16).reshape(nz, LINES, piece, 128)
        span = width // 2

        def half_of(h, carry):
            at = pl.ds(pl.multiple_of(h * span, span), span)
            value = mm(uall[0, :, :, :, at].reshape(total_rows, span), gkv[p, 0], TN)
            value = value + mm(uall[1, :, :, :, at].reshape(total_rows, span), gkv[p, 1], TN)
            value = value.astype(BF16)
            zs = pl.ds(h * (nz // 2), nz // 2)
            for j in range(2):
                share[group, zs, :, unit, 1 + j] = value[:, 128 * j : 128 * (j + 1)].reshape(
                    nz // 2, LINES, piece, 128
                )
            return carry

        lax.fori_loop(0, 2, half_of, 0)

    def back(i, carry):
        p, s = lax.div(i, 2), lax.rem(i, 2)
        attend_back(s, p)
        pl.when(s == 1)(lambda: share_pair(p))
        pl.when(i == 1)(scatters[0].start)
        pl.when(i == 2 * pairs - 1)(scatters[1].start)
        pump_in(i, "b", range(2 * pairs))
        return carry

    lax.fori_loop(0, 2 * pairs, back, 0)
    for flow in gx:
        flow.wait_sent()

    pump("b", 6)
    for flow in gg:
        for j in range(LINES):
            flow.lent_line(j)
        flow.wait_sent()

    def weigh(i, carry):
        s, zz = lax.div(i, nz), lax.rem(i, nz)
        for line in range(LINES):
            gate = jax.nn.sigmoid(jnp.sum(xall[s, zz, line].astype(F32) * router, axis=-1, keepdims=True))
            alive = lax.broadcasted_iota(jnp.int32, (rows, 1), 0) < counts[s, zz * LINES + line]
            gall[s, zz, line] = (gall[s, zz, line].astype(F32) * jnp.where(alive, gate, 0.0)).astype(BF16)
        return carry

    lax.fori_loop(0, 2 * nz, weigh, 0)

    own_gq = jnp.concatenate([gq[p].reshape(both, 128) for p in range(pairs)], axis=1)
    part[...] = mm(own_gq, wqkv[:, :half], NT)

    def grad_u(s, j):
        size = 2 * LINES * rows
        at = pl.ds(pl.multiple_of(j * size, size), size)
        parts = [gkv[p, s, at, cut] for cut in (slice(0, 128), slice(128, 256)) for p in range(pairs)]
        return mm(jnp.concatenate(parts, axis=1), wqkv[:, half:], NT).reshape(2, LINES, rows, width)

    def part_of(s):
        return part[pl.ds(pl.multiple_of(s * rows, rows), rows), :]

    def theirs(j, carry):
        xall[other, pl.ds(2 * j, 2)] = grad_u(other, j).astype(BF16)
        pump_in(j, "v", range(nz // 2))
        return carry

    lax.fori_loop(0, nz // 2, theirs, 0)
    xall[other, z, l] = (xall[other, z, l].astype(F32) + part_of(other)).astype(BF16)
    lent = [
        links.copy(lambda j=j: (xall.at[other, pl.ds(2 * j, 2)], gsib.at[pl.ds(2 * j, 2)], place.sibling))
        for j in range(nz // 2)
    ]

    def ours(j, gain_total):
        value = grad_u(c, j)
        for i in range(nz // 2):
            pl.when(j == i)(lent[i].wait_recv)
        at = pl.ds(2 * j, 2)
        value = value + gsib[at].astype(F32)
        rows_x = xall[c, at].astype(F32)
        hat = rows_x * row_scale(rows_x)
        xall[c, at] = value.astype(BF16)
        pump_in(j, "u", range(nz // 2))
        return gain_total + jnp.sum(value * hat, axis=(0, 1, 2)).reshape(1, width)

    x_own = xall[c, z, l].astype(F32)
    gain_total = jnp.sum(part_of(c) * (x_own * row_scale(x_own)), axis=0, keepdims=True)
    attn_s[pl.ds(0, rows), :] = x_own
    gain_total = lax.fori_loop(0, nz // 2, ours, gain_total)
    xall[c, z, l] = (xall[c, z, l].astype(F32) + part_of(c)).astype(BF16)
    sm[0:1] = gain_total
    for k in range(1, nz):
        small[k].start()
    pump("u", nz)
    for flow in gw:
        for j in range(LINES):
            flow.lent_line(j)

    def put(b, i, which, stage, out):
        at = pl.ds(pl.multiple_of(b * hb + i * part_ff, part_ff), part_ff)
        return pltpu.make_async_copy(stage.at[i], out.at[at, :], osem.at[which, i])

    def ff_block(b, carry):
        cut = pl.ds(pl.multiple_of(b * hb, hb), hb)

        def ff_tile(t, carry):
            s, h = lax.div(t, 2), lax.rem(t, 2)
            at = pl.ds(pl.multiple_of(h * tile, tile), tile)
            zz = pl.ds(h * (nz // 2), nz // 2)
            act, slope = gelu_parts(mm(wall[s, zz].reshape(tile, width), wup[:, cut]))
            uall[s, zz, :, :, :hb] = act.astype(BF16).reshape(nz // 2, LINES, rows, hb)
            grad_act = mm(gall[s, zz].reshape(tile, width), wdown[cut, :], NT)
            grad_pre = (slope * grad_act).astype(BF16)
            for i in range(slots):
                gkv[i, s, at] = grad_pre[:, part_ff * i : part_ff * (i + 1)]
            pump_in(b * per_block + t, "h", [j for j in range(per_block * blocks) if j % per_block < tiles])
            return carry

        lax.fori_loop(0, tiles, ff_tile, 0)

        @pl.when(b >= 1)
        def _():
            for i in range(slots):
                put(b - 1, i, 0, stage_d, gdown_o).wait()
                put(b - 1, i, 1, stage_u, gup_o).wait()

        def flush(which, stage, out, lhs, rhs):
            value = mm(lhs, rhs[...].reshape(2 * total_rows, width), TN).astype(BF16)
            for i in range(slots):
                stage[i] = value[i * part_ff : (i + 1) * part_ff]
            for i in range(slots):
                put(b, i, which, stage, out).start()

        flush(0, stage_d, gdown_o, uall[:, :, :, :, :hb].reshape(2 * total_rows, hb), gall)
        pump_in(b * per_block + tiles, "h", range(tiles, per_block * blocks, per_block))
        slopes = [gkv[i].reshape(2 * total_rows, part_ff) for i in range(slots)]
        flush(1, stage_u, gup_o, jnp.concatenate(slopes, axis=1), wall)
        pump_in(b * per_block + tiles + 1, "h", range(tiles + 1, per_block * blocks, per_block))
        return carry

    lax.fori_loop(0, blocks, ff_block, 0)
    pump("z", 0)
    assert not left
    out_copy = pltpu.make_async_copy(res, res_o, osem.at[2, 0])
    out_copy.start()
    for i in range(slots):
        put(blocks - 1, i, 0, stage_d, gdown_o).wait()
        put(blocks - 1, i, 1, stage_u, gup_o).wait()
    links.drain()
    out_copy.wait()


def finish_kernel(
    tokens, cot, pick, rows, grow, small, res_h, gup_h, gdown_h,
    mixed_o, gtok_o, gain_a_o, gain_m_o, router_o, gqkv_o, gout_o, gup_o, gdown_o,
    res, gup, gdown, qkv_s, out_s, up_s, down_s, sem_in, sem_out,
):
    up_cuts = [slice(i * 384, (i + 1) * 384) for i in range(gup.shape[0] // 384)]
    down_cuts = [slice(i * 384, (i + 1) * 384) for i in range(gdown.shape[0] // 384)]
    loads, stores = [], []

    def load(src, dst):
        loads.append(pltpu.make_async_copy(src, dst, sem_in.at[len(loads)]))
        loads[-1].start()
        return loads[-1]

    def store(src, dst):
        stores.append(pltpu.make_async_copy(src, dst, sem_out.at[len(stores)]))
        stores[-1].start()

    downs = [load(gdown_h.at[cut], gdown.at[cut]) for cut in down_cuts]
    groups = [load(res_h.at[g], res.at[g]) for g in range(2)]
    ups = [load(gup_h.at[cut], gup.at[cut]) for cut in up_cuts]
    for cut, got in zip(down_cuts, downs):
        got.wait()
        down_s[cut] = gdown[cut].astype(F32)
        store(down_s.at[cut], gdown_o.at[cut])
    width = rows.shape[1]
    half = width // 2
    for got in groups:
        got.wait()
    for i in range(3):
        for unit in range(1, 4):
            cut = slice((unit - 1) * 128, unit * 128)
            qkv_s[i, :, cut] = res[unit // 2, :, :, unit % 2, i].reshape(width, 128).astype(F32)
        store(qkv_s.at[i], gqkv_o.at[i])
        value = res[0, :, :, 0, i].reshape(width, 128).astype(F32)
        out_s[:, 256 * i : 256 * i + 128] = value[:half]
        out_s[:, 256 * i + 128 : 256 * i + 256] = value[half:]
    store(out_s, gout_o)
    for cut, got in zip(up_cuts, ups):
        got.wait()
        up_s[:, cut] = gup[cut].astype(F32).T
        store(up_s.at[:, cut], gup_o.at[:, cut])
    chosen = mm(pick[...], jnp.ones(rows.shape, BF16), TN) > 0.5
    mixed_o[...] = jnp.where(chosen, mm(pick[...], rows[...], TN), tokens[...].astype(F32)).astype(BF16)
    grad = grow[...]
    hi = grad.astype(BF16)
    rest = grad - hi.astype(F32)
    mid = rest.astype(BF16)
    lo = (rest - mid.astype(F32)).astype(BF16)
    spread = mm(pick[...], hi, TN) + (mm(pick[...], mid, TN) + mm(pick[...], lo, TN))
    gtok_o[...] = (cot[...].astype(F32) + spread).astype(BF16)
    gain_a_o[...] = small[0:1].reshape(half)
    gain_m_o[...] = small[1:2].reshape(half)
    router_o[...] = small[2:3].reshape(half)
    for made in stores:
        made.wait()


def fused_body(
    tokens, cotangent, w_qkv, w_out, w_up, w_down, gain_attn, gain_mlp, router, picked, counts
):
    nseq = lax.axis_size("seq")
    nz = nseq // LINES
    rows = picked.shape[1] // nseq
    block, width = tokens.shape[1:]
    half, ff = w_out.shape[0], w_up.shape[1]
    pairs = half // 128
    total_rows = nseq * rows
    piece = width // nseq
    vm = pltpu.VMEM
    dma = pltpu.SemaphoreType.DMA
    wide = (2, nz, LINES, rows, width)
    heads = (2 * pairs, nz, LINES, rows, 128)
    both = (2 * rows, width)
    part = (2, 3, piece, 128)
    scratch = [
        vm((block, width), BF16), vm((block, width), BF16),
        vm((width, 3 * half), BF16), vm((half, width), BF16), vm((width, ff), BF16), vm((ff, width), BF16), dma((8,)),
        vm((2, 8, half), F32), vm(wide, BF16), vm(wide, BF16), vm(heads, BF16), vm(heads, BF16),
        vm((2 * pairs, 2 * rows, 128), BF16), vm((2, rows, total_rows), F32),
        vm((2 * pairs, 2 * rows, total_rows), F32), vm((2, rows, half), BF16),
        vm((8, 128), F32), vm(both, F32), vm(both, F32), vm((2 * rows, 1), F32),
        vm(both, F32), vm(both, F32), vm(both, F32),
        vm(wide, BF16), vm(wide, BF16), vm((2 * rows, ff), F32), vm((2 * rows, ff), BF16), vm((2 * rows, ff), BF16),
        vm((2 * pairs, 2 * rows, 128), BF16), vm((pairs, 2, rows, 128), BF16), vm((pairs, 2, total_rows, 256), BF16),
        vm((nz, LINES, rows, width), BF16), vm((nz, 2, rows, width), BF16), vm((nz, rows, width), BF16),
        vm((nz - 1, rows, width), BF16),
        vm((2, nz, LINES, *part), BF16), vm((2, nz, 2, *part), BF16), vm((2, nz, *part), BF16),
        vm((2, nz - 1, *part), BF16), vm((2, nz, LINES, *part), BF16),
        vm((8, width), F32), vm((nz - 1, 8, width), F32), vm((2, 8, width), F32), vm((2, 8, width), F32),
        vm((2, 8, width), F32),
        vm((2, 256, width), BF16), vm((2, 256, width), BF16), dma((3, 2)),
        dma((MESSAGES,)), dma((MESSAGES,)),
    ]
    in_vmem = pl.BlockSpec(memory_space=pltpu.VMEM)
    in_hbm = pl.BlockSpec(memory_space=pl.ANY)
    in_smem = pl.BlockSpec(memory_space=pltpu.SMEM)
    shaped = jax.ShapeDtypeStruct
    pick, out_rows, grad_rows, res, grad_up, grad_down, small = pl.pallas_call(
        functools.partial(layer_kernel, nz),
        out_shape=(
            shaped((rows, block), BF16),
            shaped((rows, width), BF16),
            shaped((rows, width), F32),
            shaped((2, nz, LINES, *part), BF16),
            shaped((ff, width), BF16),
            shaped((ff, width), BF16),
            shaped((8, half), F32),
        ),
        in_specs=[in_hbm] * 2 + [in_vmem, in_smem] + [in_vmem] * 3 + [in_hbm] * 4,
        out_specs=(in_vmem, in_vmem, in_vmem, in_hbm, in_hbm, in_hbm, in_vmem),
        scratch_shapes=scratch,
        compiler_params=pltpu.CompilerParams(
            collective_id=0, has_side_effects=True, vmem_limit_bytes=VMEM_BYTES
        ),
        name="layer",
    )(
        tokens[0], cotangent[0], picked, counts,
        gain_attn, gain_mlp, router, w_qkv, w_out, w_up, w_down,
    )
    mixed, grad_tokens, gain_a, gain_m, grad_r, grad_qkv, grad_out, grad_up, grad_down = pl.pallas_call(
        finish_kernel,
        out_shape=(
            shaped((block, width), BF16),
            shaped((block, width), BF16),
            shaped((half,), F32),
            shaped((half,), F32),
            shaped((half,), F32),
            shaped((3, width, half), F32),
            shaped((half, width), F32),
            shaped((width, ff), F32),
            shaped((ff, width), F32),
        ),
        in_specs=[in_vmem] * 6 + [in_hbm] * 3,
        out_specs=(in_vmem,) * 5 + (in_hbm,) * 4,
        scratch_shapes=[
            vm((2, nz, LINES, *part), BF16), vm((ff, width), BF16), vm((ff, width), BF16),
            vm((3, width, half), F32), vm((half, width), F32), vm((width, ff), F32), vm((ff, width), F32),
            dma((16,)), dma((16,)),
        ],
        compiler_params=pltpu.CompilerParams(vmem_limit_bytes=VMEM_BYTES),
        name="finish",
    )(tokens[0], cotangent[0], pick, out_rows, grad_rows, small, res, grad_up, grad_down)
    return (
        mixed[None], grad_tokens[None], grad_qkv, grad_out, grad_up, grad_down, gain_a, gain_m, grad_r,
    )


def body(tokens, *rest):
    nseq, cores = lax.axis_size("seq"), lax.axis_size("wa")
    fits = nseq == 4 * LINES and cores == 2 and rest[-2].shape[1] == nseq * CAP
    return (fused_body if fits else spread_body)(tokens, *rest)


CAP = 80


def norm_rows(value, gain):
    scale = lax.rsqrt(jnp.mean(value * value, axis=-1, keepdims=True) + EPS)
    return (value * scale * gain, scale)


def norm_back(value, scale, gain, grad_out):
    normed = value * scale
    weighted = grad_out * gain
    grad_value = scale * (weighted - normed * jnp.mean(weighted * normed, axis=-1, keepdims=True))
    return (grad_value, normed)


def gelu_back(pre, grad):
    unused, pull = jax.vjp(lambda value: jax.nn.gelu(value, approximate=True), pre)
    return pull(grad)[0]


def spread_body(
    tokens, cotangent, w_qkv, w_out, w_up, w_down, gain_attn, gain_mlp, router, picked, counts
):
    f32 = jnp.float32
    bf16 = jnp.bfloat16
    nseq = lax.axis_size("seq")
    me = lax.axis_index("seq")
    side = lax.axis_index("wa")
    slots = jnp.arange(CAP, dtype=jnp.int32)
    own_rows = lax.dynamic_slice(picked, (side, me * CAP), (1, CAP))[0]
    x_own = jnp.take(tokens[0], own_rows, axis=0)
    dy_own = jnp.take(cotangent[0], own_rows, axis=0).astype(f32)
    x_rows, g_attn, g_mlp, w_router = (
        lax.all_gather(x_own[None], "wa", axis=0, tiled=True),
        lax.all_gather(gain_attn, "wa", axis=0, tiled=True),
        lax.all_gather(gain_mlp, "wa", axis=0, tiled=True),
        lax.all_gather(router, "wa", axis=0, tiled=True),
    )
    qkv_w, out_w, up_w, down_w = (w_qkv, w_out, w_up, w_down)
    streams = jnp.arange(lax.axis_size("wa"))
    stream_picked = jnp.take(picked, streams, axis=0)
    stream_counts = jnp.take(counts, streams, axis=0)
    key_index = jnp.arange(nseq * CAP, dtype=jnp.int32)
    key_device = key_index // CAP
    key_pos = stream_picked * nseq + key_device[None, :]
    key_live = (key_index % CAP)[None, :] < jnp.take(stream_counts, key_device, axis=1)
    query_index = me * CAP + slots
    query_pos = lax.dynamic_slice_in_dim(key_pos, me * CAP, CAP, 1)
    own_live = (slots < counts[side, me]).astype(f32)
    gains_a = g_attn.astype(f32)
    gains_m = g_mlp.astype(f32)
    x_keep = x_own.astype(f32)
    weight = jax.nn.sigmoid(jnp.dot(x_own, w_router, preferred_element_type=f32))
    x_wide = x_rows.astype(f32)
    normed_a, scale_a = norm_rows(x_wide, gains_a)
    u_rows = normed_a.astype(bf16)
    qkv = jnp.einsum("srd,cde->csre", u_rows, qkv_w, preferred_element_type=f32).astype(bf16)
    query = qkv[0]
    local_kv = qkv[1:]
    batch = query.shape[0]
    heads = query.shape[-1] // HD
    factor = HD ** (-0.5)
    split_q = query.reshape(batch, CAP, heads, HD)
    kv_all = lax.all_gather(local_kv, "seq", axis=2, tiled=True)
    block = 8 * CAP
    nblock = kv_all.shape[2] // block

    def block_of(start):
        keys_b = lax.dynamic_slice_in_dim(kv_all[0], start, block, 1).reshape(
            batch, block, heads, HD
        )
        vals_b = lax.dynamic_slice_in_dim(kv_all[1], start, block, 1).reshape(
            batch, block, heads, HD
        )
        k_pos = lax.dynamic_slice_in_dim(key_pos, start, block, 1)
        k_live = lax.dynamic_slice_in_dim(key_live, start, block, 1)
        k_index = start + jnp.arange(block, dtype=jnp.int32)
        allowed = (k_pos[:, None, :] <= query_pos[:, :, None]) & (
            k_live[:, None, :] | (k_index[None, None, :] == query_index[None, :, None])
        )
        raw = jnp.einsum("sqhd,skhd->shqk", split_q, keys_b, preferred_element_type=f32) * factor
        return (keys_b, vals_b, allowed, jnp.where(allowed[:, None], raw, NEG))

    def max_sum(number, carry):
        top, total = carry
        unused_k, unused_v, allowed, scores = block_of(number * block)
        new_top = jnp.maximum(top, jnp.max(scores, axis=-1, keepdims=True))
        expd = jnp.where(allowed[:, None], jnp.exp(scores - new_top), 0.0)
        return (new_top, total * jnp.exp(top - new_top) + jnp.sum(expd, axis=-1, keepdims=True))

    top_start = jnp.full((batch, heads, CAP, 1), NEG, f32)
    top, total = lax.fori_loop(
        0, nblock, max_sum, (top_start, jnp.zeros((batch, heads, CAP, 1), f32))
    )
    lse = top + jnp.log(total)

    def weigh(number, acc):
        unused_k, vals_b, allowed, scores = block_of(number * block)
        probs_low = jnp.exp(scores - lse).astype(bf16)
        return acc + jnp.einsum("shqk,skhd->sqhd", probs_low, vals_b, preferred_element_type=f32)

    acc = lax.fori_loop(0, nblock, weigh, jnp.zeros((batch, CAP, heads, HD), f32))
    attended = acc.reshape(query.shape).astype(bf16)
    attn_part = jnp.einsum("sqe,ed->sqd", attended, out_w, preferred_element_type=f32)
    attn_own = lax.psum_scatter(attn_part, "wa", scatter_dimension=0, tiled=True)[0]
    resid = x_keep + attn_own
    normed_m, scale_m = norm_rows(resid, gains_m)
    w_own = normed_m.astype(bf16)
    w_rows = lax.all_gather(w_own[None], "wa", axis=0, tiled=True)
    pre = jnp.einsum("srd,df->srf", w_rows, up_w, preferred_element_type=f32)
    act = jax.nn.gelu(pre, approximate=True).astype(bf16)
    mlp_part = jnp.einsum("srf,fd->srd", act, down_w, preferred_element_type=f32)
    mlp_own = lax.psum_scatter(
        mlp_part.astype(jnp.bfloat16), "wa", scatter_dimension=0, tiled=True
    ).astype(jnp.float32)[0]
    branch = attn_own + mlp_own
    lift = (weight * own_live)[:, None]
    out_rows = (x_keep + lift * branch).astype(bf16)
    mixed_out = tokens.at[0, own_rows].set(out_rows)
    grad_branch = dy_own * lift
    grad_logit = jnp.sum(dy_own * branch, axis=-1) * own_live * weight * (1.0 - weight)
    grad_router = jnp.dot(grad_logit, x_keep, precision=lax.Precision.HIGHEST)
    grad_m = grad_branch.astype(bf16)
    grad_m_rows = lax.all_gather(grad_m[None], "wa", axis=0, tiled=True)
    grad_down = jnp.einsum("srf,srd->fd", act, grad_m_rows, preferred_element_type=f32)
    grad_act = jnp.einsum("srd,fd->srf", grad_m_rows, down_w, preferred_element_type=f32)
    grad_pre = gelu_back(pre, grad_act).astype(bf16)
    grad_up = jnp.einsum("srd,srf->df", w_rows, grad_pre, preferred_element_type=f32)
    grad_w_part = jnp.einsum("srf,df->srd", grad_pre, up_w, preferred_element_type=f32)
    grad_w_own = lax.psum_scatter(grad_w_part, "wa", scatter_dimension=0, tiled=True)[0]
    grad_resid, hat_m = norm_back(resid, scale_m, gains_m, grad_w_own)
    grad_gain_m = jnp.sum(grad_w_own * hat_m, axis=0)
    grad_a = (grad_branch + grad_resid).astype(bf16)
    grad_a_rows = lax.all_gather(grad_a[None], "wa", axis=0, tiled=True)
    grad_out = jnp.einsum("sqe,sqd->ed", attended, grad_a_rows, preferred_element_type=f32)
    grad_attended = jnp.einsum(
        "sqd,ed->sqe", grad_a_rows, out_w, preferred_element_type=f32
    ).astype(bf16)
    split_do = grad_attended.reshape(batch, CAP, heads, HD)

    def delta_step(number, delta):
        unused_k, vals_b, allowed, scores = block_of(number * block)
        probs = jnp.exp(scores - lse)
        grad_probs = jnp.einsum("sqhd,skhd->shqk", split_do, vals_b, preferred_element_type=f32)
        return delta + jnp.sum(grad_probs * probs, axis=-1, keepdims=True)

    delta = lax.fori_loop(0, nblock, delta_step, jnp.zeros((batch, heads, CAP, 1), f32))

    def grad_step(number, carry):
        grad_query, holder = carry
        start = number * block
        keys_b, vals_b, allowed, scores = block_of(start)
        probs = jnp.exp(scores - lse)
        grad_probs = jnp.einsum("sqhd,skhd->shqk", split_do, vals_b, preferred_element_type=f32)
        grad_scores = (probs * (grad_probs - delta)).astype(bf16)
        grad_query = (
            grad_query
            + jnp.einsum("shqk,skhd->sqhd", grad_scores, keys_b, preferred_element_type=f32)
            * factor
        )
        grad_keys = (
            jnp.einsum("shqk,sqhd->skhd", grad_scores, split_q, preferred_element_type=f32) * factor
        )
        grad_values = jnp.einsum(
            "shqk,sqhd->skhd", probs.astype(bf16), split_do, preferred_element_type=f32
        )
        paired = jnp.stack([grad_keys, grad_values]).reshape(2, batch, block, heads * HD)
        holder = lax.dynamic_update_slice_in_dim(holder, paired, start, 2)
        return (grad_query, holder)

    grad_query, holder = lax.fori_loop(
        0,
        nblock,
        grad_step,
        (jnp.zeros((batch, CAP, heads, HD), f32), jnp.zeros(kv_all.shape, f32)),
    )
    kv_total = lax.psum_scatter(holder.astype(bf16), "seq", scatter_dimension=2, tiled=True)
    grad_qkv_rows = jnp.concatenate(
        [grad_query.reshape(query.shape)[None].astype(bf16), kv_total.astype(bf16)], axis=0
    )
    grad_qkv = jnp.einsum("srd,csre->cde", u_rows, grad_qkv_rows, preferred_element_type=f32)
    grad_u_part = jnp.einsum("csre,cde->srd", grad_qkv_rows, qkv_w, preferred_element_type=f32)
    part_gain_a = jnp.sum(grad_u_part * (x_wide * scale_a), axis=(0, 1))
    grad_u_all, grad_gain_a, grad_gain_m, grad_router = (
        lax.psum_scatter(
            grad_u_part.astype(jnp.bfloat16), "wa", scatter_dimension=0, tiled=True
        ).astype(jnp.float32),
        lax.psum_scatter(
            part_gain_a.astype(jnp.bfloat16), "wa", scatter_dimension=0, tiled=True
        ).astype(jnp.float32),
        lax.psum_scatter(
            grad_gain_m.astype(jnp.bfloat16), "wa", scatter_dimension=0, tiled=True
        ).astype(jnp.float32),
        lax.psum_scatter(
            grad_router.astype(jnp.bfloat16), "wa", scatter_dimension=0, tiled=True
        ).astype(jnp.float32),
    )
    grad_u_own = grad_u_all[0]
    grad_x_norm, unused = norm_back(x_keep, scale_a[side], gains_a, grad_u_own)
    grad_rows = grad_x_norm + grad_resid + grad_logit[:, None] * w_router.astype(f32)[None, :]
    grad_tokens = cotangent.astype(f32).at[0, own_rows].add(grad_rows).astype(bf16)
    shares = (grad_qkv, grad_out, grad_up, grad_down, grad_gain_a, grad_gain_m, grad_router)
    large = lax.psum(tuple(share.astype(bf16) for share in shares[:4]), "seq")
    small = lax.psum(shares[4:], "seq")
    summed = tuple(part.astype(f32) for part in large) + small
    return (
        mixed_out,
        grad_tokens,
        summed[0],
        summed[1],
        summed[2],
        summed[3],
        summed[4],
        summed[5],
        summed[6],
    )


def solution(mesh):
    return jax.shard_map(
        body,
        mesh=mesh,
        in_specs=(
            P("wa", "seq", None),
            P("wa", "seq", None),
            P(None, None, "wa"),
            P("wa", None),
            P(None, "wa"),
            P("wa", None),
            P("wa"),
            P("wa"),
            P("wa"),
            P(),
            P(),
        ),
        out_specs=(
            P("wa", "seq", None),
            P("wa", "seq", None),
            P(None, None, "wa"),
            P("wa", None),
            P(None, "wa"),
            P("wa", None),
            P("wa"),
            P("wa"),
            P("wa"),
        ),
        check_vma=False,
    )
```
